32 devices in a mesh: dp: 8 (over y, x, core), tensor: 4 (over z).
Axes of the slice: x: 2, y: 2, z: 4, core: 2. Of those that a mesh axis runs over, the one named last changes fastest.
Arguments:
- language: bfloat16 [256, 20, 768], P(('dp', 'tensor')), may hold values from -6 to 6
- visual: bfloat16 [256, 36, 768], P(('dp', 'tensor')), may hold values from -6 to 6
- word_count: int32 [256], P('dp'), may hold values from 5 to 20
- region_count: int32 [256], P('dp'), may hold values from 10 to 36
- task_flags: int32 [256, 3], P(('dp', 'tensor')), may hold values 0 or 1
- grad_language: bfloat16 [256, 20, 768], P(('dp', 'tensor')), may hold values from -6 to 6
- grad_visual: bfloat16 [256, 36, 768], P(('dp', 'tensor')), may hold values from -6 to 6
- cross_project: bfloat16 [3, 768, 768], P(None, None, 'tensor'), may hold values from -0.21875 to 0.21875
- cross_bias: float32 [2, 768], P(None, 'tensor'), may hold values from -2 to 2
- cross_out: bfloat16 [768, 768], P('tensor'), may hold values from -0.625 to 0.625
- cross_out_bias: float32 [768], replicated, may hold values from -2 to 2
- cross_gain: float32 [768], replicated, may hold values from 0.5 to 1.5
- cross_shift: float32 [768], replicated, may hold values from -2 to 2
- self_project: bfloat16 [2, 3, 768, 768], P(None, None, None, 'tensor'), may hold values from -0.21875 to 0.21875
- self_bias: float32 [2, 2, 768], P(None, None, 'tensor'), may hold values from -2 to 2
- self_out: bfloat16 [2, 768, 768], P(None, 'tensor'), may hold values from -0.625 to 0.625
- self_out_bias: float32 [2, 768], replicated, may hold values from -2 to 2
- self_gain: float32 [2, 768], replicated, may hold values from 0.5 to 1.5
- self_shift: float32 [2, 768], replicated, may hold values from -2 to 2
- feed_in: bfloat16 [2, 768, 3072], P(None, None, 'tensor'), may hold values from -0.21875 to 0.21875
- feed_in_bias: float32 [2, 3072], P(None, 'tensor'), may hold values from -2 to 2
- feed_out: bfloat16 [2, 3072, 768], P(None, 'tensor'), may hold values from -0.15625 to 0.15625
- feed_out_bias: float32 [2, 768], replicated, may hold values from -2 to 2
- feed_gain: float32 [2, 768], replicated, may hold values from 0.5 to 1.5
- feed_shift: float32 [2, 768], replicated, may hold values from -2 to 2
Outputs:
- language_out: bfloat16 [256, 20, 768], P(('dp', 'tensor'))
- visual_out: bfloat16 [256, 36, 768], P(('dp', 'tensor'))
- grad_language_in: float32 [256, 20, 768], P(('dp', 'tensor'))
- grad_visual_in: float32 [256, 36, 768], P(('dp', 'tensor'))
- grad_cross_project: float32 [3, 768, 768], P(None, 'dp', 'tensor')
- grad_cross_bias: float32 [2, 768], replicated
- grad_cross_out: float32 [768, 768], P('tensor', 'dp')
- grad_cross_out_bias: float32 [768], replicated
- grad_cross_gain: float32 [768], replicated
- grad_cross_shift: float32 [768], replicated
- grad_self_project: float32 [2, 3, 768, 768], P(None, None, 'dp', 'tensor')
- grad_self_bias: float32 [2, 2, 768], replicated
- grad_self_out: float32 [2, 768, 768], P(None, 'tensor', 'dp')
- grad_self_out_bias: float32 [2, 768], replicated
- grad_self_gain: float32 [2, 768], replicated
- grad_self_shift: float32 [2, 768], replicated
- grad_feed_in: float32 [2, 768, 3072], P(None, 'dp', 'tensor')
- grad_feed_in_bias: float32 [2, 3072], replicated
- grad_feed_out: float32 [2, 3072, 768], P(None, 'tensor', 'dp')
- grad_feed_out_bias: float32 [2, 768], replicated
- grad_feed_gain: float32 [2, 768], replicated
- grad_feed_shift: float32 [2, 768], replicated
The draws below stay inside these ranges and needn't reach their ends.
Inputs may be any that keep to these rules, and one draw needn't show every extreme that they name: `word_count`: slots at positions >= the count are padding: no query attends to them. `region_count`: slots at positions >= the count are padding: no query attends to them. `task_flags`: column 0: masked word prediction, column 1: VQA answer, column 2: GQA answer.
All inputs are finite; a program needn't handle non-finite values. No bound on the sum of `task_flags` on one device may be relied on, other than what follows from the above.
Results may differ from the reference program's by a relative error of at most 0.025.
Values may be sent and summed in bfloat16 or wider, within the bound.
A program may use at most 192 MiB of HBM per device.

```python
import jax
import jax.numpy as jnp
from jax import lax

D = 768
HEAD_DIM = 64
FF = 3072
WORDS = 20
REGIONS = 36
ITEMS = 256
N_DP = 8


def place_ends(entries, stream_key, least, top_value):
    index_at = [jax.random.randint(jax.random.fold_in(stream_key, axis), (), 0, length) for axis, length in enumerate(entries.shape)]
    widest = entries.shape.index(max(entries.shape))
    neighbour = index_at[:widest] + [(index_at[widest] + 1) % entries.shape[widest]] + index_at[widest + 1:]
    return entries.at[tuple(index_at)].set(least).at[tuple(neighbour)].set(top_value)


def steps_of(stream_key, shape, split, least, largest):
    def one(position, blocks):
        draws = jax.random.uniform(jax.random.fold_in(jax.random.fold_in(stream_key, 6), position), (blocks,), jnp.float32, least / len(split), largest / len(split))
        return jnp.repeat(jnp.exp(draws), shape[position] // blocks).reshape((-1,) + (1,) * (len(shape) - position - 1))

    gain = one(*split[0])
    for cut in split[1:]:
        gain = gain * one(*cut)
    return gain


def centred(stream_key, extent, width, most, split=(), kind=jnp.bfloat16):
    drawn = jax.random.normal(stream_key, extent, jnp.float32) * width
    if len(split) > 0:
        drawn = steps_of(stream_key, extent, split, -0.22, 0.18) * drawn
    return jnp.clip(drawn, min=-most, max=most).astype(kind)


def setup_inputs(seed: int = 0) -> dict:
    key_list = jax.random.split(jax.random.key(seed), 26)
    return {
        "language": centred(key_list[0], (ITEMS, WORDS, D), 1.0, 6.0, ((0, 32),)),
        "visual": centred(key_list[1], (ITEMS, REGIONS, D), 1.0, 6.0, ((0, 32),)),
        "word_count": place_ends(jax.random.randint(key_list[2], (ITEMS,), WORDS // 5 + 1, WORDS + 1), jax.random.fold_in(key_list[2], 1), WORDS // 5 + 1, WORDS).astype(jnp.int32),
        "region_count": place_ends(jax.random.randint(key_list[3], (ITEMS,), REGIONS // 4 + 1, REGIONS + 1), jax.random.fold_in(key_list[3], 1), REGIONS // 4 + 1, REGIONS).astype(jnp.int32),
        "task_flags": place_ends((jax.random.randint(key_list[4], (ITEMS, 3), 0, 2) < 1).astype(jnp.int32), jax.random.fold_in(key_list[4], 1), 0, 1),
        "grad_language": centred(key_list[5], (ITEMS, WORDS, D), 1.0, 6.0, ((0, 32),)),
        "grad_visual": centred(key_list[6], (ITEMS, REGIONS, D), 1.0, 6.0, ((0, 32),)),
        "cross_project": centred(key_list[7], (3, D, D), D ** -0.5, 0.21875, ((2, 4),)),
        "cross_bias": centred(key_list[8], (2, D), 0.3, 2.0, ((1, 4),), jnp.float32),
        "cross_out": centred(key_list[9], (D, D), (D // 8) ** -0.5, 0.625, ((0, 4),)),
        "cross_out_bias": centred(key_list[10], (D,), 0.3, 2.0, (), jnp.float32),
        "cross_gain": jnp.clip(1.0 + 0.1 * jax.random.normal(key_list[11], (D,), jnp.float32), 0.5, 1.5),
        "cross_shift": centred(key_list[12], (D,), 0.3, 2.0, (), jnp.float32),
        "self_project": centred(key_list[13], (2, 3, D, D), D ** -0.5, 0.21875, ((3, 4),)),
        "self_bias": centred(key_list[14], (2, 2, D), 0.3, 2.0, ((2, 4),), jnp.float32),
        "self_out": centred(key_list[15], (2, D, D), (D // 8) ** -0.5, 0.625, ((1, 4),)),
        "self_out_bias": centred(key_list[16], (2, D), 0.3, 2.0, (), jnp.float32),
        "self_gain": jnp.clip(1.0 + 0.1 * jax.random.normal(key_list[17], (2, D), jnp.float32), 0.5, 1.5),
        "self_shift": centred(key_list[18], (2, D), 0.3, 2.0, (), jnp.float32),
        "feed_in": centred(key_list[19], (2, D, FF), D ** -0.5, 0.21875, ((2, 4),)),
        "feed_in_bias": centred(key_list[20], (2, FF), 0.3, 2.0, ((1, 4),), jnp.float32),
        "feed_out": centred(key_list[21], (2, FF, D), (FF // 2) ** -0.5, 0.15625, ((1, 4),)),
        "feed_out_bias": centred(key_list[22], (2, D), 0.3, 2.0, (), jnp.float32),
        "feed_gain": jnp.clip(1.0 + 0.1 * jax.random.normal(key_list[23], (2, D), jnp.float32), 0.5, 1.5),
        "feed_shift": centred(key_list[24], (2, D), 0.3, 2.0, (), jnp.float32),
    }


@jax.custom_vjp
def low(v):
    return lax.optimization_barrier(v.astype(jnp.bfloat16)).astype(jnp.float32)

@jax.custom_vjp
def low_back(v):
    return v

def low_keep(v):
    return (low(v), None)

def low_pass(kept, grad):
    return (grad,)

def back_keep(v):
    return (v, None)

def back_low(kept, grad):
    return (low(grad),)
low.defvjp(low_keep, low_pass)
low_back.defvjp(back_keep, back_low)
layer_eps = 1e-06
masked_score = -1e+30
highest = lax.Precision.HIGHEST

def both_round(values):
    return low(low_back(values))

def layer_norm(pre_norm, norm_gain, norm_shift):
    center = pre_norm - lax.optimization_barrier(jnp.mean(pre_norm, axis=-1, keepdims=True))
    variance = lax.optimization_barrier(jnp.mean(center * center, axis=-1, keepdims=True))
    return center * lax.rsqrt(variance + layer_eps) * norm_gain + norm_shift

def project(inputs, weight):
    return jnp.einsum('itd,de->ite', inputs, weight, precision=highest)

def split_heads(packed):
    return packed.reshape(packed.shape[0], packed.shape[1], -1, HEAD_DIM)

def project_three(inputs, weight_three, bias_two):
    queries = both_round(project(inputs, weight_three[0]) + bias_two[0])
    key_rows = both_round(project(inputs, weight_three[1]))
    value_rows = both_round(project(inputs, weight_three[2]) + bias_two[1])
    return (split_heads(queries), split_heads(key_rows), split_heads(value_rows))

def attend(queries, key_rows, value_rows, key_count):
    scores = low_back(jnp.einsum('iqhd,ikhd->ihqk', queries, key_rows, precision=highest) * HEAD_DIM ** (-0.5))
    valid_keys = jnp.arange(key_rows.shape[1])[None, :] < key_count[:, None]
    scores = jnp.where(valid_keys[:, None, None, :], scores, masked_score)
    top_score = lax.optimization_barrier(jnp.max(scores, axis=-1, keepdims=True))
    weights = jnp.exp(scores - top_score)
    probabilities = weights / lax.optimization_barrier(jnp.sum(weights, axis=-1, keepdims=True))
    context = jnp.einsum('ihqk,ikhd->iqhd', low(probabilities), value_rows, precision=highest)
    context = both_round(context)
    return context.reshape(context.shape[0], context.shape[1], -1)

def forward(inputs, counts, params):
    cross_project, cross_bias, cross_out, cross_out_bias, cross_gain, cross_shift, self_project, self_bias, self_out, self_out_bias, self_gain, self_shift, feed_in, feed_in_bias, feed_out, feed_out_bias, feed_gain, feed_shift = params
    cross_heads = [project_three(inputs[stream], cross_project, cross_bias) for stream in range(2)]
    middle = []
    for stream in range(2):
        partner = 1 - stream
        context = attend(cross_heads[stream][0], cross_heads[partner][1], cross_heads[partner][2], counts[partner])
        branch = low_back(project(context, cross_out))
        middle.append(layer_norm(inputs[stream] + branch + cross_out_bias, cross_gain, cross_shift))
    results = []
    for stream in range(2):
        queries, key_rows, value_rows = project_three(low(middle[stream]), self_project[stream], self_bias[stream])
        context = attend(queries, key_rows, value_rows, counts[stream])
        branch = low_back(project(context, self_out[stream]))
        second = layer_norm(middle[stream] + branch + self_out_bias[stream], self_gain[stream], self_shift[stream])
        hidden_pre = low_back(project(low(second), feed_in[stream]) + feed_in_bias[stream])
        hidden = low(jax.nn.gelu(hidden_pre, approximate=False))
        branch = low_back(project(hidden, feed_out[stream]))
        results.append(layer_norm(second + branch + feed_out_bias[stream], feed_gain[stream], feed_shift[stream]))
    return (results[0], results[1])

def reference(language, visual, word_count, region_count, task_flags, grad_language, grad_visual, cross_project, cross_bias, cross_out, cross_out_bias, cross_gain, cross_shift, self_project, self_bias, self_out, self_out_bias, self_gain, self_shift, feed_in, feed_in_bias, feed_out, feed_out_bias, feed_gain, feed_shift):
    params = tuple((weight.astype(jnp.float32) for weight in (cross_project, cross_bias, cross_out, cross_out_bias, cross_gain, cross_shift, self_project, self_bias, self_out, self_out_bias, self_gain, self_shift, feed_in, feed_in_bias, feed_out, feed_out_bias, feed_gain, feed_shift)))
    flag_values = task_flags.astype(jnp.float32)
    word_weight = jnp.where(jnp.arange(WORDS)[None, :] == 0, jnp.maximum(flag_values[:, 1:2], flag_values[:, 2:3]), flag_values[:, 0:1])
    cot_language = grad_language.astype(jnp.float32) * word_weight[:, :, None]
    cot_visual = grad_visual.astype(jnp.float32) * flag_values[:, 0:1, None]

    def by_block(packed):
        return packed.reshape((N_DP, -1) + packed.shape[1:])
    block_inputs = (by_block(language.astype(jnp.float32)), by_block(visual.astype(jnp.float32)), by_block(word_count), by_block(region_count), by_block(cot_language), by_block(cot_visual))

    def block_step(running, block_data):
        lang_block, vis_block, words_block, regions_block, cot_lang, cot_vis = block_data
        outputs, pullback = jax.vjp(lambda first_stream, second_stream, weight_set: forward((first_stream, second_stream), (words_block, regions_block), weight_set), lang_block, vis_block, params)
        grad_first, grad_second, grad_weights = pullback((cot_lang, cot_vis))
        running = jax.tree.map(lambda running_sum, block_grad: running_sum + block_grad, running, grad_weights)
        return (running, (outputs[0].astype(jnp.bfloat16), outputs[1].astype(jnp.bfloat16), grad_first, grad_second))
    zero_grads = jax.tree.map(jnp.zeros_like, params)
    totals, stacked = lax.scan(block_step, zero_grads, block_inputs)
    language_out = stacked[0].reshape((ITEMS, WORDS, D))
    visual_out = stacked[1].reshape((ITEMS, REGIONS, D))
    grad_language_in = stacked[2].reshape((ITEMS, WORDS, D))
    grad_visual_in = stacked[3].reshape((ITEMS, REGIONS, D))
    return (language_out, visual_out, grad_language_in, grad_visual_in, totals[0], totals[1], totals[2], totals[3], totals[4], totals[5], totals[6], totals[7], totals[8], totals[9], totals[10], totals[11], totals[12], totals[13], totals[14], totals[15], totals[16], totals[17])
```

```python
import functools

import jax
import jax.numpy as jnp
from jax import lax
from jax.experimental import pallas as pl
from jax.experimental.pallas import tpu as pltpu
from jax.sharding import PartitionSpec as P

D = 768
HEAD_DIM = 64
LAYER_EPS = 1e-06
MASKED = -1e30
GROUP = 8
MESH = pl.DeviceIdType.MESH
BF = jnp.bfloat16
F32 = jnp.float32


def place():
    dp = lax.axis_index("dp")
    z = lax.axis_index("tensor")
    core = dp % 2
    bx = (dp // 2) % 2
    by = (dp // 4) % 2
    return dp, z, core, bx, by


def greet(targets):
    barrier = pltpu.get_barrier_semaphore()
    count = 0
    for device, valid in targets:
        if valid is None:
            pl.semaphore_signal(barrier, inc=1, device_id=device, device_id_type=MESH)
            count = count + 1
        else:

            @pl.when(valid)
            def _(device=device):
                pl.semaphore_signal(barrier, inc=1, device_id=device, device_id_type=MESH)

            count = count + valid.astype(jnp.int32)
    pl.semaphore_wait(barrier, count)


K_Z, K_X, K_Y, K_A, K_B, K_C, K_Z2 = 0, 1, 2, 3, 4, 5, 10
TILE = 256


def gather_steps(nz, units, whole, send_sem, recv_sem):
    dp, z, core, bx, by = place()
    low = dp % GROUP
    dev_c = (dp + 1 - 2 * core, z)
    dev_x = (dp + 2 - 4 * bx, z)
    dev_y = (dp + 4 - 8 * by, z)
    sl_x = low + 2 - 4 * bx
    sl_y = low + 4 - 8 * by
    sl_d = low + 2 - 4 * bx + 4 - 8 * by

    def copy(src, dst, u, k, kind, device):
        return pltpu.make_async_remote_copy(
            src_ref=src, dst_ref=dst, send_sem=send_sem.at[u, k, kind], recv_sem=recv_sem.at[u, k, kind], device_id=device, device_id_type=MESH
        )

    def is_attention(u):
        return len(units[u]) == 2

    def part(u, j, sl, half):
        if is_attention(u):
            size = units[u][1].shape[0]
            step = size // GROUP
            rows = pl.ds(pl.multiple_of(j * size + sl * step, 8), step)
            return whole[u].at[:, rows] if half is None else whole[u].at[2 * half : 2 * half + 2, rows]
        step = units[u][0].shape[0] // GROUP
        if half is None:
            return whole[u].at[j, pl.ds(pl.multiple_of(sl * step, 8), step)]
        return whole[u].at[j, pl.ds(pl.multiple_of(sl * step + half * (step // 2), 8), step // 2)]

    def z_copies(u, k, j, device, sending):
        if is_attention(u):
            proj, out = units[u]
            size = out.shape[0]
            step = size // GROUP
            mine = pl.ds(pl.multiple_of(low * step, 8), step)
            to = pl.ds(pl.multiple_of(j * size + low * step, 8), step)
            pairs = ((proj.at[:, mine], whole[u].at[0:3, to]), (out.at[mine], whole[u].at[3, to]))
        else:
            step = units[u][0].shape[0] // GROUP
            pairs = ((units[u][0].at[pl.ds(pl.multiple_of(low * step, 8), step)], part(u, j, low, None)),)
        return [copy(src if sending else dst, dst, u, k - 1, (K_Z, K_Z2)[i], device) for i, (src, dst) in enumerate(pairs)]

    def z_send(u, k):
        for c in z_copies(u, k, z, (dp, (z + k) % nz), True):
            c.start()

    def source(k):
        return (z + nz - k) % nz

    def peer(u, k, kind, sending):
        if kind < K_C:
            sent, got, half, device = {
                K_X: (low, sl_x, None, dev_x),
                K_Y: (low, sl_y, None, dev_y),
                K_A: (sl_x, sl_d, 0, dev_y),
                K_B: (sl_y, sl_d, 1, dev_x),
            }[kind]
        else:
            sent, half = ((low, None), (sl_x, None), (sl_y, None), (sl_d, 0), (sl_d, 1))[kind - K_C]
            device = dev_c
            got = sent + 1 - 2 * core
        block = part(u, source(k), sent if sending else got, half)
        return copy(block, block, u, k - 1, kind, device)

    def stage1(u, k):
        for c in z_copies(u, k, source(k), dev_x, False):
            c.wait_recv()
        for kind in (K_X, K_Y, K_C):
            peer(u, k, kind, True).start()

    def stage2(u, k):
        peer(u, k, K_X, False).wait_recv()
        peer(u, k, K_A, True).start()
        peer(u, k, K_C + 1, True).start()
        peer(u, k, K_Y, False).wait_recv()
        peer(u, k, K_B, True).start()
        peer(u, k, K_C + 2, True).start()

    def stage3(u, k):
        peer(u, k, K_A, False).wait_recv()
        peer(u, k, K_C + 3, True).start()
        peer(u, k, K_B, False).wait_recv()
        peer(u, k, K_C + 4, True).start()

    sequence = [(u, k) for u in range(len(units)) for k in range(1, nz)]

    def step(n):
        if n < len(sequence):
            u, k = sequence[n]
            stage1(u, k)
            if u + 2 < len(units):
                z_send(u + 2, k)
        if 1 <= n < len(sequence) + 1:
            stage2(*sequence[n - 1])
        if 2 <= n < len(sequence) + 2:
            stage3(*sequence[n - 2])

    def arrived(u):
        for k in range(1, nz):
            for kind in range(K_C, K_C + 5):
                peer(u, k, kind, False).wait_recv()

    def sent(u):
        for k in range(1, nz):
            for c in z_copies(u, k, z, (dp, (z + k) % nz), True):
                c.wait_send()
            for kind in range(K_X, K_C + 5):
                peer(u, k, kind, True).wait_send()

    def loads(u, dst, sem):
        if is_attention(u):
            proj, out = units[u]
            size = out.shape[0]
            own = pl.ds(pl.multiple_of(z * size, 8), size)
            pairs = [(proj, dst.at[0:3, own]), (out, dst.at[3, own])]
            for k in range(1, nz):
                rows = pl.ds(pl.multiple_of(source(k) * size, 8), size)
                pairs.append((whole[u].at[:, rows], dst.at[:, rows]))
        else:
            pairs = [(units[u][0], dst.at[z])]
            for k in range(1, nz):
                pairs.append((whole[u].at[source(k)], dst.at[source(k)]))
        return [pltpu.make_async_copy(src, to, sem.at[i]) for i, (src, to) in enumerate(pairs)]

    return z_send, step, arrived, sent, loads


def project(x_ref, xrows, w_ref, w0, bias_ref, b0, out_ref):
    x = x_ref[xrows, :]
    tiles = D // TILE

    def body(i, carry):
        c, t = i // tiles, i % tiles
        at = pl.ds(pl.multiple_of(t * TILE, TILE), TILE)
        y = dot(x, w_ref[w0 + c, at, :], ((1,), (1,)))
        out_ref[c, xrows, at] = (y + bias_ref[pl.ds(b0 + c, 1), at]).astype(BF)
        return carry

    lax.fori_loop(0, 3 * tiles, body, 0)


def half_lanes():
    lane = lax.broadcasted_iota(jnp.int32, (1, 2 * HEAD_DIM), 1)
    return lane < HEAD_DIM


def attend(qkv_ref, ctx_ref, p_ref, mask_ref, q0, lq, k0, lk):
    first = half_lanes()
    keep = [jnp.where(first, HEAD_DIM**-0.5, 0.0).astype(BF), jnp.where(first, 0.0, HEAD_DIM**-0.5).astype(BF)]

    def body(pair, carry):
        lanes = pl.ds(pl.multiple_of(pair * 2 * HEAD_DIM, 2 * HEAD_DIM), 2 * HEAD_DIM)
        for g in range(2):
            qr, kr = pl.ds(q0 + g * lq, lq), pl.ds(k0 + g * lk, lk)
            q, k, v = qkv_ref[0, qr, lanes], qkv_ref[1, kr, lanes], qkv_ref[2, kr, lanes]
            parts = []
            for h in range(2):
                s = dot(q * keep[h], k, ((1,), (1,))) + mask_ref[g]
                w = jnp.exp(s - jnp.max(s, axis=1, keepdims=True))
                pb = (w * (1.0 / jnp.sum(w, axis=1, keepdims=True))).astype(BF)
                p_ref[g, 2 * pair + h] = pb
                parts.append(dot(pb, v, ((1,), (0,))))
            ctx_ref[qr, lanes] = jnp.where(first, parts[0], parts[1]).astype(BF)
        return carry

    lax.fori_loop(0, D // (2 * HEAD_DIM), body, 0, unroll=2)


def out_norm(ctx_ref, start, count, w_ref, wi, resid_ref, vec_ref, v0, pre_ref, hat_ref, rstd_ref, full_ref, low_ref):
    rows = pl.ds(start, count)
    ctx = ctx_ref[rows, :]

    def tile(t, carry):
        at = pl.ds(pl.multiple_of(t * TILE, TILE), TILE)
        y = dot(ctx, w_ref[wi, :, at], ((1,), (0,)))
        pre_ref[rows, at] = y + resid_ref[rows, at].astype(F32) + vec_ref[pl.ds(v0, 1), at]
        return carry

    lax.fori_loop(0, D // TILE, tile, 0)
    gain, shift = vec_ref[v0 + 1 : v0 + 2, :], vec_ref[v0 + 2 : v0 + 3, :]

    def norm(i, carry):
        r = pl.ds(pl.multiple_of(start + i * 32, 16), 32)
        x = pre_ref[r, :]
        center = x - jnp.sum(x, axis=1, keepdims=True) * (1.0 / D)
        rstd = lax.rsqrt(jnp.sum(center * center, axis=1, keepdims=True) * (1.0 / D) + LAYER_EPS)
        hat = center * rstd
        y = hat * gain + shift
        hat_ref[r, :] = hat.astype(BF)
        rstd_ref[r, :] = jnp.broadcast_to(rstd, (32, 128))
        full_ref[r, :] = y
        low_ref[r, :] = y.astype(BF)
        return carry

    lax.fori_loop(0, count // 32, norm, 0)


def by_group(src_ref, dst_ref, start, slots):
    half = slots * GROUP // 2
    low = lax.broadcasted_iota(jnp.int32, (8, D), 0) < 4

    def body(i, carry):
        a = [src_ref[4 * i + t].astype(F32) for t in range(4)]
        for g in range(2):
            rows = []
            for t in (0, 2):
                one, two = (a[t], pltpu.roll(a[t + 1], 4, 0)) if g == 0 else (pltpu.roll(a[t], 4, 0), a[t + 1])
                rows.append(jnp.where(low, one, two))
            at = pl.ds(pl.multiple_of(start + g * half + 16 * i, 16), 16)
            dst_ref[at, :] = jnp.concatenate(rows, axis=0).astype(dst_ref.dtype)
        return carry

    lax.fori_loop(0, slots // 4, body, 0)


def fill_masks(mask_refs, counts, first):
    for n, (ref, count) in enumerate(zip(mask_refs, counts)):
        for g in range(2):
            shape = ref.shape[1:]
            row, col = (lax.broadcasted_iota(jnp.int32, shape, d) for d in range(2))
            item = jnp.bitwise_and(col, 3)
            limit = jnp.zeros(shape, jnp.int32)
            for j in range(4):
                limit = jnp.where(item == j, count[first + 4 * g + j], limit)
            seen = jnp.logical_and(jnp.bitwise_and(row, 3) == item, jnp.right_shift(col, 2) < limit)
            ref[g] = jnp.where(seen, 0.0, MASKED).astype(F32)


SLOTS = 4
PARTS = 3


def scatter_steps(nz, mixed, slot_bufs, send_sem, recv_sem, rs_out):
    grad, crecv, xa, yb, ya, xb, zbuf, zrecv = slot_bufs
    dp, z, core, bx, by = place()
    dev_c = (dp + 1 - 2 * core, z)
    dev_x = (dp + 2 - 4 * bx, z)
    dev_y = (dp + 4 - 8 * by, z)
    rows, width = crecv.shape[3], crecv.shape[4]
    half = width // 2
    lo, hi = pl.ds(0, half), pl.ds(half, half)
    zw = width // nz
    S_C, S_XA, S_YB, S_YA, S_XB, S_Z = 0, 1, 2, 3, 4, 5

    def part(i, y, x, c, lanes):
        return grad.at[(i // PARTS) % 2, y, x, c, pl.ds((i % PARTS) * rows, rows), lanes]

    def remote(src, dst, s, k, device):
        return pltpu.make_async_remote_copy(
            src_ref=src, dst_ref=dst, send_sem=send_sem.at[s, k], recv_sem=recv_sem.at[s, k], device_id=device, device_id_type=MESH
        )

    every = slice(None)

    def core_copy(i):
        s = i % SLOTS
        return remote(part(i, every, every, 1 - core, every), crecv.at[s], s, S_C, dev_c)

    def xa_copy(i):
        s = i % SLOTS
        return remote(part(i, every, 1 - bx, core, lo), xa.at[s], s, S_XA, dev_x)

    def yb_copy(i):
        s = i % SLOTS
        return remote(part(i, 1 - by, every, core, hi), yb.at[s], s, S_YB, dev_y)

    def ya_copy(i):
        s = i % SLOTS
        return remote(part(i, 1 - by, bx, core, lo), ya.at[s], s, S_YA, dev_y)

    def xb_copy(i):
        s = i % SLOTS
        return remote(part(i, by, 1 - bx, core, hi), xb.at[s], s, S_XB, dev_x)

    def z_copy(s, k):
        return remote(zbuf.at[s, (z + k) % nz], zrecv.at[s, k - 1], s, S_Z + k - 1, (dp, (z + k) % nz))

    def merge(dst, src):
        for r in range(0, rows, 16):
            at = pl.ds(r, 16)
            dst[at] = dst[at] + src[at]

    def stage_a(i):
        s = i % SLOTS
        core_copy(i).wait()

        def body(j, carry):
            merge(part(i, j // 2, j % 2, core, every), crecv.at[s, j // 2, j % 2])
            return carry

        lax.fori_loop(0, 4, body, 0)
        xa_copy(i).start()
        yb_copy(i).start()

    def stage_b(i):
        s = i % SLOTS
        xa_copy(i).wait()
        yb_copy(i).wait()

        def body(j, carry):
            merge(part(i, j, bx, core, lo), xa.at[s, j])
            merge(part(i, by, j, core, hi), yb.at[s, j])
            return carry

        lax.fori_loop(0, 2, body, 0)
        ya_copy(i).start()
        xb_copy(i).start()

    def stage_c(i):
        s = i % SLOTS
        ya_copy(i).wait()
        xb_copy(i).wait()
        own = part(i, by, bx, core, every)
        for r in range(0, rows, 16):
            at = pl.ds(r, 16)
            left = own[at, lo] + ya[s, at, :]
            right = own[at, hi] + xb[s, at, :]
            full = jnp.concatenate([left, right], axis=1)
            for t in range(nz):
                if mixed[i // PARTS]:
                    sub = zw // 4
                    row = [full[:, m * (width // 4) + t * sub : m * (width // 4) + (t + 1) * sub] for m in range(4)]
                    zbuf[s, t, at, :] = jnp.concatenate(row, axis=1)
                else:
                    zbuf[s, t, at, :] = full[:, t * zw : (t + 1) * zw]
        for k in range(1, nz):
            z_copy(s, k).start()

    def stage_d(i):
        s = i % SLOTS
        for k in range(1, nz):
            z_copy(s, k).wait()
        for r in range(0, rows, 16):
            at = pl.ds(r, 16)
            total = zbuf[s, z, at, :].astype(F32)
            for k in range(nz - 1):
                total = total + zrecv[s, k, at, :].astype(F32)
            rs_out[i, at, :] = total

    return core_copy, stage_a, stage_b, stage_c, stage_d


def small_steps(nz, small, sbuf, srecv, szrecv, small_out, send_sem, recv_sem):
    dp, z, core, bx, by = place()
    devs = ((dp + 1 - 2 * core, z), (dp + 2 - 4 * bx, z), (dp + 4 - 8 * by, z))

    def remote(src, dst, k, device):
        return pltpu.make_async_remote_copy(
            src_ref=src, dst_ref=dst, send_sem=send_sem.at[k], recv_sem=recv_sem.at[k], device_id=device, device_id_type=MESH
        )

    def pair(k):
        return remote(sbuf.at[k], srecv.at[k], k, devs[k])

    def along_z(k, sending):
        return remote(sbuf.at[3], szrecv.at[z if sending else (z + nz - k) % nz], 2 + k, (dp, (z + k) % nz))

    def stage(k):
        if k == 0:
            sbuf[0] = small[...]
            pair(0).start()
        elif k < 4:
            pair(k - 1).wait()
            sbuf[k] = sbuf[k - 1] + srecv[k - 1]
            if k < 3:
                pair(k).start()
            else:
                szrecv[z] = sbuf[3]
                for i in range(1, nz):
                    along_z(i, True).start()
        else:
            for i in range(1, nz):
                along_z(i, True).wait_send()
                along_z(i, False).wait_recv()
            total = szrecv[0]
            for i in range(1, nz):
                total = total + szrecv[i]
            small_out[...] = total

    return stage


def eighth(x):
    return jnp.sum(x.reshape(x.shape[0] // 8, 8, x.shape[1]), axis=0)


def transpose_into(t_ref, x_ref, start, count):
    for i in range(D // 128):
        t_ref[i * 128 : (i + 1) * 128, 0:count] = x_ref[pl.ds(start, count), i * 128 : (i + 1) * 128].T


def feed_forward(nb_ref, rows, w_ref, bias_ref, b0, h_ref, slope_ref, first, last):
    x = nb_ref[rows, :]
    tiles = D // TILE

    def body(i, carry):
        zb, t = i // tiles, i % tiles
        at = pl.ds(pl.multiple_of(t * TILE, TILE), TILE)
        u = dot(x, w_ref[zb, :, at], ((1,), (0,))) + bias_ref[pl.ds(b0 + zb, 1), at]
        phi = 0.5 + 0.5 * lax.erf(u * 0.5**0.5)
        h_ref[zb, rows, at] = (u * phi).astype(BF)
        slope_ref[zb, rows, at] = (phi + u * (jnp.exp(-0.5 * u * u) * 0.3989422804014327)).astype(BF)
        return carry

    lax.fori_loop(first * tiles, last * tiles, body, 0)


def feed_out_rows(h_ref, rows, w_ref, nn_ref, vec_ref, v0, res_ref):
    def body(t, carry):
        at = pl.ds(pl.multiple_of(t * TILE, TILE), TILE)
        y = nn_ref[rows, at] + vec_ref[pl.ds(v0, 1), at]
        for zb in range(h_ref.shape[0]):
            y = y + dot(h_ref[zb, rows, :], w_ref[zb, :, at], ((1,), (0,)))
        res_ref[rows, at] = y
        return carry

    lax.fori_loop(0, D // TILE, body, 0)


def norm_grad(hat, rstd, gain, g, acc):
    scaled = g * gain
    dz = rstd * (
        scaled - jnp.sum(scaled, axis=1, keepdims=True) * (1.0 / D) - hat * (jnp.sum(scaled * hat, axis=1, keepdims=True) * (1.0 / D))
    )
    return dz, (acc[0] + eighth(dz), acc[1] + eighth(g * hat), acc[2] + eighth(g))


def no_sums():
    return tuple(jnp.zeros((8, D), F32) for _ in range(3))


def keep_sums(acc, small, row):
    for i in range(3):
        small[row + i : row + i + 1, :] = jnp.sum(acc[i], axis=0, keepdims=True)


def last_norm(start, count, res_ref, vec_ref, v0, cot_ref, weight_ref, result_ref, db_ref, small, row):
    gain, shift = vec_ref[v0 + 1 : v0 + 2, :], vec_ref[v0 + 2 : v0 + 3, :]

    def body(i, acc):
        r = pl.ds(pl.multiple_of(start + i * 32, 16), 32)
        x = res_ref[r, :]
        center = x - jnp.sum(x, axis=1, keepdims=True) * (1.0 / D)
        rstd = lax.rsqrt(jnp.sum(center * center, axis=1, keepdims=True) * (1.0 / D) + LAYER_EPS)
        hat = center * rstd
        result_ref[r, :] = (hat * gain + shift).astype(BF)
        g = cot_ref[r, :].astype(F32) * weight_ref[r, 0:1]
        dz, acc = norm_grad(hat, rstd, gain, g, acc)
        res_ref[r, :] = dz
        db_ref[r, :] = dz.astype(BF)
        return acc

    keep_sums(lax.fori_loop(0, count // 32, body, no_sums()), small, row)


def norm_back(start, count, res_ref, hat_ref, rstd_ref, vec_ref, gain_row, db_ref, small, row):
    gain = vec_ref[gain_row : gain_row + 1, :]

    def body(i, acc):
        r = pl.ds(pl.multiple_of(start + i * 32, 16), 32)
        dz, acc = norm_grad(hat_ref[r, :].astype(F32), rstd_ref[r, 0:1], gain, res_ref[r, :], acc)
        res_ref[r, :] = dz
        db_ref[r, :] = dz.astype(BF)
        return acc

    keep_sums(lax.fori_loop(0, count // 32, body, no_sums()), small, row)


def hidden_grad(db_ref, rows, w_ref, slope_ref, small, row):
    db = db_ref[rows, :]
    tiles = D // TILE

    def body(i, carry):
        zb, t = i // tiles, i % tiles
        at = pl.ds(pl.multiple_of(t * TILE, TILE), TILE)
        du = (dot(db, w_ref[zb, at, :], ((1,), (1,))) * slope_ref[zb, rows, at].astype(F32)).astype(BF)
        slope_ref[zb, rows, at] = du
        small[pl.ds(row + zb, 1), at] = jnp.sum(eighth(du.astype(F32)), axis=0, keepdims=True)
        return carry

    lax.fori_loop(0, slope_ref.shape[0] * tiles, body, 0)


def add_products(res_ref, out_ref, rows, x_ref, count, w_ref, transposed):
    def body(t, carry):
        at = pl.ds(pl.multiple_of(t * TILE, TILE), TILE)
        y = res_ref[rows, at]
        for c in range(count):
            if transposed:
                y = y + dot(x_ref[c, rows, :], w_ref[c, at, :], ((1,), (1,)))
            else:
                y = y + dot(x_ref[c, rows, :], w_ref[c, :, at], ((1,), (0,)))
        out_ref[rows, at] = y
        return carry

    lax.fori_loop(0, D // TILE, body, 0)


def context_grad(db_ref, rows, w_ref, dctx_ref):
    db = db_ref[rows, :]

    def body(t, carry):
        at = pl.ds(pl.multiple_of(t * TILE, TILE), TILE)
        dctx_ref[rows, at] = dot(db, w_ref[3, at, :], ((1,), (1,))).astype(BF)
        return carry

    lax.fori_loop(0, D // TILE, body, 0)


def attend_back(qkv_ref, dctx_ref, p_ref, out_ref, q0, lq, k0, lk, first_pair=0, last_pair=D // (2 * HEAD_DIM)):
    first = half_lanes()
    keep = [jnp.where(first, 1.0, 0.0).astype(BF), jnp.where(first, 0.0, 1.0).astype(BF)]

    def body(pair, carry):
        lanes = pl.ds(pl.multiple_of(pair * 2 * HEAD_DIM, 2 * HEAD_DIM), 2 * HEAD_DIM)
        for g in range(2):
            qr, kr = pl.ds(q0 + g * lq, lq), pl.ds(k0 + g * lk, lk)
            q, k, v, dc = qkv_ref[0, qr, lanes], qkv_ref[1, kr, lanes], qkv_ref[2, kr, lanes], dctx_ref[qr, lanes]
            dq, dk, dv = [], [], []
            for h in range(2):
                pb = p_ref[g, 2 * pair + h]
                p = pb.astype(F32)
                dp = dot(dc * keep[h], v, ((1,), (1,)))
                ds = (p * (dp - jnp.sum(p * dp, axis=1, keepdims=True))).astype(BF)
                dq.append(dot(ds, k, ((1,), (0,))))
                dk.append(dot(ds, q, ((0,), (0,))))
                dv.append(dot(pb, dc, ((0,), (0,))))
            out_ref[0, qr, lanes] = (jnp.where(first, dq[0], dq[1]) * HEAD_DIM**-0.5).astype(BF)
            out_ref[1, kr, lanes] = (jnp.where(first, dk[0], dk[1]) * HEAD_DIM**-0.5).astype(BF)
            out_ref[2, kr, lanes] = jnp.where(first, dv[0], dv[1]).astype(BF)
        return carry

    lax.fori_loop(first_pair, last_pair, body, 0)


def bias_sums(x_ref, rows, count, small, row_q, row_v, add):
    ones = jnp.ones((8, count), BF)
    for c, row in ((0, row_q), (2, row_v)):
        total = dot(ones, x_ref[c, rows, :], ((1,), (0,)))[0:1, :]
        small[row : row + 1, :] = total


def grad_tiles(grad_ref, m, t_ref, count, x_ref, rows, first, last, lane0, mats):
    size = grad_ref.shape[4]
    left = t_ref[:, 0:count]
    tiles = D // TILE

    def body(i, carry):
        b, t = i // tiles, i % tiles
        at = pl.ds(pl.multiple_of(t * TILE, TILE), TILE)
        right = x_ref[b, rows, at] if mats else x_ref[rows, at]
        y = dot(left, right, ((1,), (0,))).astype(BF)
        lanes = pl.ds(pl.multiple_of(lane0 + i * TILE, TILE), TILE)
        grad_ref[m % 2, :, :, :, :, lanes] = y.reshape(2, 2, 2, size, TILE)
        return carry

    lax.fori_loop(first * tiles, last * tiles, body, 0)


CROSS, SELF1, IN1, OUT1, SELF0, IN0, OUT0 = range(7)
MIXED = (False, False, True, False, False, True, True)


def layer_kernel(nz, lens, *refs):
    cp, co, sp, so, fi, fo, word_count, region_count, flags = refs[:9]
    lang, vis, cot_lang, cot_vis, cross_b, self_b, feed_b = refs[9:16]
    cob, cg, cs, sob, sg, ss, fob, fg, fs = refs[16:25]
    whole = refs[25:32]
    rs_out, small_out, result, res = refs[32:36]
    wb0, wb1, wb2, x, qkv_c, ctx_c, p_c0, p_c1, hat1, rstd1, mb = refs[36:47]
    qkv_s, ctx_s, p_s0, p_s1, hat2, rstd2, mid, nb, hid, slope, db, dctx, t1, t2, small = refs[47:62]
    grad, crecv, xa, yb, ya, xb, zbuf, zrecv, sbuf, srecv, szrecv = refs[62:73]
    bias_src, bias_all, bias_ref, vec, weight = refs[73:78]
    masks = refs[78:82]
    send_sem, recv_sem, w_sem, bias_send, bias_recv, rs_send, rs_recv, small_send, small_recv = refs[82:]
    dp, z, core, bx, by = place()
    lw, lv = lens
    rw, rv = 2 * lw, 2 * lv
    start, count = (0, rw), (rw, rv)
    rows = (pl.ds(0, rw), pl.ds(rw, rv))
    every = pl.ds(0, rw + rv)

    bias_src[...] = jnp.zeros_like(bias_src)
    part = cross_b.shape[1]
    for t in range(nz):

        @pl.when(z == t)
        def _(t=t):
            lanes = slice(t * part, (t + 1) * part)
            for i in range(2):
                bias_src[2 * i : 2 * i + 1, lanes] = cross_b[i : i + 1, :]
                for s in range(2):
                    bias_src[3 + 3 * s + 2 * i : 4 + 3 * s + 2 * i, lanes] = self_b[s, i : i + 1, :]
            for s in range(2):
                bias_src[9 + nz * s + t : 10 + nz * s + t, :] = feed_b[s : s + 1, :]

    targets = [((dp + 1 - 2 * core, z), None), ((dp + 2 - 4 * bx, z), None), ((dp + 4 - 8 * by, z), None)]
    for k in range(1, nz):
        targets.append(((dp, (z + k) % nz), None))
    greet(targets)
    units = (
        (cp, co),
        (sp.at[1], so.at[1]),
        (fi.at[1],),
        (fo.at[1],),
        (sp.at[0], so.at[0]),
        (fi.at[0],),
        (fo.at[0],),
    )
    z_send, gather, arrived, sent, loads = gather_steps(nz, units, whole, send_sem, recv_sem)
    slot_bufs = (grad, crecv, xa, yb, ya, xb, zbuf, zrecv)
    core_copy, stage_a, stage_b, stage_c, stage_d = scatter_steps(nz, MIXED, slot_bufs, rs_send, rs_recv, rs_out)
    small_stage = small_steps(nz, small, sbuf, srecv, szrecv, small_out, small_send, small_recv)
    pieces = len(MIXED) * PARTS

    def scatter(n):
        if n + 1 < pieces:
            core_copy(n + 1).start()
        if n < pieces:
            stage_a(n)
        if 1 <= n < pieces + 1:
            stage_b(n - 1)
        if 2 <= n < pieces + 2:
            stage_c(n - 2)
        if n >= 3:
            stage_d(n - 3)

    def bias_copy(k, sending):
        return pltpu.make_async_remote_copy(
            src_ref=bias_src,
            dst_ref=bias_all.at[z if sending else (z + nz - k) % nz],
            send_sem=bias_send.at[k],
            recv_sem=bias_recv.at[k],
            device_id=(dp, (z + k) % nz),
            device_id_type=MESH,
        )

    def fetch(u, dst, turn=0, wait=True):
        if turn == 0:
            arrived(u)
        for c in loads(u, dst, w_sem.at[u + turn]):
            c.start()

    def ready(u, dst, turn=0):
        for c in loads(u, dst, w_sem.at[u + turn]):
            c.wait()

    cot = dctx

    def prepare():
        for i, ref in enumerate((cob, cg, cs)):
            vec[i : i + 1, :] = ref[...].reshape(1, D)
        for s in range(2):
            for i, ref in enumerate((sob, sg, ss)):
                vec[3 + 3 * s + i : 4 + 3 * s + i, :] = ref[s : s + 1, :]
            for i, ref in enumerate((fob, fg, fs)):
                vec[9 + 3 * s + i : 10 + 3 * s + i, :] = ref[s : s + 1, :]
        by_group(lang, x, 0, lang.shape[0])
        by_group(vis, x, rw, vis.shape[0])
        by_group(cot_lang, cot, 0, cot_lang.shape[0])
        by_group(cot_vis, cot, rw, cot_vis.shape[0])
        fill_masks(masks, (region_count, word_count, word_count, region_count), z * GROUP)
        for s in range(2):
            for g in range(2):
                row = lax.broadcasted_iota(jnp.int32, (lens[s], 128), 0)
                item = jnp.bitwise_and(row, 3)
                value = jnp.zeros((lens[s], 128), F32)
                for j in range(4):
                    n = 4 * g + j
                    other = flags[0, n].astype(F32)
                    if s == 0:
                        answer = jnp.maximum(flags[1, n], flags[2, n]).astype(F32)
                        value = jnp.where(item == j, jnp.where(row < 4, answer, other), value)
                    else:
                        value = jnp.where(item == j, other, value)
                weight[start[s] + g * lens[s] : start[s] + (g + 1) * lens[s], :] = value

    def bias_sum():
        for k in range(1, nz):
            bias_copy(k, False).wait_recv()
        bias_all[z] = bias_src[...]
        total = bias_all[0]
        for k in range(1, nz):
            total = total + bias_all[k]
        bias_ref[...] = total

    w_self, w_in, w_out = (wb0, wb1), (wb2, wb2), (wb1, wb0)
    u_self, u_in, u_out = (SELF0, SELF1), (IN0, IN1), (OUT0, OUT1)

    def cross_project_all():
        ready(CROSS, wb0)
        bias_sum()
        project(x, every, wb0, 0, bias_ref, 0, qkv_c)

    def cross_forward(s):
        if s == 0:
            attend(qkv_c, ctx_c, p_c0, masks[0], 0, lw, rw, lv)
        else:
            attend(qkv_c, ctx_c, p_c1, masks[1], rw, lv, 0, lw)

    def cross_norm(s):
        out_norm(ctx_c, start[s], count[s], wb0, 3, x, vec, 0, res, hat1, rstd1, mid, mb)

    def self_project(s):
        ready(u_self[s], w_self[s])
        project(mb, rows[s], w_self[s], 0, bias_ref, 3 + 3 * s, qkv_s)

    def self_forward(s):
        attend(qkv_s, ctx_s, (p_s0, p_s1)[s], masks[2 + s], start[s], lens[s], start[s], lens[s])

    def self_norm(s):
        out_norm(ctx_s, start[s], count[s], w_self[s], 3, mid, vec, 3 + 3 * s, res, hat2, rstd2, mid, nb)

    def forward(s, first, last):
        if first == 0:
            ready(u_in[s], w_in[s])
        feed_forward(nb, rows[s], w_in[s], bias_ref, 9 + nz * s, hid, slope, first, last)

    def out_rows(s):
        ready(u_out[s], w_out[s])
        feed_out_rows(hid, rows[s], w_out[s], mid, vec, 9 + 3 * s, res)

    def norm3(s):
        last_norm(start[s], count[s], res, vec, 9 + 3 * s, cot, weight, result, db, small, 15 + 3 * s)

    def du(s):
        hidden_grad(db, rows[s], w_out[s], slope, small, 21 + nz * s)

    def dn(s):
        add_products(res, res, rows[s], slope, nz, w_in[s], True)

    def self_in(s):
        norm_back(start[s], count[s], res, hat2, rstd2, vec, 4 + 3 * s, db, small, 7 + 5 * s)
        context_grad(db, rows[s], w_self[s], dctx)

    def self_back(s, first, last):
        attend_back(qkv_s, dctx, (p_s0, p_s1)[s], hid, start[s], lens[s], start[s], lens[s], first, last)

    def self_sums(s):
        bias_sums(hid, rows[s], count[s], small, 5 + 5 * s, 6 + 5 * s, False)

    def dm(s):
        add_products(res, res, rows[s], hid, 3, w_self[s], False)

    def cross_in():
        ready(CROSS, wb1, 7)
        norm_back(0, rw + rv, res, hat1, rstd1, vec, 1, nb, small, 2)
        context_grad(nb, every, wb1, dctx)

    def cross_back(s):
        attend_back(qkv_c, dctx, (p_c0, p_c1)[s], slope, start[s], lens[s], start[1 - s], lens[1 - s])

    def cross_sums():
        bias_sums(slope, every, rw + rv, small, 0, 1, False)
        small_stage(0)

    def finish_rows():
        add_products(res, res, every, slope, 3, wb1, False)

    def grads(m):
        if m < 6:
            s = 1 - m // 3
            if m % 3 < 2:
                turned, src, right = ((t1, db, hid), (t2, nb, slope))[m % 3]
                transpose_into(turned, src, start[s], count[s])
                grad_tiles(grad, m, turned, count[s], right, rows[s], 0, nz, 0, True)
                return
            src, at, n, back, ctx, dqkv, dz = mb, start[s], count[s], rows[s], ctx_s, hid, db
        else:
            src, at, n, back, ctx, dqkv, dz = x, 0, rw + rv, every, ctx_c, slope, nb
        transpose_into(t1, dz, at, n)
        transpose_into(t2, src, at, n)
        grad_tiles(grad, m, t2, n, dqkv, back, 0, 3, 0, True)
        grad_tiles(grad, m, t1, n, ctx, back, 0, 1, 3 * D, False)

    for k in range(1, nz):
        z_send(0, k)
    for k in range(1, nz):
        bias_copy(k, True).start()
    for k in range(1, nz):
        z_send(1, k)
    prepare()
    for n in range(5):
        gather(n)
    fetch(CROSS, wb0)
    gather(5)
    cross_project_all()
    gather(6)
    cross_forward(1)
    gather(7)
    fetch(SELF1, wb1)
    cross_norm(1)
    gather(8)
    self_project(1)
    gather(9)
    self_forward(1)
    gather(10)
    fetch(IN1, wb2)
    self_norm(1)
    cross_forward(0)
    gather(11)
    forward(1, 0, 2)
    cross_norm(0)
    gather(12)
    forward(1, 2, nz)
    gather(13)
    fetch(OUT1, wb0)
    out_rows(1)
    norm3(1)
    gather(14)
    grads(0)
    core_copy(0).start()
    du(1)
    scatter(0)
    gather(15)
    grads(1)
    scatter(1)
    gather(16)
    fetch(SELF0, wb0)
    dn(1)
    self_in(1)
    scatter(2)
    gather(17)
    self_back(1, 0, 3)
    scatter(3)
    gather(18)
    self_back(1, 3, 6)
    scatter(4)
    gather(19)
    fetch(IN0, wb2)
    dm(1)
    self_sums(1)
    grads(2)
    scatter(5)
    gather(20)
    self_project(0)
    self_forward(0)
    scatter(6)
    gather(21)
    self_norm(0)
    forward(0, 0, nz)
    scatter(7)
    gather(22)
    fetch(OUT0, wb1)
    out_rows(0)
    norm3(0)
    grads(3)
    scatter(8)
    du(0)
    fetch(CROSS, wb1, 7)
    scatter(9)
    dn(0)
    scatter(10)
    grads(4)
    scatter(11)
    self_in(0)
    self_back(0, 0, 6)
    scatter(12)
    dm(0)
    cross_in()
    scatter(13)
    self_sums(0)
    grads(5)
    scatter(14)
    cross_back(0)
    scatter(15)
    cross_back(1)
    scatter(16)
    grads(6)
    scatter(17)
    cross_sums()
    scatter(18)
    small_stage(1)
    finish_rows()
    scatter(19)
    small_stage(2)
    scatter(20)
    small_stage(3)
    scatter(21)
    small_stage(4)
    scatter(22)
    scatter(23)
    for u in range(len(units)):
        sent(u)
    for k in range(1, nz):
        bias_copy(k, True).wait_send()


def layer(nz, lens, shards, counts, flags, inputs, biases, vectors):
    rows = 2 * sum(lens)
    lw, lv = lens
    nh = D // HEAD_DIM
    size = D // GROUP // PARTS
    width = 4 * D
    any_spec = pl.BlockSpec(memory_space=pl.ANY)
    vmem = pl.BlockSpec(memory_space=pltpu.VMEM)
    smem = pl.BlockSpec(memory_space=pltpu.SMEM)
    sd = jax.ShapeDtypeStruct
    vm = pltpu.VMEM
    total = len(MIXED) * PARTS
    dma = pltpu.SemaphoreType.DMA
    act = vm((rows, D), BF)
    outs = pl.pallas_call(
        functools.partial(layer_kernel, nz, lens),
        out_shape=[sd((4, D, D), BF)] * 7
        + [sd((total, size, width // nz), F32), sd((32, D), F32), sd((rows, D), BF), sd((rows, D), F32)],
        in_specs=[any_spec] * 6 + [smem] * 3 + [vmem] * 16,
        out_specs=[any_spec] * 7 + [vmem] * 4,
        scratch_shapes=[
            vm((4, D, D), BF),
            vm((4, D, D), BF),
            vm((4, D, D), BF),
            act,
            vm((3, rows, D), BF),
            act,
            vm((2, nh, lw, lv), BF),
            vm((2, nh, lv, lw), BF),
            act,
            vm((rows, 128), F32),
            act,
            vm((3, rows, D), BF),
            act,
            vm((2, nh, lw, lw), BF),
            vm((2, nh, lv, lv), BF),
            act,
            vm((rows, 128), F32),
            vm((rows, D), F32),
            act,
            vm((nz, rows, D), BF),
            vm((nz, rows, D), BF),
            act,
            act,
            vm((D, rows), BF),
            vm((D, rows), BF),
            vm((32, D), F32),
            vm((2, 2, 2, 2, size * PARTS, width), BF),
            vm((SLOTS, 2, 2, size, width), BF),
            vm((SLOTS, 2, size, width // 2), BF),
            vm((SLOTS, 2, size, width // 2), BF),
            vm((SLOTS, size, width // 2), BF),
            vm((SLOTS, size, width // 2), BF),
            vm((SLOTS, nz, size, width // nz), BF),
            vm((SLOTS, nz - 1, size, width // nz), BF),
            vm((4, 32, D), F32),
            vm((3, 32, D), F32),
            vm((nz, 32, D), F32),
            vm((24, D), F32),
            vm((nz, 24, D), F32),
            vm((24, D), F32),
            vm((16, D), F32),
            vm((rows, 128), F32),
            vm((2, lw, lv), F32),
            vm((2, lv, lw), F32),
            vm((2, lw, lw), F32),
            vm((2, lv, lv), F32),
            dma((7, nz - 1, K_Z2 + 1)),
            dma((7, nz - 1, K_Z2 + 1)),
            dma((8, nz + 1)),
            dma((nz,)),
            dma((nz,)),
            dma((SLOTS, 4 + nz)),
            dma((SLOTS, 4 + nz)),
            dma((2 + nz,)),
            dma((2 + nz,)),
        ],
        compiler_params=pltpu.CompilerParams(collective_id=1, has_side_effects=True, vmem_limit_bytes=VMEM_BYTES),
        name="layer",
    )(*shards, *counts, flags, *inputs, *biases, *vectors)
    return outs[7:]


VMEM_BYTES = 62 << 20


def finish_kernel(es, nz, slots, *refs):
    loads = [pltpu.make_async_copy(src, dst, refs[30].at[i]) for i, (src, dst) in enumerate(zip(refs[:4], refs[26:30]))]
    for c in loads:
        c.start()
    sums, small, result, dinput = refs[26:30]
    refs = refs[:26]
    lang, vis, dlang, dvis, gcp, gcb, gco, gcob, gcg, gcs, gsp, gsb, gso, gsob, gsg, gss, gfi, gfib, gfo, gfob, gfg, gfs = refs[4:]
    parts, rows = sums.shape[1], sums.shape[2]
    low = lax.broadcasted_iota(jnp.int32, (8, D), 0) < 4

    def by_slot(src, dst, start, n):
        half = n * GROUP // 2

        def body(i, carry):
            g = [src[pl.ds(pl.multiple_of(start + h * half + 16 * i, 16), 16), :].astype(F32) for h in range(2)]
            for t in range(2):
                one, two = g[0][8 * t : 8 * t + 8], g[1][8 * t : 8 * t + 8]
                dst[4 * i + 2 * t] = jnp.where(low, one, pltpu.roll(two, 4, 0)).astype(dst.dtype)
                dst[4 * i + 2 * t + 1] = jnp.where(low, pltpu.roll(one, 4, 0), two).astype(dst.dtype)
            return carry

        lax.fori_loop(0, n // 4, body, 0)

    loads[2].wait()
    by_slot(result, lang, 0, slots[0])
    by_slot(result, vis, GROUP * slots[0], slots[1])
    loads[3].wait()
    by_slot(dinput, dlang, 0, slots[0])
    by_slot(dinput, dvis, GROUP * slots[0], slots[1])
    loads[0].wait()
    loads[1].wait()
    for s in range(2):
        first = 3 * (1 - s)
        for p in range(parts):
            gfo[s, p * rows : (p + 1) * rows, :] = sums[first, p]
            gfi[s, p * rows : (p + 1) * rows, :] = sums[first + 1, p]
    for i, proj, out in ((5, gsp.at[0], gso.at[0]), (2, gsp.at[1], gso.at[1]), (6, gcp, gco)):
        full = sums[i].reshape(parts * rows, D)
        for c in range(3):
            proj[c] = full[:, c * es : (c + 1) * es]
        out[...] = full[:, 3 * es :].T
    gcb[...] = small[0:2]
    for i, ref in enumerate((gcob, gcg, gcs)):
        ref[...] = small[2 + i : 3 + i].reshape(D)
    for s in range(2):
        gsb[s] = small[5 + 5 * s : 7 + 5 * s]
        for i, ref in enumerate((gsob, gsg, gss)):
            ref[s : s + 1] = small[7 + 5 * s + i : 8 + 5 * s + i]
        for i, ref in enumerate((gfob, gfg, gfs)):
            ref[s : s + 1] = small[15 + 3 * s + i : 16 + 3 * s + i]
        for t in range(nz):
            gfib[s : s + 1, t * D : (t + 1) * D] = small[21 + nz * s + t : 22 + nz * s + t]


def finish(es, nz, slots, sums, small, result, dinput):
    sd = jax.ShapeDtypeStruct
    chunk = D // GROUP
    vmem = pl.BlockSpec(memory_space=pltpu.VMEM)
    two, one = sd((2, D), F32), sd((D,), F32)
    shapes = (
        [sd((n, GROUP, D), dt) for dt in (BF, F32) for n in slots]
        + [sd((3, chunk, es), F32), two, sd((es, chunk), F32), one, one, one]
        + [sd((2, 3, chunk, es), F32), sd((2, 2, D), F32), sd((2, es, chunk), F32), two, two, two]
        + [sd((2, chunk, D), F32), sd((2, nz * D), F32), sd((2, chunk, D), F32), two, two, two]
    )
    return pl.pallas_call(
        functools.partial(finish_kernel, es, nz, slots),
        out_shape=shapes,
        in_specs=[pl.BlockSpec(memory_space=pltpu.HBM)] * 4,
        out_specs=[vmem] * len(shapes),
        scratch_shapes=[pltpu.VMEM(v.shape, v.dtype) for v in (sums, small, result, dinput)] + [pltpu.SemaphoreType.DMA((4,))],
        compiler_params=pltpu.CompilerParams(vmem_limit_bytes=40 << 20),
        name="finish",
    )(sums, small, result, dinput)


def dot(a, b, dims):
    return lax.dot_general(a, b, (dims, ((), ())), preferred_element_type=F32)


def per_device(nz, ndp, *args):
    (
        language,
        visual,
        word_count,
        region_count,
        task_flags,
        grad_language,
        grad_visual,
        cross_project,
        cross_bias,
        cross_out,
        cross_out_bias,
        cross_gain,
        cross_shift,
        self_project,
        self_bias,
        self_out,
        self_out_bias,
        self_gain,
        self_shift,
        feed_in,
        feed_in_bias,
        feed_out,
        feed_out_bias,
        feed_gain,
        feed_shift,
    ) = args
    items = language.shape[0]
    slots = (language.shape[1], visual.shape[1])
    counts_rows = (items * slots[0], items * slots[1])
    z = lax.axis_index("tensor")
    es = cross_project.shape[2]
    fs = feed_in.shape[2]
    lens = tuple(items // 2 * n for n in slots)
    shards = (jnp.swapaxes(cross_project, 1, 2), cross_out, jnp.swapaxes(self_project, 2, 3), self_out, feed_in, feed_out)
    sums, vectors, result, dinput = layer(
        nz,
        lens,
        shards,
        (word_count, region_count),
        task_flags.T,
        tuple(jnp.swapaxes(v, 0, 1) for v in (language, visual, grad_language, grad_visual)),
        (cross_bias, self_bias, feed_in_bias),
        (cross_out_bias, cross_gain, cross_shift, self_out_bias, self_gain, self_shift, feed_out_bias, feed_gain, feed_shift),
    )
    outer = ndp // GROUP
    if outer == 1:
        outs = list(finish(es, nz, slots, sums.reshape((7, PARTS) + sums.shape[1:]), vectors, result, dinput))
        for i in range(4):
            outs[i] = jnp.swapaxes(outs[i], 0, 1)
        outs[18] = jnp.swapaxes(outs[18], 1, 2)
        return tuple(outs)
    sums = sums.reshape(7, -1, sums.shape[2])
    if outer > 1:
        members = [[i * GROUP + j for i in range(outer)] for j in range(GROUP)]
        sums = lax.psum_scatter(sums, "dp", scatter_dimension=1, axis_index_groups=members, tiled=True)
        sums = lax.ppermute(sums, "dp", [(i * GROUP + j, j * outer + i) for i in range(outer) for j in range(GROUP)])
        vectors = lax.psum(vectors, "dp", axis_index_groups=members)
    names = [("out", 1), ("in", 1), ("self", 1), ("out", 0), ("in", 0), ("self", 0), "cross"]
    total = {name: sums[i] for i, name in enumerate(names)}

    def columns(v):
        return jnp.stack([v[:, i * es : (i + 1) * es] for i in range(3)]), v[:, 3 * es :].T

    gcp, gco = columns(total["cross"])
    gs = [columns(total["self", s]) for s in range(2)]
    v = vectors

    def by_item(x, s, shape):
        x = x[s * counts_rows[0] : s * counts_rows[0] + counts_rows[s]]
        return x.reshape(2, shape[1], shape[0] // 2, D).transpose(0, 2, 1, 3).reshape(shape)

    f0 = 21
    nf = nz * fs // D
    return (
        by_item(result, 0, language.shape),
        by_item(result, 1, visual.shape),
        by_item(dinput, 0, language.shape),
        by_item(dinput, 1, visual.shape),
        gcp,
        v[0:2],
        gco,
        v[2],
        v[3],
        v[4],
        jnp.stack([gs[0][0], gs[1][0]]),
        jnp.stack([v[5:7], v[10:12]]),
        jnp.stack([gs[0][1], gs[1][1]]),
        jnp.stack([v[7], v[12]]),
        jnp.stack([v[8], v[13]]),
        jnp.stack([v[9], v[14]]),
        jnp.stack([total["in", 0], total["in", 1]]),
        v[f0 : f0 + 2 * nf].reshape(2, nz * fs),
        jnp.stack([total["out", 0].T, total["out", 1].T]),
        jnp.stack([v[15], v[18]]),
        jnp.stack([v[16], v[19]]),
        jnp.stack([v[17], v[20]]),
    )


def solution(mesh):
    rows = P(("dp", "tensor"), None, None)
    placed = (
        rows,
        rows,
        P("dp"),
        P("dp"),
        P(("dp", "tensor"), None),
        rows,
        rows,
        P(None, None, "tensor"),
        P(None, "tensor"),
        P("tensor", None),
        P(),
        P(),
        P(),
        P(None, None, None, "tensor"),
        P(None, None, "tensor"),
        P(None, "tensor", None),
        P(),
        P(),
        P(),
        P(None, None, "tensor"),
        P(None, "tensor"),
        P(None, "tensor", None),
        P(),
        P(),
        P(),
    )
    return jax.shard_map(
        functools.partial(per_device, mesh.shape["tensor"], mesh.shape["dp"]),
        mesh=mesh,
        in_specs=placed,
        out_specs=(
            rows,
            rows,
            rows,
            rows,
            P(None, "dp", "tensor"),
            P(),
            P("tensor", "dp"),
            P(),
            P(),
            P(),
            P(None, None, "dp", "tensor"),
            P(),
            P(None, "tensor", "dp"),
            P(),
            P(),
            P(),
            P(None, "dp", "tensor"),
            P(),
            P(None, "tensor", "dp"),
            P(),
            P(),
            P(),
        ),
        check_vma=False,
    )
```

```python
import functools

import jax
import jax.numpy as jnp
from jax import lax
from jax.experimental import pallas as pl
from jax.experimental.pallas import tpu as pltpu
from jax.sharding import PartitionSpec as P

D = 768
HEAD_DIM = 64
LAYER_EPS = 1e-06
MASKED = -1e30
GROUP = 8
MESH = pl.DeviceIdType.MESH
BF = jnp.bfloat16
F32 = jnp.float32


def place():
    dp = lax.axis_index("dp")
    z = lax.axis_index("tensor")
    core = dp % 2
    bx = (dp // 2) % 2
    by = (dp // 4) % 2
    return dp, z, core, bx, by


def greet(targets):
    barrier = pltpu.get_barrier_semaphore()
    count = 0
    for device, valid in targets:
        if valid is None:
            pl.semaphore_signal(barrier, inc=1, device_id=device, device_id_type=MESH)
            count = count + 1
        else:

            @pl.when(valid)
            def _(device=device):
                pl.semaphore_signal(barrier, inc=1, device_id=device, device_id_type=MESH)

            count = count + valid.astype(jnp.int32)
    pl.semaphore_wait(barrier, count)


K_Z, K_X, K_Y, K_A, K_B, K_Z2, K_C = 0, 1, 2, 3, 4, 5, 6
TILE = 256


def gather_steps(nz, units, whole, send_sem, recv_sem, core_sem):
    dp, z, core, bx, by = place()
    low = dp % GROUP
    dev_c = (dp + 1 - 2 * core, z)
    dev_x = (dp + 2 - 4 * bx, z)
    dev_y = (dp + 4 - 8 * by, z)
    sl_x = low + 2 - 4 * bx
    sl_y = low + 4 - 8 * by
    sl_d = low + 2 - 4 * bx + 4 - 8 * by

    def copy(src, dst, u, k, kind, device):
        got = core_sem.at[u] if kind >= K_C else recv_sem.at[u, k, kind]
        return pltpu.make_async_remote_copy(
            src_ref=src, dst_ref=dst, send_sem=send_sem.at[u], recv_sem=got, device_id=device, device_id_type=MESH
        )

    def is_attention(u):
        return len(units[u]) == 2

    def part(u, j, sl, half):
        if is_attention(u):
            size = units[u][1].shape[0]
            step = size // GROUP
            rows = pl.ds(pl.multiple_of(j * size + sl * step, 8), step)
            return whole[u].at[:, rows] if half is None else whole[u].at[2 * half : 2 * half + 2, rows]
        step = units[u][0].shape[0] // GROUP
        if half is None:
            return whole[u].at[j, pl.ds(pl.multiple_of(sl * step, 8), step)]
        return whole[u].at[j, pl.ds(pl.multiple_of(sl * step + half * (step // 2), 8), step // 2)]

    def z_copies(u, k, j, device, sending):
        if is_attention(u):
            proj, out = units[u]
            size = out.shape[0]
            step = size // GROUP
            mine = pl.ds(pl.multiple_of(low * step, 8), step)
            to = pl.ds(pl.multiple_of(j * size + low * step, 8), step)
            pairs = ((proj.at[:, mine], whole[u].at[0:3, to]), (out.at[mine], whole[u].at[3, to]))
        else:
            step = units[u][0].shape[0] // GROUP
            pairs = ((units[u][0].at[pl.ds(pl.multiple_of(low * step, 8), step)], part(u, j, low, None)),)
        return [copy(src if sending else dst, dst, u, k - 1, (K_Z, K_Z2)[i], device) for i, (src, dst) in enumerate(pairs)]

    def z_send(u, k):
        for c in z_copies(u, k, z, (dp, (z + k) % nz), True):
            c.start()

    def source(k):
        return (z + nz - k) % nz

    def peer(u, k, kind, sending):
        if kind < K_C:
            sent, got, half, device = {
                K_X: (low, sl_x, None, dev_x),
                K_Y: (low, sl_y, None, dev_y),
                K_A: (sl_x, sl_d, 0, dev_y),
                K_B: (sl_y, sl_d, 1, dev_x),
            }[kind]
        else:
            sent, half = ((low, None), (sl_x, None), (sl_y, None), (sl_d, 0), (sl_d, 1))[kind - K_C]
            device = dev_c
            got = sent + 1 - 2 * core
        block = part(u, source(k), sent if sending else got, half)
        return copy(block, block, u, k - 1, kind, device)

    def stage1(u, k):
        for c in z_copies(u, k, source(k), dev_x, False):
            c.wait_recv()
        for kind in (K_X, K_Y, K_C):
            peer(u, k, kind, True).start()

    def stage2(u, k):
        peer(u, k, K_X, False).wait_recv()
        peer(u, k, K_A, True).start()
        peer(u, k, K_C + 1, True).start()
        peer(u, k, K_Y, False).wait_recv()
        peer(u, k, K_B, True).start()
        peer(u, k, K_C + 2, True).start()

    def stage3(u, k):
        peer(u, k, K_A, False).wait_recv()
        peer(u, k, K_C + 3, True).start()
        peer(u, k, K_B, False).wait_recv()
        peer(u, k, K_C + 4, True).start()

    sequence = [(u, k) for u in range(len(units)) for k in range(1, nz)]

    def step(n):
        if n < len(sequence):
            u, k = sequence[n]
            stage1(u, k)
            if u + 2 < len(units):
                z_send(u + 2, k)
        if 1 <= n < len(sequence) + 1:
            stage2(*sequence[n - 1])
        if 2 <= n < len(sequence) + 2:
            stage3(*sequence[n - 2])

    def arrived(u):
        block = whole[u].at[0 : nz - 1, 0 : D // 2]
        pltpu.make_async_copy(block, block, core_sem.at[u]).wait()

    def sent(u):
        block = whole[u].at[0 : nz - 1]
        pltpu.make_async_copy(block, block, send_sem.at[u]).wait()

    def loads(u, dst, sem):
        if is_attention(u):
            proj, out = units[u]
            size = out.shape[0]
            own = pl.ds(pl.multiple_of(z * size, 8), size)
            pairs = [(proj, dst.at[0:3, own]), (out, dst.at[3, own])]
            for k in range(1, nz):
                rows = pl.ds(pl.multiple_of(source(k) * size, 8), size)
                pairs.append((whole[u].at[:, rows], dst.at[:, rows]))
        else:
            pairs = [(units[u][0], dst.at[z])]
            for k in range(1, nz):
                pairs.append((whole[u].at[source(k)], dst.at[source(k)]))
        return [pltpu.make_async_copy(src, to, sem.at[i]) for i, (src, to) in enumerate(pairs)]

    return z_send, step, arrived, sent, loads


def project(x_ref, xrows, w_ref, w0, bias_ref, b0, out_ref):
    x = x_ref[xrows, :]
    tiles = D // TILE

    def body(i, carry):
        c, t = i // tiles, i % tiles
        at = pl.ds(pl.multiple_of(t * TILE, TILE), TILE)
        y = dot(x, w_ref[w0 + c, at, :], ((1,), (1,)))
        out_ref[c, xrows, at] = (y + bias_ref[pl.ds(b0 + c, 1), at]).astype(BF)
        return carry

    lax.fori_loop(0, 3 * tiles, body, 0)


def half_lanes():
    lane = lax.broadcasted_iota(jnp.int32, (1, 2 * HEAD_DIM), 1)
    return lane < HEAD_DIM


def attend(qkv_ref, ctx_ref, p_ref, mask_ref, q0, lq, k0, lk):
    first = half_lanes()
    keep = [jnp.where(first, HEAD_DIM**-0.5, 0.0).astype(BF), jnp.where(first, 0.0, HEAD_DIM**-0.5).astype(BF)]

    def body(pair, carry):
        lanes = pl.ds(pl.multiple_of(pair * 2 * HEAD_DIM, 2 * HEAD_DIM), 2 * HEAD_DIM)
        for g in range(2):
            qr, kr = pl.ds(q0 + g * lq, lq), pl.ds(k0 + g * lk, lk)
            q, k, v = qkv_ref[0, qr, lanes], qkv_ref[1, kr, lanes], qkv_ref[2, kr, lanes]
            parts = []
            for h in range(2):
                s = dot(q * keep[h], k, ((1,), (1,))) + mask_ref[g]
                w = jnp.exp(s - jnp.max(s, axis=1, keepdims=True))
                pb = (w * (1.0 / jnp.sum(w, axis=1, keepdims=True))).astype(BF)
                p_ref[g, 2 * pair + h] = pb
                parts.append(dot(pb, v, ((1,), (0,))))
            ctx_ref[qr, lanes] = jnp.where(first, parts[0], parts[1]).astype(BF)
        return carry

    lax.fori_loop(0, D // (2 * HEAD_DIM), body, 0, unroll=2)


def out_norm(ctx_ref, start, count, w_ref, wi, resid_ref, vec_ref, v0, pre_ref, hat_ref, rstd_ref, full_ref, low_ref):
    rows = pl.ds(start, count)
    ctx = ctx_ref[rows, :]

    def tile(t, carry):
        at = pl.ds(pl.multiple_of(t * TILE, TILE), TILE)
        y = dot(ctx, w_ref[wi, :, at], ((1,), (0,)))
        pre_ref[rows, at] = y + resid_ref[rows, at].astype(F32) + vec_ref[pl.ds(v0, 1), at]
        return carry

    lax.fori_loop(0, D // TILE, tile, 0)
    gain, shift = vec_ref[v0 + 1 : v0 + 2, :], vec_ref[v0 + 2 : v0 + 3, :]

    def norm(i, carry):
        r = pl.ds(pl.multiple_of(start + i * 32, 16), 32)
        x = pre_ref[r, :]
        center = x - jnp.sum(x, axis=1, keepdims=True) * (1.0 / D)
        rstd = lax.rsqrt(jnp.sum(center * center, axis=1, keepdims=True) * (1.0 / D) + LAYER_EPS)
        hat = center * rstd
        y = hat * gain + shift
        hat_ref[r, :] = hat.astype(BF)
        rstd_ref[r, :] = jnp.broadcast_to(rstd, (32, 128))
        full_ref[r, :] = y
        low_ref[r, :] = y.astype(BF)
        return carry

    lax.fori_loop(0, count // 32, norm, 0)


def by_group(src_ref, dst_ref, start, slots):
    half = slots * GROUP // 2
    low = lax.broadcasted_iota(jnp.int32, (8, D), 0) < 4

    def body(i, carry):
        a = [src_ref[4 * i + t].astype(F32) for t in range(4)]
        for g in range(2):
            rows = []
            for t in (0, 2):
                one, two = (a[t], pltpu.roll(a[t + 1], 4, 0)) if g == 0 else (pltpu.roll(a[t], 4, 0), a[t + 1])
                rows.append(jnp.where(low, one, two))
            at = pl.ds(pl.multiple_of(start + g * half + 16 * i, 16), 16)
            dst_ref[at, :] = jnp.concatenate(rows, axis=0).astype(dst_ref.dtype)
        return carry

    lax.fori_loop(0, slots // 4, body, 0)


def fill_masks(mask_refs, counts, first):
    for n, (ref, count) in enumerate(zip(mask_refs, counts)):
        for g in range(2):
            shape = ref.shape[1:]
            row, col = (lax.broadcasted_iota(jnp.int32, shape, d) for d in range(2))
            item = jnp.bitwise_and(col, 3)
            limit = jnp.zeros(shape, jnp.int32)
            for j in range(4):
                limit = jnp.where(item == j, count[first + 4 * g + j], limit)
            seen = jnp.logical_and(jnp.bitwise_and(row, 3) == item, jnp.right_shift(col, 2) < limit)
            ref[g] = jnp.where(seen, 0.0, MASKED).astype(F32)


SLOTS = 4
CORE_SLOTS = 7
PARTS = 3


def scatter_steps(nz, mixed, slot_bufs, send_sem, recv_sem, rs_out):
    grad, crecv, xa, yb, ya, xb, zbuf, zrecv = slot_bufs
    dp, z, core, bx, by = place()
    dev_c = (dp + 1 - 2 * core, z)
    dev_x = (dp + 2 - 4 * bx, z)
    dev_y = (dp + 4 - 8 * by, z)
    rows, width = crecv.shape[3], crecv.shape[4]
    half = width // 2
    lo, hi = pl.ds(0, half), pl.ds(half, half)
    zw = width // nz
    S_C, S_XA, S_YB, S_YA, S_XB, S_Z = 0, 1, 2, 3, 4, 5

    def part(i, c):
        return grad.at[:, :, c, pl.ds((i % PARTS) * rows, rows)]

    def remote(src, dst, s, k, device):
        return pltpu.make_async_remote_copy(
            src_ref=src, dst_ref=dst, send_sem=send_sem.at[s, k], recv_sem=recv_sem.at[s, k], device_id=device, device_id_type=MESH
        )

    def core_copy(i):
        return remote(part(i, 1 - core), crecv.at[i % CORE_SLOTS], i % CORE_SLOTS, S_C, dev_c)

    def xa_copy(i):
        s = i % SLOTS
        return remote(crecv.at[i % CORE_SLOTS, :, 1 - bx, :, lo], xa.at[s], s, S_XA, dev_x)

    def yb_copy(i):
        s = i % SLOTS
        return remote(crecv.at[i % CORE_SLOTS, 1 - by, :, :, hi], yb.at[s], s, S_YB, dev_y)

    def ya_copy(i):
        s = i % SLOTS
        return remote(crecv.at[i % CORE_SLOTS, 1 - by, bx, :, lo], ya.at[s], s, S_YA, dev_y)

    def xb_copy(i):
        s = i % SLOTS
        return remote(crecv.at[i % CORE_SLOTS, by, 1 - bx, :, hi], xb.at[s], s, S_XB, dev_x)

    def z_copy(s, k):
        return remote(zbuf.at[s, (z + k) % nz], zrecv.at[s, k - 1], s, S_Z + k - 1, (dp, (z + k) % nz))

    def merge(dst, src):
        for r in range(0, rows, 16):
            at = pl.ds(r, 16)
            dst[at] = dst[at] + src[at]

    def stage_a(i):
        core_copy(i).wait()
        mine = part(i, core)

        def body(j, carry):
            merge(crecv.at[i % CORE_SLOTS, j // 2, j % 2], mine.at[j // 2, j % 2])
            return carry

        lax.fori_loop(0, 4, body, 0)
        xa_copy(i).start()
        yb_copy(i).start()

    def stage_b(i):
        s = i % SLOTS
        xa_copy(i).wait()
        yb_copy(i).wait()

        def body(j, carry):
            merge(crecv.at[i % CORE_SLOTS, j, bx, :, lo], xa.at[s, j])
            merge(crecv.at[i % CORE_SLOTS, by, j, :, hi], yb.at[s, j])
            return carry

        lax.fori_loop(0, 2, body, 0)
        ya_copy(i).start()
        xb_copy(i).start()

    def stage_c(i):
        s = i % SLOTS
        ya_copy(i).wait()
        xb_copy(i).wait()
        own = crecv.at[i % CORE_SLOTS, by, bx]
        for r in range(0, rows, 16):
            at = pl.ds(r, 16)
            left = own[at, lo] + ya[s, at, :]
            right = own[at, hi] + xb[s, at, :]
            full = jnp.concatenate([left, right], axis=1)
            for t in range(nz):
                if mixed[i // PARTS]:
                    sub = zw // 4
                    row = [full[:, m * (width // 4) + t * sub : m * (width // 4) + (t + 1) * sub] for m in range(4)]
                    zbuf[s, t, at, :] = jnp.concatenate(row, axis=1)
                else:
                    zbuf[s, t, at, :] = full[:, t * zw : (t + 1) * zw]
        for k in range(1, nz):
            z_copy(s, k).start()

    def stage_d(i):
        s = i % SLOTS
        for k in range(1, nz):
            z_copy(s, k).wait()
        for r in range(0, rows, 16):
            at = pl.ds(r, 16)
            total = zbuf[s, z, at, :].astype(F32)
            for k in range(nz - 1):
                total = total + zrecv[s, k, at, :].astype(F32)
            rs_out[i, at, :] = total

    return core_copy, stage_a, stage_b, stage_c, stage_d


def small_steps(nz, small, sbuf, srecv, szrecv, small_out, send_sem, recv_sem):
    dp, z, core, bx, by = place()
    devs = ((dp + 1 - 2 * core, z), (dp + 2 - 4 * bx, z), (dp + 4 - 8 * by, z))

    def remote(src, dst, k, device):
        return pltpu.make_async_remote_copy(
            src_ref=src, dst_ref=dst, send_sem=send_sem.at[k], recv_sem=recv_sem.at[k], device_id=device, device_id_type=MESH
        )

    def pair(k):
        return remote(sbuf.at[k], srecv.at[k], k, devs[k])

    def along_z(k, sending):
        return remote(sbuf.at[3], szrecv.at[z if sending else (z + nz - k) % nz], 2 + k, (dp, (z + k) % nz))

    def stage(k):
        if k == 0:
            sbuf[0] = small[...]
            pair(0).start()
        elif k < 4:
            pair(k - 1).wait()
            sbuf[k] = sbuf[k - 1] + srecv[k - 1]
            if k < 3:
                pair(k).start()
            else:
                szrecv[z] = sbuf[3]
                for i in range(1, nz):
                    along_z(i, True).start()
        else:
            for i in range(1, nz):
                along_z(i, True).wait_send()
                along_z(i, False).wait_recv()
            total = szrecv[0]
            for i in range(1, nz):
                total = total + szrecv[i]
            small_out[...] = total

    return stage


def eighth(x):
    return jnp.sum(x.reshape(x.shape[0] // 8, 8, x.shape[1]), axis=0)


def transpose_into(t_ref, x_ref, start, count):
    for i in range(D // 128):
        t_ref[i * 128 : (i + 1) * 128, 0:count] = x_ref[pl.ds(start, count), i * 128 : (i + 1) * 128].T


def feed_forward(nb_ref, rows, w_ref, bias_ref, b0, h_ref, slope_ref, first, last):
    x = nb_ref[rows, :]
    tiles = D // TILE

    def body(i, carry):
        zb, t = i // tiles, i % tiles
        at = pl.ds(pl.multiple_of(t * TILE, TILE), TILE)
        u = dot(x, w_ref[zb, :, at], ((1,), (0,))) + bias_ref[pl.ds(b0 + zb, 1), at]
        phi = 0.5 + 0.5 * lax.erf(u * 0.5**0.5)
        h_ref[zb, rows, at] = (u * phi).astype(BF)
        slope_ref[zb, rows, at] = (phi + u * (jnp.exp(-0.5 * u * u) * 0.3989422804014327)).astype(BF)
        return carry

    lax.fori_loop(first * tiles, last * tiles, body, 0)


def feed_out_rows(h_ref, rows, w_ref, nn_ref, vec_ref, v0, res_ref):
    def body(t, carry):
        at = pl.ds(pl.multiple_of(t * TILE, TILE), TILE)
        y = nn_ref[rows, at] + vec_ref[pl.ds(v0, 1), at]
        for zb in range(h_ref.shape[0]):
            y = y + dot(h_ref[zb, rows, :], w_ref[zb, :, at], ((1,), (0,)))
        res_ref[rows, at] = y
        return carry

    lax.fori_loop(0, D // TILE, body, 0)


def norm_grad(hat, rstd, gain, g, acc):
    scaled = g * gain
    dz = rstd * (
        scaled - jnp.sum(scaled, axis=1, keepdims=True) * (1.0 / D) - hat * (jnp.sum(scaled * hat, axis=1, keepdims=True) * (1.0 / D))
    )
    return dz, (acc[0] + eighth(dz), acc[1] + eighth(g * hat), acc[2] + eighth(g))


def no_sums():
    return tuple(jnp.zeros((8, D), F32) for _ in range(3))


def keep_sums(acc, small, row):
    for i in range(3):
        small[row + i : row + i + 1, :] = jnp.sum(acc[i], axis=0, keepdims=True)


def last_norm(start, count, res_ref, vec_ref, v0, cot_ref, weight_ref, result_ref, db_ref, small, row):
    gain, shift = vec_ref[v0 + 1 : v0 + 2, :], vec_ref[v0 + 2 : v0 + 3, :]

    def body(i, acc):
        r = pl.ds(pl.multiple_of(start + i * 32, 16), 32)
        x = res_ref[r, :]
        center = x - jnp.sum(x, axis=1, keepdims=True) * (1.0 / D)
        rstd = lax.rsqrt(jnp.sum(center * center, axis=1, keepdims=True) * (1.0 / D) + LAYER_EPS)
        hat = center * rstd
        result_ref[r, :] = (hat * gain + shift).astype(BF)
        g = cot_ref[r, :].astype(F32) * weight_ref[r, 0:1]
        dz, acc = norm_grad(hat, rstd, gain, g, acc)
        res_ref[r, :] = dz
        db_ref[r, :] = dz.astype(BF)
        return acc

    keep_sums(lax.fori_loop(0, count // 32, body, no_sums()), small, row)


def norm_back(start, count, res_ref, hat_ref, rstd_ref, vec_ref, gain_row, db_ref, small, row):
    gain = vec_ref[gain_row : gain_row + 1, :]

    def body(i, acc):
        r = pl.ds(pl.multiple_of(start + i * 32, 16), 32)
        dz, acc = norm_grad(hat_ref[r, :].astype(F32), rstd_ref[r, 0:1], gain, res_ref[r, :], acc)
        res_ref[r, :] = dz
        db_ref[r, :] = dz.astype(BF)
        return acc

    keep_sums(lax.fori_loop(0, count // 32, body, no_sums()), small, row)


def hidden_grad(db_ref, rows, w_ref, slope_ref, small, row):
    db = db_ref[rows, :]
    tiles = D // TILE

    def body(i, carry):
        zb, t = i // tiles, i % tiles
        at = pl.ds(pl.multiple_of(t * TILE, TILE), TILE)
        du = (dot(db, w_ref[zb, at, :], ((1,), (1,))) * slope_ref[zb, rows, at].astype(F32)).astype(BF)
        slope_ref[zb, rows, at] = du
        small[pl.ds(row + zb, 1), at] = jnp.sum(eighth(du.astype(F32)), axis=0, keepdims=True)
        return carry

    lax.fori_loop(0, slope_ref.shape[0] * tiles, body, 0)


def add_products(res_ref, out_ref, rows, x_ref, count, w_ref, transposed):
    def body(t, carry):
        at = pl.ds(pl.multiple_of(t * TILE, TILE), TILE)
        y = res_ref[rows, at]
        for c in range(count):
            if transposed:
                y = y + dot(x_ref[c, rows, :], w_ref[c, at, :], ((1,), (1,)))
            else:
                y = y + dot(x_ref[c, rows, :], w_ref[c, :, at], ((1,), (0,)))
        out_ref[rows, at] = y
        return carry

    lax.fori_loop(0, D // TILE, body, 0)


def context_grad(db_ref, rows, w_ref, dctx_ref):
    db = db_ref[rows, :]

    def body(t, carry):
        at = pl.ds(pl.multiple_of(t * TILE, TILE), TILE)
        dctx_ref[rows, at] = dot(db, w_ref[3, at, :], ((1,), (1,))).astype(BF)
        return carry

    lax.fori_loop(0, D // TILE, body, 0)


def attend_back(qkv_ref, dctx_ref, p_ref, out_ref, q0, lq, k0, lk, first_pair=0, last_pair=D // (2 * HEAD_DIM)):
    first = half_lanes()
    keep = [jnp.where(first, 1.0, 0.0).astype(BF), jnp.where(first, 0.0, 1.0).astype(BF)]

    def body(pair, carry):
        lanes = pl.ds(pl.multiple_of(pair * 2 * HEAD_DIM, 2 * HEAD_DIM), 2 * HEAD_DIM)
        for g in range(2):
            qr, kr = pl.ds(q0 + g * lq, lq), pl.ds(k0 + g * lk, lk)
            q, k, v, dc = qkv_ref[0, qr, lanes], qkv_ref[1, kr, lanes], qkv_ref[2, kr, lanes], dctx_ref[qr, lanes]
            dq, dk, dv = [], [], []
            for h in range(2):
                pb = p_ref[g, 2 * pair + h]
                p = pb.astype(F32)
                dp = dot(dc * keep[h], v, ((1,), (1,)))
                ds = (p * (dp - jnp.sum(p * dp, axis=1, keepdims=True))).astype(BF)
                dq.append(dot(ds, k, ((1,), (0,))))
                dk.append(dot(ds, q, ((0,), (0,))))
                dv.append(dot(pb, dc, ((0,), (0,))))
            out_ref[0, qr, lanes] = (jnp.where(first, dq[0], dq[1]) * HEAD_DIM**-0.5).astype(BF)
            out_ref[1, kr, lanes] = (jnp.where(first, dk[0], dk[1]) * HEAD_DIM**-0.5).astype(BF)
            out_ref[2, kr, lanes] = jnp.where(first, dv[0], dv[1]).astype(BF)
        return carry

    lax.fori_loop(first_pair, last_pair, body, 0)


def bias_sums(x_ref, rows, count, small, row_q, row_v, add):
    ones = jnp.ones((8, count), BF)
    for c, row in ((0, row_q), (2, row_v)):
        total = dot(ones, x_ref[c, rows, :], ((1,), (0,)))[0:1, :]
        small[row : row + 1, :] = total


def grad_tiles(grad_ref, m, t_ref, count, x_ref, rows, first, last, lane0, mats):
    size = grad_ref.shape[3]
    left = t_ref[:, 0:count]
    tiles = D // TILE

    def body(i, carry):
        b, t = i // tiles, i % tiles
        at = pl.ds(pl.multiple_of(t * TILE, TILE), TILE)
        right = x_ref[b, rows, at] if mats else x_ref[rows, at]
        y = dot(left, right, ((1,), (0,))).astype(BF)
        lanes = pl.ds(pl.multiple_of(lane0 + i * TILE, TILE), TILE)
        grad_ref[:, :, :, :, lanes] = y.reshape(2, 2, 2, size, TILE)
        return carry

    lax.fori_loop(first * tiles, last * tiles, body, 0)


CROSS, SELF1, IN1, OUT1, SELF0, IN0, OUT0 = range(7)
MIXED = (False, False, True, False, False, True, True)


def layer_kernel(nz, lens, *refs):
    cp, co, sp, so, fi, fo, word_count, region_count, flags = refs[:9]
    lang, vis, cot_lang, cot_vis, cross_b, self_b, feed_b = refs[9:16]
    cob, cg, cs, sob, sg, ss, fob, fg, fs = refs[16:25]
    whole = refs[25:32]
    rs_out, small_out, result, res = refs[32:36]
    wb3 = refs[36]
    refs = refs[1:]
    wb0, wb1, wb2, x, qkv_c, ctx_c, p_c0, p_c1, hat1, rstd1, mb = refs[36:47]
    qkv_s, ctx_s, p_s0, p_s1, hat2, rstd2, mid, nb, hid, slope, db, dctx, t1, t2, small = refs[47:62]
    grad, crecv, xa, yb, ya, xb, zbuf, zrecv, sbuf, srecv, szrecv = refs[62:73]
    bias_src, bias_all, bias_ref, vec, weight = refs[73:78]
    masks = refs[78:82]
    send_sem, recv_sem, core_sem, w_sem, bias_send, bias_recv, rs_send, rs_recv, small_send, small_recv = refs[82:]
    dp, z, core, bx, by = place()
    lw, lv = lens
    rw, rv = 2 * lw, 2 * lv
    start, count = (0, rw), (rw, rv)
    rows = (pl.ds(0, rw), pl.ds(rw, rv))
    every = pl.ds(0, rw + rv)

    bias_src[...] = jnp.zeros_like(bias_src)
    part = cross_b.shape[1]
    for t in range(nz):

        @pl.when(z == t)
        def _(t=t):
            lanes = slice(t * part, (t + 1) * part)
            for i in range(2):
                bias_src[2 * i : 2 * i + 1, lanes] = cross_b[i : i + 1, :]
                for s in range(2):
                    bias_src[3 + 3 * s + 2 * i : 4 + 3 * s + 2 * i, lanes] = self_b[s, i : i + 1, :]
            for s in range(2):
                bias_src[9 + nz * s + t : 10 + nz * s + t, :] = feed_b[s : s + 1, :]

    targets = [((dp + 1 - 2 * core, z), None), ((dp + 2 - 4 * bx, z), None), ((dp + 4 - 8 * by, z), None)]
    for k in range(1, nz):
        targets.append(((dp, (z + k) % nz), None))
    greet(targets)
    units = (
        (cp, co),
        (sp.at[1], so.at[1]),
        (fi.at[1],),
        (fo.at[1],),
        (sp.at[0], so.at[0]),
        (fi.at[0],),
        (fo.at[0],),
    )
    z_send, gather, arrived, sent, loads = gather_steps(nz, units, whole, send_sem, recv_sem, core_sem)
    slot_bufs = (grad, crecv, xa, yb, ya, xb, zbuf, zrecv)
    core_copy, stage_a, stage_b, stage_c, stage_d = scatter_steps(nz, MIXED, slot_bufs, rs_send, rs_recv, rs_out)
    small_stage = small_steps(nz, small, sbuf, srecv, szrecv, small_out, small_send, small_recv)
    pieces = len(MIXED) * PARTS

    def scatter(n):
        if n + 1 < pieces and (n + 1) % PARTS:
            core_copy(n + 1).start()
        if n < pieces:
            stage_a(n)
        if 1 <= n < pieces + 1:
            stage_b(n - 1)
        if 2 <= n < pieces + 2:
            stage_c(n - 2)
        if 3 <= n < pieces + 3:
            stage_d(n - 3)

    def bias_copy(k, sending):
        return pltpu.make_async_remote_copy(
            src_ref=bias_src,
            dst_ref=bias_all.at[z if sending else (z + nz - k) % nz],
            send_sem=bias_send.at[k],
            recv_sem=bias_recv.at[k],
            device_id=(dp, (z + k) % nz),
            device_id_type=MESH,
        )

    def fetch(u, dst):
        arrived(u)
        for c in loads(u, dst, w_sem.at[u]):
            c.start()

    def ready(u, dst):
        for c in loads(u, dst, w_sem.at[u]):
            c.wait()

    cot = dctx

    def prepare():
        for i, ref in enumerate((cob, cg, cs)):
            vec[i : i + 1, :] = ref[...].reshape(1, D)
        for s in range(2):
            for i, ref in enumerate((sob, sg, ss)):
                vec[3 + 3 * s + i : 4 + 3 * s + i, :] = ref[s : s + 1, :]
            for i, ref in enumerate((fob, fg, fs)):
                vec[9 + 3 * s + i : 10 + 3 * s + i, :] = ref[s : s + 1, :]
        by_group(lang, x, 0, lang.shape[0])
        by_group(vis, x, rw, vis.shape[0])
        by_group(cot_lang, cot, 0, cot_lang.shape[0])
        by_group(cot_vis, cot, rw, cot_vis.shape[0])
        fill_masks(masks, (region_count, word_count, word_count, region_count), z * GROUP)
        for s in range(2):
            for g in range(2):
                row = lax.broadcasted_iota(jnp.int32, (lens[s], 128), 0)
                item = jnp.bitwise_and(row, 3)
                value = jnp.zeros((lens[s], 128), F32)
                for j in range(4):
                    n = 4 * g + j
                    other = flags[0, n].astype(F32)
                    if s == 0:
                        answer = jnp.maximum(flags[1, n], flags[2, n]).astype(F32)
                        value = jnp.where(item == j, jnp.where(row < 4, answer, other), value)
                    else:
                        value = jnp.where(item == j, other, value)
                weight[start[s] + g * lens[s] : start[s] + (g + 1) * lens[s], :] = value

    def bias_sum():
        for k in range(1, nz):
            bias_copy(k, False).wait_recv()
        bias_all[z] = bias_src[...]
        total = bias_all[0]
        for k in range(1, nz):
            total = total + bias_all[k]
        bias_ref[...] = total

    w_self, w_in, w_out = (wb3, wb1), (wb2, wb2), (wb1, wb3)
    u_self, u_in, u_out = (SELF0, SELF1), (IN0, IN1), (OUT0, OUT1)

    def cross_project_all():
        ready(CROSS, wb0)
        bias_sum()
        project(x, every, wb0, 0, bias_ref, 0, qkv_c)

    def cross_forward(s):
        if s == 0:
            attend(qkv_c, ctx_c, p_c0, masks[0], 0, lw, rw, lv)
        else:
            attend(qkv_c, ctx_c, p_c1, masks[1], rw, lv, 0, lw)

    def cross_norm(s):
        out_norm(ctx_c, start[s], count[s], wb0, 3, x, vec, 0, res, hat1, rstd1, mid, mb)

    def self_project(s):
        ready(u_self[s], w_self[s])
        project(mb, rows[s], w_self[s], 0, bias_ref, 3 + 3 * s, qkv_s)

    def self_forward(s):
        attend(qkv_s, ctx_s, (p_s0, p_s1)[s], masks[2 + s], start[s], lens[s], start[s], lens[s])

    def self_norm(s):
        out_norm(ctx_s, start[s], count[s], w_self[s], 3, mid, vec, 3 + 3 * s, res, hat2, rstd2, mid, nb)

    def forward(s, first, last):
        if first == 0:
            ready(u_in[s], w_in[s])
        feed_forward(nb, rows[s], w_in[s], bias_ref, 9 + nz * s, hid, slope, first, last)

    def out_rows(s):
        ready(u_out[s], w_out[s])
        feed_out_rows(hid, rows[s], w_out[s], mid, vec, 9 + 3 * s, res)

    def norm3(s):
        last_norm(start[s], count[s], res, vec, 9 + 3 * s, cot, weight, result, db, small, 15 + 3 * s)

    def du(s):
        hidden_grad(db, rows[s], w_out[s], slope, small, 21 + nz * s)

    def dn(s):
        add_products(res, res, rows[s], slope, nz, w_in[s], True)

    def self_in(s):
        norm_back(start[s], count[s], res, hat2, rstd2, vec, 4 + 3 * s, db, small, 7 + 5 * s)
        context_grad(db, rows[s], w_self[s], dctx)

    def self_back(s, first, last):
        attend_back(qkv_s, dctx, (p_s0, p_s1)[s], hid, start[s], lens[s], start[s], lens[s], first, last)

    def self_sums(s):
        bias_sums(hid, rows[s], count[s], small, 5 + 5 * s, 6 + 5 * s, False)

    def dm(s):
        add_products(res, res, rows[s], hid, 3, w_self[s], False)

    def cross_in():
        norm_back(0, rw + rv, res, hat1, rstd1, vec, 1, nb, small, 2)
        context_grad(nb, every, wb0, dctx)

    def cross_back(s, first, last):
        attend_back(qkv_c, dctx, (p_c0, p_c1)[s], slope, start[s], lens[s], start[1 - s], lens[1 - s], first, last)

    def cross_sums():
        bias_sums(slope, every, rw + rv, small, 0, 1, False)
        small_stage(0)

    def finish_rows():
        add_products(res, res, every, slope, 3, wb0, False)

    def grads(m):
        if m < 6:
            s = 1 - m // 3
            if m % 3 < 2:
                turned, src, right = ((t1, db, hid), (t2, nb, slope))[m % 3]
                transpose_into(turned, src, start[s], count[s])
                grad_tiles(grad, m, turned, count[s], right, rows[s], 0, nz, 0, True)
                core_copy(m * PARTS).start()
                return
            src, at, n, back, ctx, dqkv, dz = mb, start[s], count[s], rows[s], ctx_s, hid, db
        else:
            src, at, n, back, ctx, dqkv, dz = x, 0, rw + rv, every, ctx_c, slope, nb
        transpose_into(t1, dz, at, n)
        transpose_into(t2, src, at, n)
        grad_tiles(grad, m, t2, n, dqkv, back, 0, 3, 0, True)
        grad_tiles(grad, m, t1, n, ctx, back, 0, 1, 3 * D, False)
        core_copy(m * PARTS).start()

    for k in range(1, nz):
        z_send(0, k)
    for k in range(1, nz):
        bias_copy(k, True).start()
    for k in range(1, nz):
        z_send(1, k)
    prepare()
    for n in range(5):
        gather(n)
    fetch(CROSS, wb0)
    gather(5)
    cross_project_all()
    gather(6)
    cross_forward(1)
    gather(7)
    fetch(SELF1, wb1)
    cross_norm(1)
    gather(8)
    self_project(1)
    gather(9)
    self_forward(1)
    gather(10)
    fetch(IN1, wb2)
    self_norm(1)
    gather(11)
    forward(1, 0, 2)
    gather(12)
    forward(1, 2, nz)
    gather(13)
    fetch(OUT1, wb3)
    gather(14)
    out_rows(1)
    norm3(1)
    grads(0)
    gather(15)
    du(1)
    scatter(0)
    gather(16)
    fetch(SELF0, wb3)
    dn(1)
    scatter(1)
    gather(17)
    self_in(1)
    scatter(2)
    grads(1)
    gather(18)
    self_back(1, 0, 3)
    scatter(3)
    gather(19)
    fetch(IN0, wb2)
    self_back(1, 3, 6)
    scatter(4)
    gather(20)
    dm(1)
    self_sums(1)
    scatter(5)
    grads(2)
    gather(21)
    cross_forward(0)
    scatter(6)
    gather(22)
    fetch(OUT0, wb1)
    cross_norm(0)
    self_project(0)
    self_forward(0)
    scatter(7)
    self_norm(0)
    forward(0, 0, nz)
    out_rows(0)
    norm3(0)
    scatter(8)
    grads(3)
    du(0)
    scatter(9)
    dn(0)
    self_in(0)
    scatter(10)
    self_back(0, 0, 6)
    scatter(11)
    grads(4)
    dm(0)
    cross_in()
    scatter(12)
    cross_back(0, 0, 3)
    scatter(13)
    cross_back(0, 3, 6)
    scatter(14)
    self_sums(0)
    grads(5)
    cross_back(1, 0, 3)
    scatter(15)
    cross_back(1, 3, 6)
    scatter(16)
    cross_sums()
    scatter(17)
    grads(6)
    scatter(18)
    small_stage(1)
    scatter(19)
    small_stage(2)
    finish_rows()
    scatter(20)
    small_stage(3)
    scatter(21)
    small_stage(4)
    scatter(22)
    scatter(23)
    for u in range(len(units)):
        sent(u)
    for k in range(1, nz):
        bias_copy(k, True).wait_send()


def layer(nz, lens, shards, counts, flags, inputs, biases, vectors):
    rows = 2 * sum(lens)
    lw, lv = lens
    nh = D // HEAD_DIM
    size = D // GROUP // PARTS
    width = 4 * D
    any_spec = pl.BlockSpec(memory_space=pl.ANY)
    vmem = pl.BlockSpec(memory_space=pltpu.VMEM)
    smem = pl.BlockSpec(memory_space=pltpu.SMEM)
    sd = jax.ShapeDtypeStruct
    vm = pltpu.VMEM
    total = len(MIXED) * PARTS
    dma = pltpu.SemaphoreType.DMA
    act = vm((rows, D), BF)
    outs = pl.pallas_call(
        functools.partial(layer_kernel, nz, lens),
        out_shape=[sd((4, D, D), BF)] * 7
        + [sd((total, size, width // nz), F32), sd((32, D), F32), sd((rows, D), BF), sd((rows, D), F32)],
        in_specs=[any_spec] * 6 + [smem] * 3 + [vmem] * 16,
        out_specs=[any_spec] * 7 + [vmem] * 4,
        scratch_shapes=[
            vm((4, D, D), BF),
            vm((4, D, D), BF),
            vm((4, D, D), BF),
            vm((4, D, D), BF),
            act,
            vm((3, rows, D), BF),
            act,
            vm((2, nh, lw, lv), BF),
            vm((2, nh, lv, lw), BF),
            act,
            vm((rows, 128), F32),
            act,
            vm((3, rows, D), BF),
            act,
            vm((2, nh, lw, lw), BF),
            vm((2, nh, lv, lv), BF),
            act,
            vm((rows, 128), F32),
            vm((rows, D), F32),
            act,
            vm((nz, rows, D), BF),
            vm((nz, rows, D), BF),
            act,
            act,
            vm((D, rows), BF),
            vm((D, rows), BF),
            vm((32, D), F32),
            vm((2, 2, 2, size * PARTS, width), BF),
            vm((CORE_SLOTS, 2, 2, size, width), BF),
            vm((SLOTS, 2, size, width // 2), BF),
            vm((SLOTS, 2, size, width // 2), BF),
            vm((SLOTS, size, width // 2), BF),
            vm((SLOTS, size, width // 2), BF),
            vm((SLOTS, nz, size, width // nz), BF),
            vm((SLOTS, nz - 1, size, width // nz), BF),
            vm((4, 32, D), F32),
            vm((3, 32, D), F32),
            vm((nz, 32, D), F32),
            vm((24, D), F32),
            vm((nz, 24, D), F32),
            vm((24, D), F32),
            vm((16, D), F32),
            vm((rows, 128), F32),
            vm((2, lw, lv), F32),
            vm((2, lv, lw), F32),
            vm((2, lw, lw), F32),
            vm((2, lv, lv), F32),
            dma((7,)),
            dma((7, nz - 1, K_C)),
            dma((7,)),
            dma((7, nz + 1)),
            dma((nz,)),
            dma((nz,)),
            dma((CORE_SLOTS, 4 + nz)),
            dma((CORE_SLOTS, 4 + nz)),
            dma((2 + nz,)),
            dma((2 + nz,)),
        ],
        compiler_params=pltpu.CompilerParams(collective_id=1, has_side_effects=True, vmem_limit_bytes=VMEM_BYTES),
        name="layer",
    )(*shards, *counts, flags, *inputs, *biases, *vectors)
    return outs[7:]


VMEM_BYTES = 63 << 20


def finish_kernel(es, nz, slots, *refs):
    loads = [pltpu.make_async_copy(src, dst, refs[30].at[i]) for i, (src, dst) in enumerate(zip(refs[:4], refs[26:30]))]
    for c in loads:
        c.start()
    sums, small, result, dinput = refs[26:30]
    refs = refs[:26]
    lang, vis, dlang, dvis, gcp, gcb, gco, gcob, gcg, gcs, gsp, gsb, gso, gsob, gsg, gss, gfi, gfib, gfo, gfob, gfg, gfs = refs[4:]
    parts, rows = sums.shape[1], sums.shape[2]
    low = lax.broadcasted_iota(jnp.int32, (8, D), 0) < 4

    def by_slot(src, dst, start, n):
        half = n * GROUP // 2

        def body(i, carry):
            g = [src[pl.ds(pl.multiple_of(start + h * half + 16 * i, 16), 16), :].astype(F32) for h in range(2)]
            for t in range(2):
                one, two = g[0][8 * t : 8 * t + 8], g[1][8 * t : 8 * t + 8]
                dst[4 * i + 2 * t] = jnp.where(low, one, pltpu.roll(two, 4, 0)).astype(dst.dtype)
                dst[4 * i + 2 * t + 1] = jnp.where(low, pltpu.roll(one, 4, 0), two).astype(dst.dtype)
            return carry

        lax.fori_loop(0, n // 4, body, 0)

    loads[2].wait()
    by_slot(result, lang, 0, slots[0])
    by_slot(result, vis, GROUP * slots[0], slots[1])
    loads[3].wait()
    by_slot(dinput, dlang, 0, slots[0])
    by_slot(dinput, dvis, GROUP * slots[0], slots[1])
    loads[0].wait()
    loads[1].wait()
    for s in range(2):
        first = 3 * (1 - s)
        for p in range(parts):
            gfo[s, p * rows : (p + 1) * rows, :] = sums[first, p]
            gfi[s, p * rows : (p + 1) * rows, :] = sums[first + 1, p]
    for i, proj, out in ((5, gsp.at[0], gso.at[0]), (2, gsp.at[1], gso.at[1]), (6, gcp, gco)):
        full = sums[i].reshape(parts * rows, D)
        for c in range(3):
            proj[c] = full[:, c * es : (c + 1) * es]
        out[...] = full[:, 3 * es :].T
    gcb[...] = small[0:2]
    for i, ref in enumerate((gcob, gcg, gcs)):
        ref[...] = small[2 + i : 3 + i].reshape(D)
    for s in range(2):
        gsb[s] = small[5 + 5 * s : 7 + 5 * s]
        for i, ref in enumerate((gsob, gsg, gss)):
            ref[s : s + 1] = small[7 + 5 * s + i : 8 + 5 * s + i]
        for i, ref in enumerate((gfob, gfg, gfs)):
            ref[s : s + 1] = small[15 + 3 * s + i : 16 + 3 * s + i]
        for t in range(nz):
            gfib[s : s + 1, t * D : (t + 1) * D] = small[21 + nz * s + t : 22 + nz * s + t]


def finish(es, nz, slots, sums, small, result, dinput):
    sd = jax.ShapeDtypeStruct
    chunk = D // GROUP
    vmem = pl.BlockSpec(memory_space=pltpu.VMEM)
    two, one = sd((2, D), F32), sd((D,), F32)
    shapes = (
        [sd((n, GROUP, D), dt) for dt in (BF, F32) for n in slots]
        + [sd((3, chunk, es), F32), two, sd((es, chunk), F32), one, one, one]
        + [sd((2, 3, chunk, es), F32), sd((2, 2, D), F32), sd((2, es, chunk), F32), two, two, two]
        + [sd((2, chunk, D), F32), sd((2, nz * D), F32), sd((2, chunk, D), F32), two, two, two]
    )
    return pl.pallas_call(
        functools.partial(finish_kernel, es, nz, slots),
        out_shape=shapes,
        in_specs=[pl.BlockSpec(memory_space=pltpu.HBM)] * 4,
        out_specs=[vmem] * len(shapes),
        scratch_shapes=[pltpu.VMEM(v.shape, v.dtype) for v in (sums, small, result, dinput)] + [pltpu.SemaphoreType.DMA((4,))],
        compiler_params=pltpu.CompilerParams(vmem_limit_bytes=VMEM_BYTES),
        name="finish",
    )(sums, small, result, dinput)


def dot(a, b, dims):
    return lax.dot_general(a, b, (dims, ((), ())), preferred_element_type=F32)


def per_device(nz, ndp, *args):
    (
        language,
        visual,
        word_count,
        region_count,
        task_flags,
        grad_language,
        grad_visual,
        cross_project,
        cross_bias,
        cross_out,
        cross_out_bias,
        cross_gain,
        cross_shift,
        self_project,
        self_bias,
        self_out,
        self_out_bias,
        self_gain,
        self_shift,
        feed_in,
        feed_in_bias,
        feed_out,
        feed_out_bias,
        feed_gain,
        feed_shift,
    ) = args
    items = language.shape[0]
    slots = (language.shape[1], visual.shape[1])
    counts_rows = (items * slots[0], items * slots[1])
    z = lax.axis_index("tensor")
    es = cross_project.shape[2]
    fs = feed_in.shape[2]
    lens = tuple(items // 2 * n for n in slots)
    shards = (jnp.swapaxes(cross_project, 1, 2), cross_out, jnp.swapaxes(self_project, 2, 3), self_out, feed_in, feed_out)
    sums, vectors, result, dinput = layer(
        nz,
        lens,
        shards,
        (word_count, region_count),
        task_flags.T,
        tuple(jnp.swapaxes(v, 0, 1) for v in (language, visual, grad_language, grad_visual)),
        (cross_bias, self_bias, feed_in_bias),
        (cross_out_bias, cross_gain, cross_shift, self_out_bias, self_gain, self_shift, feed_out_bias, feed_gain, feed_shift),
    )
    outer = ndp // GROUP
    if outer == 1:
        outs = list(finish(es, nz, slots, sums.reshape((7, PARTS) + sums.shape[1:]), vectors, result, dinput))
        for i in range(4):
            outs[i] = jnp.swapaxes(outs[i], 0, 1)
        outs[18] = jnp.swapaxes(outs[18], 1, 2)
        return tuple(outs)
    sums = sums.reshape(7, -1, sums.shape[2])
    if outer > 1:
        members = [[i * GROUP + j for i in range(outer)] for j in range(GROUP)]
        sums = lax.psum_scatter(sums, "dp", scatter_dimension=1, axis_index_groups=members, tiled=True)
        sums = lax.ppermute(sums, "dp", [(i * GROUP + j, j * outer + i) for i in range(outer) for j in range(GROUP)])
        vectors = lax.psum(vectors, "dp", axis_index_groups=members)
    names = [("out", 1), ("in", 1), ("self", 1), ("out", 0), ("in", 0), ("self", 0), "cross"]
    total = {name: sums[i] for i, name in enumerate(names)}

    def columns(v):
        return jnp.stack([v[:, i * es : (i + 1) * es] for i in range(3)]), v[:, 3 * es :].T

    gcp, gco = columns(total["cross"])
    gs = [columns(total["self", s]) for s in range(2)]
    v = vectors

    def by_item(x, s, shape):
        x = x[s * counts_rows[0] : s * counts_rows[0] + counts_rows[s]]
        return x.reshape(2, shape[1], shape[0] // 2, D).transpose(0, 2, 1, 3).reshape(shape)

    f0 = 21
    nf = nz * fs // D
    return (
        by_item(result, 0, language.shape),
        by_item(result, 1, visual.shape),
        by_item(dinput, 0, language.shape),
        by_item(dinput, 1, visual.shape),
        gcp,
        v[0:2],
        gco,
        v[2],
        v[3],
        v[4],
        jnp.stack([gs[0][0], gs[1][0]]),
        jnp.stack([v[5:7], v[10:12]]),
        jnp.stack([gs[0][1], gs[1][1]]),
        jnp.stack([v[7], v[12]]),
        jnp.stack([v[8], v[13]]),
        jnp.stack([v[9], v[14]]),
        jnp.stack([total["in", 0], total["in", 1]]),
        v[f0 : f0 + 2 * nf].reshape(2, nz * fs),
        jnp.stack([total["out", 0].T, total["out", 1].T]),
        jnp.stack([v[15], v[18]]),
        jnp.stack([v[16], v[19]]),
        jnp.stack([v[17], v[20]]),
    )


def solution(mesh):
    rows = P(("dp", "tensor"), None, None)
    placed = (
        rows,
        rows,
        P("dp"),
        P("dp"),
        P(("dp", "tensor"), None),
        rows,
        rows,
        P(None, None, "tensor"),
        P(None, "tensor"),
        P("tensor", None),
        P(),
        P(),
        P(),
        P(None, None, None, "tensor"),
        P(None, None, "tensor"),
        P(None, "tensor", None),
        P(),
        P(),
        P(),
        P(None, None, "tensor"),
        P(None, "tensor"),
        P(None, "tensor", None),
        P(),
        P(),
        P(),
    )
    return jax.shard_map(
        functools.partial(per_device, mesh.shape["tensor"], mesh.shape["dp"]),
        mesh=mesh,
        in_specs=placed,
        out_specs=(
            rows,
            rows,
            rows,
            rows,
            P(None, "dp", "tensor"),
            P(),
            P("tensor", "dp"),
            P(),
            P(),
            P(),
            P(None, None, "dp", "tensor"),
            P(),
            P(None, "tensor", "dp"),
            P(),
            P(),
            P(),
            P(None, "dp", "tensor"),
            P(),
            P(None, "tensor", "dp"),
            P(),
            P(),
            P(),
        ),
        check_vma=False,
    )
```

```python
import functools

import jax
import jax.numpy as jnp
from jax import lax
from jax.experimental import pallas as pl
from jax.experimental.pallas import tpu as pltpu
from jax.sharding import PartitionSpec as P

D = 768
HEAD_DIM = 64
LAYER_EPS = 1e-06
MASKED = -1e30
GROUP = 8
MESH = pl.DeviceIdType.MESH
BF = jnp.bfloat16
F32 = jnp.float32


def place():
    dp = lax.axis_index("dp")
    z = lax.axis_index("tensor")
    core = dp % 2
    bx = (dp // 2) % 2
    by = (dp // 4) % 2
    return dp, z, core, bx, by


def greet(targets):
    barrier = pltpu.get_barrier_semaphore()
    count = 0
    for device, valid in targets:
        if valid is None:
            pl.semaphore_signal(barrier, inc=1, device_id=device, device_id_type=MESH)
            count = count + 1
        else:

            @pl.when(valid)
            def _(device=device):
                pl.semaphore_signal(barrier, inc=1, device_id=device, device_id_type=MESH)

            count = count + valid.astype(jnp.int32)
    pl.semaphore_wait(barrier, count)


K_Z, K_X, K_Y, K_A, K_B, K_Z2, K_C = 0, 1, 2, 3, 4, 5, 6
TILE = 256


def gather_steps(nz, units, whole, send_sem, recv_sem, core_sem):
    dp, z, core, bx, by = place()
    low = dp % GROUP
    dev_c = (dp + 1 - 2 * core, z)
    dev_x = (dp + 2 - 4 * bx, z)
    dev_y = (dp + 4 - 8 * by, z)
    sl_x = low + 2 - 4 * bx
    sl_y = low + 4 - 8 * by
    sl_d = low + 2 - 4 * bx + 4 - 8 * by

    def copy(src, dst, u, k, kind, device):
        got = core_sem.at[u] if kind >= K_C else recv_sem.at[u, k, kind]
        return pltpu.make_async_remote_copy(
            src_ref=src, dst_ref=dst, send_sem=send_sem.at[u], recv_sem=got, device_id=device, device_id_type=MESH
        )

    def is_attention(u):
        return len(units[u]) == 2

    def part(u, j, sl, half):
        if is_attention(u):
            size = units[u][1].shape[0]
            step = size // GROUP
            rows = pl.ds(pl.multiple_of(j * size + sl * step, 8), step)
            return whole[u].at[:, rows] if half is None else whole[u].at[2 * half : 2 * half + 2, rows]
        step = units[u][0].shape[0] // GROUP
        if half is None:
            return whole[u].at[j, pl.ds(pl.multiple_of(sl * step, 8), step)]
        return whole[u].at[j, pl.ds(pl.multiple_of(sl * step + half * (step // 2), 8), step // 2)]

    def z_copies(u, k, j, device, sending):
        if is_attention(u):
            proj, out = units[u]
            size = out.shape[0]
            step = size // GROUP
            mine = pl.ds(pl.multiple_of(low * step, 8), step)
            to = pl.ds(pl.multiple_of(j * size + low * step, 8), step)
            pairs = ((proj.at[:, mine], whole[u].at[0:3, to]), (out.at[mine], whole[u].at[3, to]))
        else:
            step = units[u][0].shape[0] // GROUP
            pairs = ((units[u][0].at[pl.ds(pl.multiple_of(low * step, 8), step)], part(u, j, low, None)),)
        return [copy(src if sending else dst, dst, u, k - 1, (K_Z, K_Z2)[i], device) for i, (src, dst) in enumerate(pairs)]

    def z_send(u, k):
        for c in z_copies(u, k, z, (dp, (z + k) % nz), True):
            c.start()

    def source(k):
        return (z + nz - k) % nz

    def peer(u, k, kind, sending):
        if kind < K_C:
            sent, got, half, device = {
                K_X: (low, sl_x, None, dev_x),
                K_Y: (low, sl_y, None, dev_y),
                K_A: (sl_x, sl_d, 0, dev_y),
                K_B: (sl_y, sl_d, 1, dev_x),
            }[kind]
        else:
            sent, half = ((low, None), (sl_x, None), (sl_y, None), (sl_d, 0), (sl_d, 1))[kind - K_C]
            device = dev_c
            got = sent + 1 - 2 * core
        block = part(u, source(k), sent if sending else got, half)
        return copy(block, block, u, k - 1, kind, device)

    def stage1(u, k):
        for c in z_copies(u, k, source(k), dev_x, False):
            c.wait_recv()
        for kind in (K_X, K_Y, K_C):
            peer(u, k, kind, True).start()

    def stage2(u, k):
        peer(u, k, K_X, False).wait_recv()
        peer(u, k, K_A, True).start()
        peer(u, k, K_C + 1, True).start()
        peer(u, k, K_Y, False).wait_recv()
        peer(u, k, K_B, True).start()
        peer(u, k, K_C + 2, True).start()

    def stage3(u, k):
        peer(u, k, K_A, False).wait_recv()
        peer(u, k, K_C + 3, True).start()
        peer(u, k, K_B, False).wait_recv()
        peer(u, k, K_C + 4, True).start()

    sequence = [(u, k) for u in range(len(units)) for k in range(1, nz)]

    def step(n):
        if n < len(sequence):
            u, k = sequence[n]
            stage1(u, k)
            if u + 2 < len(units):
                z_send(u + 2, k)
        if 1 <= n < len(sequence) + 1:
            stage2(*sequence[n - 1])
        if 2 <= n < len(sequence) + 2:
            stage3(*sequence[n - 2])

    def arrived(u):
        block = whole[u].at[0 : nz - 1, 0 : D // 2]
        pltpu.make_async_copy(block, block, core_sem.at[u]).wait()

    def sent(u):
        block = whole[u].at[0 : nz - 1]
        pltpu.make_async_copy(block, block, send_sem.at[u]).wait()

    def loads(u, dst, sem):
        if is_attention(u):
            proj, out = units[u]
            size = out.shape[0]
            own = pl.ds(pl.multiple_of(z * size, 8), size)
            pairs = [(proj, dst.at[0:3, own]), (out, dst.at[3, own])]
            for k in range(1, nz):
                rows = pl.ds(pl.multiple_of(source(k) * size, 8), size)
                pairs.append((whole[u].at[:, rows], dst.at[:, rows]))
        else:
            pairs = [(units[u][0], dst.at[z])]
            for k in range(1, nz):
                pairs.append((whole[u].at[source(k)], dst.at[source(k)]))
        return [pltpu.make_async_copy(src, to, sem.at[i]) for i, (src, to) in enumerate(pairs)]

    return z_send, step, arrived, sent, loads


def project(x_ref, xrows, w_ref, w0, bias_ref, b0, out_ref):
    x = x_ref[xrows, :]
    tiles = D // TILE

    def body(i, carry):
        c, t = i // tiles, i % tiles
        at = pl.ds(pl.multiple_of(t * TILE, TILE), TILE)
        y = dot(x, w_ref[w0 + c, at, :], ((1,), (1,)))
        out_ref[c, xrows, at] = (y + bias_ref[pl.ds(b0 + c, 1), at]).astype(BF)
        return carry

    lax.fori_loop(0, 3 * tiles, body, 0)


def half_lanes():
    lane = lax.broadcasted_iota(jnp.int32, (1, 2 * HEAD_DIM), 1)
    return lane < HEAD_DIM


def attend(qkv_ref, ctx_ref, p_ref, mask_ref, q0, lq, k0, lk):
    first = half_lanes()
    keep = [jnp.where(first, HEAD_DIM**-0.5, 0.0).astype(BF), jnp.where(first, 0.0, HEAD_DIM**-0.5).astype(BF)]

    def body(pair, carry):
        lanes = pl.ds(pl.multiple_of(pair * 2 * HEAD_DIM, 2 * HEAD_DIM), 2 * HEAD_DIM)
        for g in range(2):
            qr, kr = pl.ds(q0 + g * lq, lq), pl.ds(k0 + g * lk, lk)
            q, k, v = qkv_ref[0, qr, lanes], qkv_ref[1, kr, lanes], qkv_ref[2, kr, lanes]
            parts = []
            for h in range(2):
                s = dot(q * keep[h], k, ((1,), (1,))) + mask_ref[g]
                w = jnp.exp(s - jnp.max(s, axis=1, keepdims=True))
                pb = (w * (1.0 / jnp.sum(w, axis=1, keepdims=True))).astype(BF)
                p_ref[g, 2 * pair + h] = pb
                parts.append(dot(pb, v, ((1,), (0,))))
            ctx_ref[qr, lanes] = jnp.where(first, parts[0], parts[1]).astype(BF)
        return carry

    lax.fori_loop(0, D // (2 * HEAD_DIM), body, 0, unroll=2)


def out_norm(ctx_ref, start, count, w_ref, wi, resid_ref, vec_ref, v0, pre_ref, hat_ref, rstd_ref, full_ref, low_ref):
    rows = pl.ds(start, count)
    ctx = ctx_ref[rows, :]

    def tile(t, carry):
        at = pl.ds(pl.multiple_of(t * TILE, TILE), TILE)
        y = dot(ctx, w_ref[wi, :, at], ((1,), (0,)))
        pre_ref[rows, at] = y + resid_ref[rows, at].astype(F32) + vec_ref[pl.ds(v0, 1), at]
        return carry

    lax.fori_loop(0, D // TILE, tile, 0)
    gain, shift = vec_ref[v0 + 1 : v0 + 2, :], vec_ref[v0 + 2 : v0 + 3, :]

    def norm(i, carry):
        r = pl.ds(pl.multiple_of(start + i * 32, 16), 32)
        x = pre_ref[r, :]
        center = x - jnp.sum(x, axis=1, keepdims=True) * (1.0 / D)
        rstd = lax.rsqrt(jnp.sum(center * center, axis=1, keepdims=True) * (1.0 / D) + LAYER_EPS)
        hat = center * rstd
        y = hat * gain + shift
        hat_ref[r, :] = hat.astype(BF)
        rstd_ref[r, :] = jnp.broadcast_to(rstd, (32, 128))
        full_ref[r, :] = y
        low_ref[r, :] = y.astype(BF)
        return carry

    lax.fori_loop(0, count // 32, norm, 0)


def by_group(src_ref, dst_ref, start, slots):
    half = slots * GROUP // 2
    low = lax.broadcasted_iota(jnp.int32, (8, D), 0) < 4

    def body(i, carry):
        a = [src_ref[4 * i + t].astype(F32) for t in range(4)]
        for g in range(2):
            rows = []
            for t in (0, 2):
                one, two = (a[t], pltpu.roll(a[t + 1], 4, 0)) if g == 0 else (pltpu.roll(a[t], 4, 0), a[t + 1])
                rows.append(jnp.where(low, one, two))
            at = pl.ds(pl.multiple_of(start + g * half + 16 * i, 16), 16)
            dst_ref[at, :] = jnp.concatenate(rows, axis=0).astype(dst_ref.dtype)
        return carry

    lax.fori_loop(0, slots // 4, body, 0)


def fill_masks(mask_refs, counts, first):
    for n, (ref, count) in enumerate(zip(mask_refs, counts)):
        for g in range(2):
            shape = ref.shape[1:]
            row, col = (lax.broadcasted_iota(jnp.int32, shape, d) for d in range(2))
            item = jnp.bitwise_and(col, 3)
            limit = jnp.zeros(shape, jnp.int32)
            for j in range(4):
                limit = jnp.where(item == j, count[first + 4 * g + j], limit)
            seen = jnp.logical_and(jnp.bitwise_and(row, 3) == item, jnp.right_shift(col, 2) < limit)
            ref[g] = jnp.where(seen, 0.0, MASKED).astype(F32)


SLOTS = 4
CORE_SLOTS = 6
PARTS = 3


def scatter_steps(nz, mixed, slot_bufs, send_sem, recv_sem, rs_out):
    grad, crecv, xa, yb, ya, xb, zbuf, zrecv = slot_bufs
    dp, z, core, bx, by = place()
    dev_c = (dp + 1 - 2 * core, z)
    dev_x = (dp + 2 - 4 * bx, z)
    dev_y = (dp + 4 - 8 * by, z)
    rows, width = crecv.shape[3], crecv.shape[4]
    half = width // 2
    lo, hi = pl.ds(0, half), pl.ds(half, half)
    zw = width // nz
    S_C, S_XA, S_YB, S_YA, S_XB, S_Z = 0, 1, 2, 3, 4, 5

    def part(i, c):
        return grad.at[:, :, c, pl.ds((i % PARTS) * rows, rows)]

    def remote(src, dst, s, k, device):
        return pltpu.make_async_remote_copy(
            src_ref=src, dst_ref=dst, send_sem=send_sem.at[s, k], recv_sem=recv_sem.at[s, k], device_id=device, device_id_type=MESH
        )

    def core_copy(i):
        return remote(part(i, 1 - core), crecv.at[i % CORE_SLOTS], i % CORE_SLOTS, S_C, dev_c)

    def xa_copy(i):
        s = i % SLOTS
        return remote(crecv.at[i % CORE_SLOTS, :, 1 - bx, :, lo], xa.at[s], s, S_XA, dev_x)

    def yb_copy(i):
        s = i % SLOTS
        return remote(crecv.at[i % CORE_SLOTS, 1 - by, :, :, hi], yb.at[s], s, S_YB, dev_y)

    def ya_copy(i):
        s = i % SLOTS
        return remote(crecv.at[i % CORE_SLOTS, 1 - by, bx, :, lo], ya.at[s], s, S_YA, dev_y)

    def xb_copy(i):
        s = i % SLOTS
        return remote(crecv.at[i % CORE_SLOTS, by, 1 - bx, :, hi], xb.at[s], s, S_XB, dev_x)

    def z_copy(s, k):
        return remote(zbuf.at[s, (z + k) % nz], zrecv.at[s, k - 1], s, S_Z + k - 1, (dp, (z + k) % nz))

    def merge(dst, src):
        for r in range(0, rows, 16):
            at = pl.ds(r, 16)
            dst[at] = dst[at] + src[at]

    def stage_a(i):
        core_copy(i).wait()
        mine = part(i, core)

        def body(j, carry):
            merge(crecv.at[i % CORE_SLOTS, j // 2, j % 2], mine.at[j // 2, j % 2])
            return carry

        lax.fori_loop(0, 4, body, 0, unroll=2)
        xa_copy(i).start()
        yb_copy(i).start()

    def stage_b(i):
        s = i % SLOTS
        xa_copy(i).wait()
        yb_copy(i).wait()

        def body(j, carry):
            merge(crecv.at[i % CORE_SLOTS, j, bx, :, lo], xa.at[s, j])
            merge(crecv.at[i % CORE_SLOTS, by, j, :, hi], yb.at[s, j])
            return carry

        lax.fori_loop(0, 2, body, 0, unroll=2)
        ya_copy(i).start()
        xb_copy(i).start()

    def stage_c(i):
        s = i % SLOTS
        ya_copy(i).wait()
        xb_copy(i).wait()
        own = crecv.at[i % CORE_SLOTS, by, bx]
        for r in range(0, rows, 16):
            at = pl.ds(r, 16)
            left = own[at, lo] + ya[s, at, :]
            right = own[at, hi] + xb[s, at, :]
            full = jnp.concatenate([left, right], axis=1)
            for t in range(nz):
                if mixed[i // PARTS]:
                    sub = zw // 4
                    row = [full[:, m * (width // 4) + t * sub : m * (width // 4) + (t + 1) * sub] for m in range(4)]
                    zbuf[s, t, at, :] = jnp.concatenate(row, axis=1)
                else:
                    zbuf[s, t, at, :] = full[:, t * zw : (t + 1) * zw]
        for k in range(1, nz):
            z_copy(s, k).start()

    def stage_d(i):
        s = i % SLOTS
        for k in range(1, nz):
            z_copy(s, k).wait()
        for r in range(0, rows, 16):
            at = pl.ds(r, 16)
            total = zbuf[s, z, at, :].astype(F32)
            for k in range(nz - 1):
                total = total + zrecv[s, k, at, :].astype(F32)
            rs_out[i, at, :] = total

    return core_copy, stage_a, stage_b, stage_c, stage_d


def small_steps(nz, small, sbuf, srecv, szrecv, small_out, send_sem, recv_sem):
    dp, z, core, bx, by = place()
    devs = ((dp + 1 - 2 * core, z), (dp + 2 - 4 * bx, z), (dp + 4 - 8 * by, z))

    def remote(src, dst, k, device):
        return pltpu.make_async_remote_copy(
            src_ref=src, dst_ref=dst, send_sem=send_sem.at[k], recv_sem=recv_sem.at[k], device_id=device, device_id_type=MESH
        )

    def pair(k):
        return remote(sbuf.at[k], srecv.at[k], k, devs[k])

    def along_z(k, sending):
        return remote(sbuf.at[3], szrecv.at[z if sending else (z + nz - k) % nz], 2 + k, (dp, (z + k) % nz))

    def stage(k):
        if k == 0:
            sbuf[0] = small[...]
            pair(0).start()
        elif k < 4:
            pair(k - 1).wait()
            sbuf[k] = sbuf[k - 1] + srecv[k - 1]
            if k < 3:
                pair(k).start()
            else:
                szrecv[z] = sbuf[3]
                for i in range(1, nz):
                    along_z(i, True).start()
        else:
            for i in range(1, nz):
                along_z(i, True).wait_send()
                along_z(i, False).wait_recv()
            total = szrecv[0]
            for i in range(1, nz):
                total = total + szrecv[i]
            small_out[...] = total

    return stage


def eighth(x):
    return jnp.sum(x.reshape(x.shape[0] // 8, 8, x.shape[1]), axis=0)


def transpose_into(t_ref, x_ref, start, count):
    for i in range(D // 128):
        t_ref[i * 128 : (i + 1) * 128, 0:count] = x_ref[pl.ds(start, count), i * 128 : (i + 1) * 128].T


def feed_forward(nb_ref, rows, w_ref, bias_ref, b0, h_ref, slope_ref, first, last):
    x = nb_ref[rows, :]
    tiles = D // TILE

    def body(i, carry):
        zb, t = i // tiles, i % tiles
        at = pl.ds(pl.multiple_of(t * TILE, TILE), TILE)
        u = dot(x, w_ref[zb, :, at], ((1,), (0,))) + bias_ref[pl.ds(b0 + zb, 1), at]
        phi = 0.5 + 0.5 * lax.erf(u * 0.5**0.5)
        h_ref[zb, rows, at] = (u * phi).astype(BF)
        slope_ref[zb, rows, at] = (phi + u * (jnp.exp(-0.5 * u * u) * 0.3989422804014327)).astype(BF)
        return carry

    lax.fori_loop(first * tiles, last * tiles, body, 0)


def feed_out_rows(h_ref, rows, w_ref, nn_ref, vec_ref, v0, res_ref):
    def body(t, carry):
        at = pl.ds(pl.multiple_of(t * TILE, TILE), TILE)
        y = nn_ref[rows, at] + vec_ref[pl.ds(v0, 1), at]
        for zb in range(h_ref.shape[0]):
            y = y + dot(h_ref[zb, rows, :], w_ref[zb, :, at], ((1,), (0,)))
        res_ref[rows, at] = y
        return carry

    lax.fori_loop(0, D // TILE, body, 0)


def norm_grad(hat, rstd, gain, g, acc):
    scaled = g * gain
    dz = rstd * (
        scaled - jnp.sum(scaled, axis=1, keepdims=True) * (1.0 / D) - hat * (jnp.sum(scaled * hat, axis=1, keepdims=True) * (1.0 / D))
    )
    return dz, (acc[0] + eighth(dz), acc[1] + eighth(g * hat), acc[2] + eighth(g))


def no_sums():
    return tuple(jnp.zeros((8, D), F32) for _ in range(3))


def keep_sums(acc, small, row):
    for i in range(3):
        small[row + i : row + i + 1, :] = jnp.sum(acc[i], axis=0, keepdims=True)


def last_norm(start, count, res_ref, vec_ref, v0, cot_ref, weight_ref, result_ref, db_ref, small, row):
    gain, shift = vec_ref[v0 + 1 : v0 + 2, :], vec_ref[v0 + 2 : v0 + 3, :]

    def body(i, acc):
        r = pl.ds(pl.multiple_of(start + i * 32, 16), 32)
        x = res_ref[r, :]
        center = x - jnp.sum(x, axis=1, keepdims=True) * (1.0 / D)
        rstd = lax.rsqrt(jnp.sum(center * center, axis=1, keepdims=True) * (1.0 / D) + LAYER_EPS)
        hat = center * rstd
        result_ref[r, :] = (hat * gain + shift).astype(BF)
        g = cot_ref[r, :].astype(F32) * weight_ref[r, 0:1]
        dz, acc = norm_grad(hat, rstd, gain, g, acc)
        res_ref[r, :] = dz
        db_ref[r, :] = dz.astype(BF)
        return acc

    keep_sums(lax.fori_loop(0, count // 32, body, no_sums()), small, row)


def norm_back(start, count, res_ref, hat_ref, rstd_ref, vec_ref, gain_row, db_ref, small, row):
    gain = vec_ref[gain_row : gain_row + 1, :]

    def body(i, acc):
        r = pl.ds(pl.multiple_of(start + i * 32, 16), 32)
        dz, acc = norm_grad(hat_ref[r, :].astype(F32), rstd_ref[r, 0:1], gain, res_ref[r, :], acc)
        res_ref[r, :] = dz
        db_ref[r, :] = dz.astype(BF)
        return acc

    keep_sums(lax.fori_loop(0, count // 32, body, no_sums()), small, row)


def hidden_grad(db_ref, rows, w_ref, slope_ref, small, row):
    db = db_ref[rows, :]
    tiles = D // TILE

    def body(i, carry):
        zb, t = i // tiles, i % tiles
        at = pl.ds(pl.multiple_of(t * TILE, TILE), TILE)
        du = (dot(db, w_ref[zb, at, :], ((1,), (1,))) * slope_ref[zb, rows, at].astype(F32)).astype(BF)
        slope_ref[zb, rows, at] = du
        small[pl.ds(row + zb, 1), at] = jnp.sum(eighth(du.astype(F32)), axis=0, keepdims=True)
        return carry

    lax.fori_loop(0, slope_ref.shape[0] * tiles, body, 0)


def add_products(res_ref, out_ref, rows, x_ref, count, w_ref, transposed):
    def body(t, carry):
        at = pl.ds(pl.multiple_of(t * TILE, TILE), TILE)
        y = res_ref[rows, at]
        for c in range(count):
            if transposed:
                y = y + dot(x_ref[c, rows, :], w_ref[c, at, :], ((1,), (1,)))
            else:
                y = y + dot(x_ref[c, rows, :], w_ref[c, :, at], ((1,), (0,)))
        out_ref[rows, at] = y
        return carry

    lax.fori_loop(0, D // TILE, body, 0)


def context_grad(db_ref, rows, w_ref, dctx_ref):
    db = db_ref[rows, :]

    def body(t, carry):
        at = pl.ds(pl.multiple_of(t * TILE, TILE), TILE)
        dctx_ref[rows, at] = dot(db, w_ref[3, at, :], ((1,), (1,))).astype(BF)
        return carry

    lax.fori_loop(0, D // TILE, body, 0)


def attend_back(qkv_ref, dctx_ref, p_ref, out_ref, q0, lq, k0, lk, first_pair=0, last_pair=D // (2 * HEAD_DIM)):
    first = half_lanes()
    keep = [jnp.where(first, 1.0, 0.0).astype(BF), jnp.where(first, 0.0, 1.0).astype(BF)]

    def body(pair, carry):
        lanes = pl.ds(pl.multiple_of(pair * 2 * HEAD_DIM, 2 * HEAD_DIM), 2 * HEAD_DIM)
        for g in range(2):
            qr, kr = pl.ds(q0 + g * lq, lq), pl.ds(k0 + g * lk, lk)
            q, k, v, dc = qkv_ref[0, qr, lanes], qkv_ref[1, kr, lanes], qkv_ref[2, kr, lanes], dctx_ref[qr, lanes]
            dq, dk, dv = [], [], []
            for h in range(2):
                pb = p_ref[g, 2 * pair + h]
                p = pb.astype(F32)
                dp = dot(dc * keep[h], v, ((1,), (1,)))
                ds = (p * (dp - jnp.sum(p * dp, axis=1, keepdims=True))).astype(BF)
                dq.append(dot(ds, k, ((1,), (0,))))
                dk.append(dot(ds, q, ((0,), (0,))))
                dv.append(dot(pb, dc, ((0,), (0,))))
            out_ref[0, qr, lanes] = (jnp.where(first, dq[0], dq[1]) * HEAD_DIM**-0.5).astype(BF)
            out_ref[1, kr, lanes] = (jnp.where(first, dk[0], dk[1]) * HEAD_DIM**-0.5).astype(BF)
            out_ref[2, kr, lanes] = jnp.where(first, dv[0], dv[1]).astype(BF)
        return carry

    lax.fori_loop(first_pair, last_pair, body, 0)


def bias_sums(x_ref, rows, count, small, row_q, row_v, add):
    ones = jnp.ones((8, count), BF)
    for c, row in ((0, row_q), (2, row_v)):
        total = dot(ones, x_ref[c, rows, :], ((1,), (0,)))[0:1, :]
        small[row : row + 1, :] = total


def grad_tiles(grad_ref, m, t_ref, count, x_ref, rows, first, last, lane0, mats):
    size = grad_ref.shape[3]
    left = t_ref[:, 0:count]
    tiles = D // TILE

    def body(i, carry):
        b, t = i // tiles, i % tiles
        at = pl.ds(pl.multiple_of(t * TILE, TILE), TILE)
        right = x_ref[b, rows, at] if mats else x_ref[rows, at]
        y = dot(left, right, ((1,), (0,))).astype(BF)
        lanes = pl.ds(pl.multiple_of(lane0 + i * TILE, TILE), TILE)
        grad_ref[:, :, :, :, lanes] = y.reshape(2, 2, 2, size, TILE)
        return carry

    lax.fori_loop(first * tiles, last * tiles, body, 0, unroll=3)


CROSS, SELF1, IN1, OUT1, SELF0, IN0, OUT0 = range(7)
MIXED = (False, False, True, False, False, True, True)


def layer_kernel(nz, lens, *refs):
    cp, co, sp, so, fi, fo, word_count, region_count, flags = refs[:9]
    lang, vis, cot_lang, cot_vis, cross_b, self_b, feed_b = refs[9:16]
    cob, cg, cs, sob, sg, ss, fob, fg, fs = refs[16:25]
    whole = refs[25:32]
    rs_out, small_out, result, res = refs[32:36]
    wb3 = refs[36]
    refs = refs[1:]
    wb0, wb1, wb2, x, qkv_c, ctx_c, p_c0, p_c1, hat1, rstd1, mb = refs[36:47]
    qkv_s, ctx_s, p_s0, p_s1, hat2, rstd2, mid, nb, hid, slope, db, dctx, t1, t2, small = refs[47:62]
    grad, crecv, xa, yb, ya, xb, zbuf, zrecv, sbuf, srecv, szrecv = refs[62:73]
    bias_src, bias_all, bias_ref, vec, weight = refs[73:78]
    masks = refs[78:82]
    send_sem, recv_sem, core_sem, w_sem, bias_send, bias_recv, rs_send, rs_recv, small_send, small_recv = refs[82:]
    dp, z, core, bx, by = place()
    lw, lv = lens
    rw, rv = 2 * lw, 2 * lv
    start, count = (0, rw), (rw, rv)
    rows = (pl.ds(0, rw), pl.ds(rw, rv))
    every = pl.ds(0, rw + rv)

    bias_src[...] = jnp.zeros_like(bias_src)
    part = cross_b.shape[1]
    for t in range(nz):

        @pl.when(z == t)
        def _(t=t):
            lanes = slice(t * part, (t + 1) * part)
            for i in range(2):
                bias_src[2 * i : 2 * i + 1, lanes] = cross_b[i : i + 1, :]
                for s in range(2):
                    bias_src[3 + 3 * s + 2 * i : 4 + 3 * s + 2 * i, lanes] = self_b[s, i : i + 1, :]
            for s in range(2):
                bias_src[9 + nz * s + t : 10 + nz * s + t, :] = feed_b[s : s + 1, :]

    targets = [((dp + 1 - 2 * core, z), None), ((dp + 2 - 4 * bx, z), None), ((dp + 4 - 8 * by, z), None)]
    for k in range(1, nz):
        targets.append(((dp, (z + k) % nz), None))
    greet(targets)
    units = (
        (cp, co),
        (sp.at[1], so.at[1]),
        (fi.at[1],),
        (fo.at[1],),
        (sp.at[0], so.at[0]),
        (fi.at[0],),
        (fo.at[0],),
    )
    z_send, gather, arrived, sent, loads = gather_steps(nz, units, whole, send_sem, recv_sem, core_sem)
    slot_bufs = (grad, crecv, xa, yb, ya, xb, zbuf, zrecv)
    core_copy, stage_a, stage_b, stage_c, stage_d = scatter_steps(nz, MIXED, slot_bufs, rs_send, rs_recv, rs_out)
    small_stage = small_steps(nz, small, sbuf, srecv, szrecv, small_out, small_send, small_recv)
    pieces = len(MIXED) * PARTS

    def scatter(n):
        if n + 1 < pieces and (n + 1) % PARTS:
            core_copy(n + 1).start()
        if n < pieces:
            stage_a(n)
        if 1 <= n < pieces + 1:
            stage_b(n - 1)
        if 2 <= n < pieces + 2:
            stage_c(n - 2)
        if 3 <= n < pieces + 3:
            stage_d(n - 3)

    def bias_copy(k, sending):
        return pltpu.make_async_remote_copy(
            src_ref=bias_src,
            dst_ref=bias_all.at[z if sending else (z + nz - k) % nz],
            send_sem=bias_send.at[k],
            recv_sem=bias_recv.at[k],
            device_id=(dp, (z + k) % nz),
            device_id_type=MESH,
        )

    def fetch(u, dst):
        arrived(u)
        for c in loads(u, dst, w_sem.at[u]):
            c.start()

    def ready(u, dst):
        for c in loads(u, dst, w_sem.at[u]):
            c.wait()

    cot = dctx

    def prepare():
        for i, ref in enumerate((cob, cg, cs)):
            vec[i : i + 1, :] = ref[...].reshape(1, D)
        for s in range(2):
            for i, ref in enumerate((sob, sg, ss)):
                vec[3 + 3 * s + i : 4 + 3 * s + i, :] = ref[s : s + 1, :]
            for i, ref in enumerate((fob, fg, fs)):
                vec[9 + 3 * s + i : 10 + 3 * s + i, :] = ref[s : s + 1, :]
        by_group(lang, x, 0, lang.shape[0])
        by_group(vis, x, rw, vis.shape[0])
        by_group(cot_lang, cot, 0, cot_lang.shape[0])
        by_group(cot_vis, cot, rw, cot_vis.shape[0])
        fill_masks(masks, (region_count, word_count, word_count, region_count), z * GROUP)
        for s in range(2):
            for g in range(2):
                row = lax.broadcasted_iota(jnp.int32, (lens[s], 128), 0)
                item = jnp.bitwise_and(row, 3)
                value = jnp.zeros((lens[s], 128), F32)
                for j in range(4):
                    n = 4 * g + j
                    other = flags[0, n].astype(F32)
                    if s == 0:
                        answer = jnp.maximum(flags[1, n], flags[2, n]).astype(F32)
                        value = jnp.where(item == j, jnp.where(row < 4, answer, other), value)
                    else:
                        value = jnp.where(item == j, other, value)
                weight[start[s] + g * lens[s] : start[s] + (g + 1) * lens[s], :] = value

    def bias_sum():
        for k in range(1, nz):
            bias_copy(k, False).wait_recv()
        bias_all[z] = bias_src[...]
        total = bias_all[0]
        for k in range(1, nz):
            total = total + bias_all[k]
        bias_ref[...] = total

    w_self, w_in, w_out = (wb3, wb1), (wb2, wb2), (wb1, wb3)
    u_self, u_in, u_out = (SELF0, SELF1), (IN0, IN1), (OUT0, OUT1)

    def cross_project_all():
        ready(CROSS, wb0)
        bias_sum()
        project(x, every, wb0, 0, bias_ref, 0, qkv_c)

    def cross_forward(s):
        if s == 0:
            attend(qkv_c, ctx_c, p_c0, masks[0], 0, lw, rw, lv)
        else:
            attend(qkv_c, ctx_c, p_c1, masks[1], rw, lv, 0, lw)

    def cross_norm(s):
        out_norm(ctx_c, start[s], count[s], wb0, 3, x, vec, 0, res, hat1, rstd1, mid, mb)

    def self_project(s):
        ready(u_self[s], w_self[s])
        project(mb, rows[s], w_self[s], 0, bias_ref, 3 + 3 * s, qkv_s)

    def self_forward(s):
        attend(qkv_s, ctx_s, (p_s0, p_s1)[s], masks[2 + s], start[s], lens[s], start[s], lens[s])

    def self_norm(s):
        out_norm(ctx_s, start[s], count[s], w_self[s], 3, mid, vec, 3 + 3 * s, res, hat2, rstd2, mid, nb)

    def forward(s, first, last):
        if first == 0:
            ready(u_in[s], w_in[s])
        feed_forward(nb, rows[s], w_in[s], bias_ref, 9 + nz * s, hid, slope, first, last)

    def out_rows(s):
        ready(u_out[s], w_out[s])
        feed_out_rows(hid, rows[s], w_out[s], mid, vec, 9 + 3 * s, res)

    def norm3(s):
        last_norm(start[s], count[s], res, vec, 9 + 3 * s, cot, weight, result, db, small, 15 + 3 * s)

    def du(s):
        hidden_grad(db, rows[s], w_out[s], slope, small, 21 + nz * s)

    def dn(s):
        add_products(res, res, rows[s], slope, nz, w_in[s], True)

    def self_in(s):
        norm_back(start[s], count[s], res, hat2, rstd2, vec, 4 + 3 * s, db, small, 7 + 5 * s)
        context_grad(db, rows[s], w_self[s], dctx)

    def self_back(s, first, last):
        attend_back(qkv_s, dctx, (p_s0, p_s1)[s], hid, start[s], lens[s], start[s], lens[s], first, last)

    def self_sums(s):
        bias_sums(hid, rows[s], count[s], small, 5 + 5 * s, 6 + 5 * s, False)

    def dm(s):
        add_products(res, res, rows[s], hid, 3, w_self[s], False)

    def cross_in():
        norm_back(0, rw + rv, res, hat1, rstd1, vec, 1, nb, small, 2)
        context_grad(nb, every, wb0, dctx)

    def cross_back(s, first, last):
        attend_back(qkv_c, dctx, (p_c0, p_c1)[s], slope, start[s], lens[s], start[1 - s], lens[1 - s], first, last)

    def cross_sums():
        bias_sums(slope, every, rw + rv, small, 0, 1, False)
        small_stage(0)

    def finish_rows():
        add_products(res, res, every, slope, 3, wb0, False)

    def grads(m):
        if m < 6:
            s = 1 - m // 3
            if m % 3 < 2:
                turned, src, right = ((t1, db, hid), (t2, nb, slope))[m % 3]
                transpose_into(turned, src, start[s], count[s])
                grad_tiles(grad, m, turned, count[s], right, rows[s], 0, nz, 0, True)
                core_copy(m * PARTS).start()
                return
            src, at, n, back, ctx, dqkv, dz = mb, start[s], count[s], rows[s], ctx_s, hid, db
        else:
            src, at, n, back, ctx, dqkv, dz = x, 0, rw + rv, every, ctx_c, slope, nb
        transpose_into(t1, dz, at, n)
        transpose_into(t2, src, at, n)
        grad_tiles(grad, m, t2, n, dqkv, back, 0, 3, 0, True)
        grad_tiles(grad, m, t1, n, ctx, back, 0, 1, 3 * D, False)
        core_copy(m * PARTS).start()

    for k in range(1, nz):
        z_send(0, k)
    for k in range(1, nz):
        bias_copy(k, True).start()
    for k in range(1, nz):
        z_send(1, k)
    prepare()
    for n in range(5):
        gather(n)
    fetch(CROSS, wb0)
    gather(5)
    cross_project_all()
    gather(6)
    cross_forward(1)
    gather(7)
    fetch(SELF1, wb1)
    cross_norm(1)
    gather(8)
    self_project(1)
    gather(9)
    self_forward(1)
    gather(10)
    fetch(IN1, wb2)
    self_norm(1)
    gather(11)
    forward(1, 0, 2)
    gather(12)
    forward(1, 2, nz)
    gather(13)
    fetch(OUT1, wb3)
    gather(14)
    out_rows(1)
    norm3(1)
    grads(0)
    gather(15)
    du(1)
    scatter(0)
    gather(16)
    fetch(SELF0, wb3)
    dn(1)
    scatter(1)
    gather(17)
    self_in(1)
    scatter(2)
    grads(1)
    gather(18)
    self_back(1, 0, 3)
    scatter(3)
    gather(19)
    fetch(IN0, wb2)
    self_back(1, 3, 6)
    scatter(4)
    gather(20)
    dm(1)
    self_sums(1)
    scatter(5)
    grads(2)
    gather(21)
    cross_forward(0)
    scatter(6)
    gather(22)
    fetch(OUT0, wb1)
    cross_norm(0)
    self_project(0)
    self_forward(0)
    scatter(7)
    self_norm(0)
    forward(0, 0, nz)
    out_rows(0)
    norm3(0)
    scatter(8)
    grads(3)
    du(0)
    scatter(9)
    dn(0)
    self_in(0)
    scatter(10)
    self_back(0, 0, 6)
    scatter(11)
    grads(4)
    dm(0)
    cross_in()
    scatter(12)
    cross_back(0, 0, 3)
    scatter(13)
    cross_back(0, 3, 6)
    scatter(14)
    self_sums(0)
    grads(5)
    cross_back(1, 0, 3)
    scatter(15)
    cross_back(1, 3, 6)
    scatter(16)
    cross_sums()
    scatter(17)
    grads(6)
    scatter(18)
    small_stage(1)
    scatter(19)
    small_stage(2)
    finish_rows()
    scatter(20)
    small_stage(3)
    scatter(21)
    small_stage(4)
    scatter(22)
    scatter(23)
    for u in range(len(units)):
        sent(u)
    for k in range(1, nz):
        bias_copy(k, True).wait_send()


def layer(nz, lens, shards, counts, flags, inputs, biases, vectors):
    rows = 2 * sum(lens)
    lw, lv = lens
    nh = D // HEAD_DIM
    size = D // GROUP // PARTS
    width = 4 * D
    any_spec = pl.BlockSpec(memory_space=pl.ANY)
    vmem = pl.BlockSpec(memory_space=pltpu.VMEM)
    smem = pl.BlockSpec(memory_space=pltpu.SMEM)
    sd = jax.ShapeDtypeStruct
    vm = pltpu.VMEM
    total = len(MIXED) * PARTS
    dma = pltpu.SemaphoreType.DMA
    act = vm((rows, D), BF)
    outs = pl.pallas_call(
        functools.partial(layer_kernel, nz, lens),
        out_shape=[sd((4, D, D), BF)] * 7
        + [sd((total, size, width // nz), F32), sd((32, D), F32), sd((rows, D), BF), sd((rows, D), F32)],
        in_specs=[any_spec] * 6 + [smem] * 3 + [vmem] * 16,
        out_specs=[any_spec] * 7 + [vmem] * 4,
        scratch_shapes=[
            vm((4, D, D), BF),
            vm((4, D, D), BF),
            vm((4, D, D), BF),
            vm((4, D, D), BF),
            act,
            vm((3, rows, D), BF),
            act,
            vm((2, nh, lw, lv), BF),
            vm((2, nh, lv, lw), BF),
            act,
            vm((rows, 128), F32),
            act,
            vm((3, rows, D), BF),
            act,
            vm((2, nh, lw, lw), BF),
            vm((2, nh, lv, lv), BF),
            act,
            vm((rows, 128), F32),
            vm((rows, D), F32),
            act,
            vm((nz, rows, D), BF),
            vm((nz, rows, D), BF),
            act,
            act,
            vm((D, rows), BF),
            vm((D, rows), BF),
            vm((32, D), F32),
            vm((2, 2, 2, size * PARTS, width), BF),
            vm((CORE_SLOTS, 2, 2, size, width), BF),
            vm((SLOTS, 2, size, width // 2), BF),
            vm((SLOTS, 2, size, width // 2), BF),
            vm((SLOTS, size, width // 2), BF),
            vm((SLOTS, size, width // 2), BF),
            vm((SLOTS, nz, size, width // nz), BF),
            vm((SLOTS, nz - 1, size, width // nz), BF),
            vm((4, 32, D), F32),
            vm((3, 32, D), F32),
            vm((nz, 32, D), F32),
            vm((24, D), F32),
            vm((nz, 24, D), F32),
            vm((24, D), F32),
            vm((16, D), F32),
            vm((rows, 128), F32),
            vm((2, lw, lv), F32),
            vm((2, lv, lw), F32),
            vm((2, lw, lw), F32),
            vm((2, lv, lv), F32),
            dma((7,)),
            dma((7, nz - 1, K_C)),
            dma((7,)),
            dma((7, nz + 1)),
            dma((nz,)),
            dma((nz,)),
            dma((CORE_SLOTS, 4 + nz)),
            dma((CORE_SLOTS, 4 + nz)),
            dma((2 + nz,)),
            dma((2 + nz,)),
        ],
        compiler_params=pltpu.CompilerParams(collective_id=1, has_side_effects=True, vmem_limit_bytes=VMEM_BYTES),
        name="layer",
    )(*shards, *counts, flags, *inputs, *biases, *vectors)
    return outs[7:]


VMEM_BYTES = 63 << 20


def finish_kernel(es, nz, slots, *refs):
    loads = [pltpu.make_async_copy(src, dst, refs[30].at[i]) for i, (src, dst) in enumerate(zip(refs[:4], refs[26:30]))]
    for c in loads:
        c.start()
    sums, small, result, dinput = refs[26:30]
    refs = refs[:26]
    lang, vis, dlang, dvis, gcp, gcb, gco, gcob, gcg, gcs, gsp, gsb, gso, gsob, gsg, gss, gfi, gfib, gfo, gfob, gfg, gfs = refs[4:]
    parts, rows = sums.shape[1], sums.shape[2]
    low = lax.broadcasted_iota(jnp.int32, (8, D), 0) < 4

    def by_slot(src, dst, start, n):
        half = n * GROUP // 2

        def body(i, carry):
            g = [src[pl.ds(pl.multiple_of(start + h * half + 16 * i, 16), 16), :].astype(F32) for h in range(2)]
            for t in range(2):
                one, two = g[0][8 * t : 8 * t + 8], g[1][8 * t : 8 * t + 8]
                dst[4 * i + 2 * t] = jnp.where(low, one, pltpu.roll(two, 4, 0)).astype(dst.dtype)
                dst[4 * i + 2 * t + 1] = jnp.where(low, pltpu.roll(one, 4, 0), two).astype(dst.dtype)
            return carry

        lax.fori_loop(0, n // 4, body, 0)

    loads[2].wait()
    by_slot(result, lang, 0, slots[0])
    by_slot(result, vis, GROUP * slots[0], slots[1])
    loads[3].wait()
    by_slot(dinput, dlang, 0, slots[0])
    by_slot(dinput, dvis, GROUP * slots[0], slots[1])
    loads[0].wait()
    loads[1].wait()
    for s in range(2):
        first = 3 * (1 - s)
        for p in range(parts):
            gfo[s, p * rows : (p + 1) * rows, :] = sums[first, p]
            gfi[s, p * rows : (p + 1) * rows, :] = sums[first + 1, p]
    for i, proj, out in ((5, gsp.at[0], gso.at[0]), (2, gsp.at[1], gso.at[1]), (6, gcp, gco)):
        full = sums[i].reshape(parts * rows, D)
        for c in range(3):
            proj[c] = full[:, c * es : (c + 1) * es]
        out[...] = full[:, 3 * es :].T
    gcb[...] = small[0:2]
    for i, ref in enumerate((gcob, gcg, gcs)):
        ref[...] = small[2 + i : 3 + i].reshape(D)
    for s in range(2):
        gsb[s] = small[5 + 5 * s : 7 + 5 * s]
        for i, ref in enumerate((gsob, gsg, gss)):
            ref[s : s + 1] = small[7 + 5 * s + i : 8 + 5 * s + i]
        for i, ref in enumerate((gfob, gfg, gfs)):
            ref[s : s + 1] = small[15 + 3 * s + i : 16 + 3 * s + i]
        for t in range(nz):
            gfib[s : s + 1, t * D : (t + 1) * D] = small[21 + nz * s + t : 22 + nz * s + t]


def finish(es, nz, slots, sums, small, result, dinput):
    sd = jax.ShapeDtypeStruct
    chunk = D // GROUP
    vmem = pl.BlockSpec(memory_space=pltpu.VMEM)
    two, one = sd((2, D), F32), sd((D,), F32)
    shapes = (
        [sd((n, GROUP, D), dt) for dt in (BF, F32) for n in slots]
        + [sd((3, chunk, es), F32), two, sd((es, chunk), F32), one, one, one]
        + [sd((2, 3, chunk, es), F32), sd((2, 2, D), F32), sd((2, es, chunk), F32), two, two, two]
        + [sd((2, chunk, D), F32), sd((2, nz * D), F32), sd((2, chunk, D), F32), two, two, two]
    )
    return pl.pallas_call(
        functools.partial(finish_kernel, es, nz, slots),
        out_shape=shapes,
        in_specs=[pl.BlockSpec(memory_space=pltpu.HBM)] * 4,
        out_specs=[vmem] * len(shapes),
        scratch_shapes=[pltpu.VMEM(v.shape, v.dtype) for v in (sums, small, result, dinput)] + [pltpu.SemaphoreType.DMA((4,))],
        compiler_params=pltpu.CompilerParams(vmem_limit_bytes=VMEM_BYTES),
        name="finish",
    )(sums, small, result, dinput)


def dot(a, b, dims):
    return lax.dot_general(a, b, (dims, ((), ())), preferred_element_type=F32)


def per_device(nz, ndp, *args):
    (
        language,
        visual,
        word_count,
        region_count,
        task_flags,
        grad_language,
        grad_visual,
        cross_project,
        cross_bias,
        cross_out,
        cross_out_bias,
        cross_gain,
        cross_shift,
        self_project,
        self_bias,
        self_out,
        self_out_bias,
        self_gain,
        self_shift,
        feed_in,
        feed_in_bias,
        feed_out,
        feed_out_bias,
        feed_gain,
        feed_shift,
    ) = args
    items = language.shape[0]
    slots = (language.shape[1], visual.shape[1])
    counts_rows = (items * slots[0], items * slots[1])
    z = lax.axis_index("tensor")
    es = cross_project.shape[2]
    fs = feed_in.shape[2]
    lens = tuple(items // 2 * n for n in slots)
    shards = (jnp.swapaxes(cross_project, 1, 2), cross_out, jnp.swapaxes(self_project, 2, 3), self_out, feed_in, feed_out)
    sums, vectors, result, dinput = layer(
        nz,
        lens,
        shards,
        (word_count, region_count),
        task_flags.T,
        tuple(jnp.swapaxes(v, 0, 1) for v in (language, visual, grad_language, grad_visual)),
        (cross_bias, self_bias, feed_in_bias),
        (cross_out_bias, cross_gain, cross_shift, self_out_bias, self_gain, self_shift, feed_out_bias, feed_gain, feed_shift),
    )
    outer = ndp // GROUP
    if outer == 1:
        outs = list(finish(es, nz, slots, sums.reshape((7, PARTS) + sums.shape[1:]), vectors, result, dinput))
        for i in range(4):
            outs[i] = jnp.swapaxes(outs[i], 0, 1)
        outs[18] = jnp.swapaxes(outs[18], 1, 2)
        return tuple(outs)
    sums = sums.reshape(7, -1, sums.shape[2])
    if outer > 1:
        members = [[i * GROUP + j for i in range(outer)] for j in range(GROUP)]
        sums = lax.psum_scatter(sums, "dp", scatter_dimension=1, axis_index_groups=members, tiled=True)
        sums = lax.ppermute(sums, "dp", [(i * GROUP + j, j * outer + i) for i in range(outer) for j in range(GROUP)])
        vectors = lax.psum(vectors, "dp", axis_index_groups=members)
    names = [("out", 1), ("in", 1), ("self", 1), ("out", 0), ("in", 0), ("self", 0), "cross"]
    total = {name: sums[i] for i, name in enumerate(names)}

    def columns(v):
        return jnp.stack([v[:, i * es : (i + 1) * es] for i in range(3)]), v[:, 3 * es :].T

    gcp, gco = columns(total["cross"])
    gs = [columns(total["self", s]) for s in range(2)]
    v = vectors

    def by_item(x, s, shape):
        x = x[s * counts_rows[0] : s * counts_rows[0] + counts_rows[s]]
        return x.reshape(2, shape[1], shape[0] // 2, D).transpose(0, 2, 1, 3).reshape(shape)

    f0 = 21
    nf = nz * fs // D
    return (
        by_item(result, 0, language.shape),
        by_item(result, 1, visual.shape),
        by_item(dinput, 0, language.shape),
        by_item(dinput, 1, visual.shape),
        gcp,
        v[0:2],
        gco,
        v[2],
        v[3],
        v[4],
        jnp.stack([gs[0][0], gs[1][0]]),
        jnp.stack([v[5:7], v[10:12]]),
        jnp.stack([gs[0][1], gs[1][1]]),
        jnp.stack([v[7], v[12]]),
        jnp.stack([v[8], v[13]]),
        jnp.stack([v[9], v[14]]),
        jnp.stack([total["in", 0], total["in", 1]]),
        v[f0 : f0 + 2 * nf].reshape(2, nz * fs),
        jnp.stack([total["out", 0].T, total["out", 1].T]),
        jnp.stack([v[15], v[18]]),
        jnp.stack([v[16], v[19]]),
        jnp.stack([v[17], v[20]]),
    )


def solution(mesh):
    rows = P(("dp", "tensor"), None, None)
    placed = (
        rows,
        rows,
        P("dp"),
        P("dp"),
        P(("dp", "tensor"), None),
        rows,
        rows,
        P(None, None, "tensor"),
        P(None, "tensor"),
        P("tensor", None),
        P(),
        P(),
        P(),
        P(None, None, None, "tensor"),
        P(None, None, "tensor"),
        P(None, "tensor", None),
        P(),
        P(),
        P(),
        P(None, None, "tensor"),
        P(None, "tensor"),
        P(None, "tensor", None),
        P(),
        P(),
        P(),
    )
    return jax.shard_map(
        functools.partial(per_device, mesh.shape["tensor"], mesh.shape["dp"]),
        mesh=mesh,
        in_specs=placed,
        out_specs=(
            rows,
            rows,
            rows,
            rows,
            P(None, "dp", "tensor"),
            P(),
            P("tensor", "dp"),
            P(),
            P(),
            P(),
            P(None, None, "dp", "tensor"),
            P(),
            P(None, "tensor", "dp"),
            P(),
            P(),
            P(),
            P(None, "dp", "tensor"),
            P(),
            P(None, "tensor", "dp"),
            P(),
            P(),
            P(),
        ),
        check_vma=False,
    )
```

```python
import functools

import jax
import jax.numpy as jnp
from jax import lax
from jax.experimental import pallas as pl
from jax.experimental.pallas import tpu as pltpu
from jax.sharding import PartitionSpec as P

D = 768
HEAD_DIM = 64
LAYER_EPS = 1e-06
MASKED = -1e30
GROUP = 8
MESH = pl.DeviceIdType.MESH
BF = jnp.bfloat16
F32 = jnp.float32


def place():
    dp = lax.axis_index("dp")
    z = lax.axis_index("tensor")
    core = dp % 2
    bx = (dp // 2) % 2
    by = (dp // 4) % 2
    return dp, z, core, bx, by


def greet(targets):
    barrier = pltpu.get_barrier_semaphore()
    count = 0
    for device, valid in targets:
        if valid is None:
            pl.semaphore_signal(barrier, inc=1, device_id=device, device_id_type=MESH)
            count = count + 1
        else:

            @pl.when(valid)
            def _(device=device):
                pl.semaphore_signal(barrier, inc=1, device_id=device, device_id_type=MESH)

            count = count + valid.astype(jnp.int32)
    pl.semaphore_wait(barrier, count)


K_Z, K_X, K_Y, K_A, K_B, K_Z2, K_C = 0, 1, 2, 3, 4, 5, 6
TILE = 256


def gather_steps(nz, units, whole, send_sem, recv_sem, core_sem):
    dp, z, core, bx, by = place()
    low = dp % GROUP
    dev_c = (dp + 1 - 2 * core, z)
    dev_x = (dp + 2 - 4 * bx, z)
    dev_y = (dp + 4 - 8 * by, z)
    sl_x = low + 2 - 4 * bx
    sl_y = low + 4 - 8 * by
    sl_d = low + 2 - 4 * bx + 4 - 8 * by

    def copy(src, dst, u, k, kind, device):
        got = core_sem.at[u] if kind >= K_C else recv_sem.at[u, k, kind]
        return pltpu.make_async_remote_copy(
            src_ref=src, dst_ref=dst, send_sem=send_sem.at[u], recv_sem=got, device_id=device, device_id_type=MESH
        )

    def is_attention(u):
        return len(units[u]) == 2

    def part(u, j, sl, half):
        if is_attention(u):
            size = units[u][1].shape[0]
            step = size // GROUP
            rows = pl.ds(pl.multiple_of(j * size + sl * step, 8), step)
            return whole[u].at[:, rows] if half is None else whole[u].at[2 * half : 2 * half + 2, rows]
        step = units[u][0].shape[0] // GROUP
        if half is None:
            return whole[u].at[j, pl.ds(pl.multiple_of(sl * step, 8), step)]
        return whole[u].at[j, pl.ds(pl.multiple_of(sl * step + half * (step // 2), 8), step // 2)]

    def z_copies(u, k, j, device, sending):
        if is_attention(u):
            proj, out = units[u]
            size = out.shape[0]
            step = size // GROUP
            mine = pl.ds(pl.multiple_of(low * step, 8), step)
            to = pl.ds(pl.multiple_of(j * size + low * step, 8), step)
            pairs = ((proj.at[:, mine], whole[u].at[0:3, to]), (out.at[mine], whole[u].at[3, to]))
        else:
            step = units[u][0].shape[0] // GROUP
            pairs = ((units[u][0].at[pl.ds(pl.multiple_of(low * step, 8), step)], part(u, j, low, None)),)
        return [copy(src if sending else dst, dst, u, k - 1, (K_Z, K_Z2)[i], device) for i, (src, dst) in enumerate(pairs)]

    def z_send(u, k):
        for c in z_copies(u, k, z, (dp, (z + k) % nz), True):
            c.start()

    def source(k):
        return (z + nz - k) % nz

    def peer(u, k, kind, sending):
        if kind < K_C:
            sent, got, half, device = {
                K_X: (low, sl_x, None, dev_x),
                K_Y: (low, sl_y, None, dev_y),
                K_A: (sl_x, sl_d, 0, dev_y),
                K_B: (sl_y, sl_d, 1, dev_x),
            }[kind]
        else:
            sent, half = ((low, None), (sl_x, None), (sl_y, None), (sl_d, 0), (sl_d, 1))[kind - K_C]
            device = dev_c
            got = sent + 1 - 2 * core
        block = part(u, source(k), sent if sending else got, half)
        return copy(block, block, u, k - 1, kind, device)

    def stage1(u, k):
        for c in z_copies(u, k, source(k), dev_x, False):
            c.wait_recv()
        for kind in (K_X, K_Y, K_C):
            peer(u, k, kind, True).start()

    def stage2(u, k):
        peer(u, k, K_X, False).wait_recv()
        peer(u, k, K_A, True).start()
        peer(u, k, K_C + 1, True).start()
        peer(u, k, K_Y, False).wait_recv()
        peer(u, k, K_B, True).start()
        peer(u, k, K_C + 2, True).start()

    def stage3(u, k):
        peer(u, k, K_A, False).wait_recv()
        peer(u, k, K_C + 3, True).start()
        peer(u, k, K_B, False).wait_recv()
        peer(u, k, K_C + 4, True).start()

    sequence = [(u, k) for u in range(len(units)) for k in range(1, nz)]

    def step(n):
        if n < len(sequence):
            u, k = sequence[n]
            stage1(u, k)
            if u + 2 < len(units):
                z_send(u + 2, k)
        if 1 <= n < len(sequence) + 1:
            stage2(*sequence[n - 1])
        if 2 <= n < len(sequence) + 2:
            stage3(*sequence[n - 2])

    def arrived(u):
        block = whole[u].at[0 : nz - 1, 0 : D // 2]
        pltpu.make_async_copy(block, block, core_sem.at[u]).wait()

    def sent(u):
        block = whole[u].at[0 : nz - 1]
        pltpu.make_async_copy(block, block, send_sem.at[u]).wait()

    def loads(u, dst, sem):
        if is_attention(u):
            proj, out = units[u]
            size = out.shape[0]
            own = pl.ds(pl.multiple_of(z * size, 8), size)
            pairs = [(proj, dst.at[0:3, own]), (out, dst.at[3, own])]
            for k in range(1, nz):
                rows = pl.ds(pl.multiple_of(source(k) * size, 8), size)
                pairs.append((whole[u].at[:, rows], dst.at[:, rows]))
        else:
            pairs = [(units[u][0], dst.at[z])]
            for k in range(1, nz):
                pairs.append((whole[u].at[source(k)], dst.at[source(k)]))
        return [pltpu.make_async_copy(src, to, sem.at[i]) for i, (src, to) in enumerate(pairs)]

    return z_send, step, arrived, sent, loads


def project(x_ref, xrows, w_ref, w0, bias_ref, b0, out_ref):
    x = x_ref[xrows, :]
    tiles = D // TILE

    def body(i, carry):
        c, t = i // tiles, i % tiles
        at = pl.ds(pl.multiple_of(t * TILE, TILE), TILE)
        y = dot(x, w_ref[w0 + c, at, :], ((1,), (1,)))
        out_ref[c, xrows, at] = (y + bias_ref[pl.ds(b0 + c, 1), at]).astype(BF)
        return carry

    lax.fori_loop(0, 3 * tiles, body, 0, unroll=3)


def half_lanes():
    lane = lax.broadcasted_iota(jnp.int32, (1, 2 * HEAD_DIM), 1)
    return lane < HEAD_DIM


def attend(qkv_ref, ctx_ref, p_ref, mask_ref, q0, lq, k0, lk):
    first = half_lanes()
    keep = [jnp.where(first, HEAD_DIM**-0.5, 0.0).astype(BF), jnp.where(first, 0.0, HEAD_DIM**-0.5).astype(BF)]

    def body(pair, carry):
        lanes = pl.ds(pl.multiple_of(pair * 2 * HEAD_DIM, 2 * HEAD_DIM), 2 * HEAD_DIM)
        for g in range(2):
            qr, kr = pl.ds(q0 + g * lq, lq), pl.ds(k0 + g * lk, lk)
            q, k, v = qkv_ref[0, qr, lanes], qkv_ref[1, kr, lanes], qkv_ref[2, kr, lanes]
            parts = []
            for h in range(2):
                s = dot(q * keep[h], k, ((1,), (1,))) + mask_ref[g]
                w = jnp.exp(s - jnp.max(s, axis=1, keepdims=True))
                pb = (w * (1.0 / jnp.sum(w, axis=1, keepdims=True))).astype(BF)
                p_ref[g, 2 * pair + h] = pb
                parts.append(dot(pb, v, ((1,), (0,))))
            ctx_ref[qr, lanes] = jnp.where(first, parts[0], parts[1]).astype(BF)
        return carry

    lax.fori_loop(0, D // (2 * HEAD_DIM), body, 0, unroll=3)


def out_norm(ctx_ref, start, count, w_ref, wi, resid_ref, vec_ref, v0, pre_ref, hat_ref, rstd_ref, full_ref, low_ref):
    rows = pl.ds(start, count)
    ctx = ctx_ref[rows, :]

    def tile(t, carry):
        at = pl.ds(pl.multiple_of(t * TILE, TILE), TILE)
        y = dot(ctx, w_ref[wi, :, at], ((1,), (0,)))
        pre_ref[rows, at] = y + resid_ref[rows, at].astype(F32) + vec_ref[pl.ds(v0, 1), at]
        return carry

    lax.fori_loop(0, D // TILE, tile, 0)
    gain, shift = vec_ref[v0 + 1 : v0 + 2, :], vec_ref[v0 + 2 : v0 + 3, :]

    def norm(i, carry):
        r = pl.ds(pl.multiple_of(start + i * 32, 16), 32)
        x = pre_ref[r, :]
        center = x - jnp.sum(x, axis=1, keepdims=True) * (1.0 / D)
        rstd = lax.rsqrt(jnp.sum(center * center, axis=1, keepdims=True) * (1.0 / D) + LAYER_EPS)
        hat = center * rstd
        y = hat * gain + shift
        hat_ref[r, :] = hat.astype(BF)
        rstd_ref[r, :] = jnp.broadcast_to(rstd, (32, 128))
        full_ref[r, :] = y
        low_ref[r, :] = y.astype(BF)
        return carry

    lax.fori_loop(0, count // 32, norm, 0)


def by_group(src_ref, dst_ref, start, slots):
    half = slots * GROUP // 2
    low = lax.broadcasted_iota(jnp.int32, (8, D), 0) < 4

    def body(i, carry):
        a = [src_ref[4 * i + t].astype(F32) for t in range(4)]
        for g in range(2):
            rows = []
            for t in (0, 2):
                one, two = (a[t], pltpu.roll(a[t + 1], 4, 0)) if g == 0 else (pltpu.roll(a[t], 4, 0), a[t + 1])
                rows.append(jnp.where(low, one, two))
            at = pl.ds(pl.multiple_of(start + g * half + 16 * i, 16), 16)
            dst_ref[at, :] = jnp.concatenate(rows, axis=0).astype(dst_ref.dtype)
        return carry

    lax.fori_loop(0, slots // 4, body, 0)


def fill_masks(mask_refs, counts, first):
    for n, (ref, count) in enumerate(zip(mask_refs, counts)):
        for g in range(2):
            shape = ref.shape[1:]
            row, col = (lax.broadcasted_iota(jnp.int32, shape, d) for d in range(2))
            item = jnp.bitwise_and(col, 3)
            limit = jnp.zeros(shape, jnp.int32)
            for j in range(4):
                limit = jnp.where(item == j, count[first + 4 * g + j], limit)
            seen = jnp.logical_and(jnp.bitwise_and(row, 3) == item, jnp.right_shift(col, 2) < limit)
            ref[g] = jnp.where(seen, 0.0, MASKED).astype(F32)


SLOTS = 4
CORE_SLOTS = 6
PARTS = 3


def scatter_steps(nz, mixed, slot_bufs, send_sem, recv_sem, rs_out):
    grad, crecv, xa, yb, ya, xb, zbuf, zrecv = slot_bufs
    dp, z, core, bx, by = place()
    dev_c = (dp + 1 - 2 * core, z)
    dev_x = (dp + 2 - 4 * bx, z)
    dev_y = (dp + 4 - 8 * by, z)
    rows, width = crecv.shape[3], crecv.shape[4]
    half = width // 2
    lo, hi = pl.ds(0, half), pl.ds(half, half)
    zw = width // nz
    S_C, S_XA, S_YB, S_YA, S_XB, S_Z = 0, 1, 2, 3, 4, 5

    def part(i, c):
        return grad.at[:, :, c, pl.ds((i % PARTS) * rows, rows)]

    def remote(src, dst, s, k, device):
        return pltpu.make_async_remote_copy(
            src_ref=src, dst_ref=dst, send_sem=send_sem.at[s, k], recv_sem=recv_sem.at[s, k], device_id=device, device_id_type=MESH
        )

    def core_copy(i):
        return remote(part(i, 1 - core), crecv.at[i % CORE_SLOTS], i % CORE_SLOTS, S_C, dev_c)

    def xa_copy(i):
        s = i % SLOTS
        return remote(crecv.at[i % CORE_SLOTS, :, 1 - bx, :, lo], xa.at[s], s, S_XA, dev_x)

    def yb_copy(i):
        s = i % SLOTS
        return remote(crecv.at[i % CORE_SLOTS, 1 - by, :, :, hi], yb.at[s], s, S_YB, dev_y)

    def ya_copy(i):
        s = i % SLOTS
        return remote(crecv.at[i % CORE_SLOTS, 1 - by, bx, :, lo], ya.at[s], s, S_YA, dev_y)

    def xb_copy(i):
        s = i % SLOTS
        return remote(crecv.at[i % CORE_SLOTS, by, 1 - bx, :, hi], xb.at[s], s, S_XB, dev_x)

    def z_copy(s, k):
        return remote(zbuf.at[s, (z + k) % nz], zrecv.at[s, k - 1], s, S_Z + k - 1, (dp, (z + k) % nz))

    def merge(dst, src):
        for r in range(0, rows, 16):
            at = pl.ds(r, 16)
            dst[at] = dst[at] + src[at]

    def stage_a(i):
        core_copy(i).wait()
        mine = part(i, core)

        def body(j, carry):
            merge(crecv.at[i % CORE_SLOTS, j // 2, j % 2], mine.at[j // 2, j % 2])
            return carry

        lax.fori_loop(0, 4, body, 0, unroll=2)
        xa_copy(i).start()
        yb_copy(i).start()

    def stage_b(i):
        s = i % SLOTS
        xa_copy(i).wait()
        yb_copy(i).wait()

        def body(j, carry):
            merge(crecv.at[i % CORE_SLOTS, j, bx, :, lo], xa.at[s, j])
            merge(crecv.at[i % CORE_SLOTS, by, j, :, hi], yb.at[s, j])
            return carry

        lax.fori_loop(0, 2, body, 0, unroll=2)
        ya_copy(i).start()
        xb_copy(i).start()

    def stage_c(i):
        s = i % SLOTS
        ya_copy(i).wait()
        xb_copy(i).wait()
        own = crecv.at[i % CORE_SLOTS, by, bx]
        for r in range(0, rows, 16):
            at = pl.ds(r, 16)
            left = own[at, lo] + ya[s, at, :]
            right = own[at, hi] + xb[s, at, :]
            full = jnp.concatenate([left, right], axis=1)
            for t in range(nz):
                if mixed[i // PARTS]:
                    sub = zw // 4
                    row = [full[:, m * (width // 4) + t * sub : m * (width // 4) + (t + 1) * sub] for m in range(4)]
                    zbuf[s, t, at, :] = jnp.concatenate(row, axis=1)
                else:
                    zbuf[s, t, at, :] = full[:, t * zw : (t + 1) * zw]
        for k in range(1, nz):
            z_copy(s, k).start()

    def stage_d(i):
        s = i % SLOTS
        for k in range(1, nz):
            z_copy(s, k).wait()
        for r in range(0, rows, 16):
            at = pl.ds(r, 16)
            total = zbuf[s, z, at, :].astype(F32)
            for k in range(nz - 1):
                total = total + zrecv[s, k, at, :].astype(F32)
            rs_out[i, at, :] = total

    return core_copy, stage_a, stage_b, stage_c, stage_d


def small_steps(nz, small, sbuf, srecv, szrecv, small_out, send_sem, recv_sem):
    dp, z, core, bx, by = place()
    devs = ((dp + 1 - 2 * core, z), (dp + 2 - 4 * bx, z), (dp + 4 - 8 * by, z))

    def remote(src, dst, k, device):
        return pltpu.make_async_remote_copy(
            src_ref=src, dst_ref=dst, send_sem=send_sem.at[k], recv_sem=recv_sem.at[k], device_id=device, device_id_type=MESH
        )

    def pair(k):
        return remote(sbuf.at[k], srecv.at[k], k, devs[k])

    def along_z(k, sending):
        return remote(sbuf.at[3], szrecv.at[z if sending else (z + nz - k) % nz], 2 + k, (dp, (z + k) % nz))

    def stage(k):
        if k == 0:
            sbuf[0] = small[...]
            pair(0).start()
        elif k < 4:
            pair(k - 1).wait()
            sbuf[k] = sbuf[k - 1] + srecv[k - 1]
            if k < 3:
                pair(k).start()
            else:
                szrecv[z] = sbuf[3]
                for i in range(1, nz):
                    along_z(i, True).start()
        else:
            for i in range(1, nz):
                along_z(i, True).wait_send()
                along_z(i, False).wait_recv()
            total = szrecv[0]
            for i in range(1, nz):
                total = total + szrecv[i]
            small_out[...] = total

    return stage


def eighth(x):
    return jnp.sum(x.reshape(x.shape[0] // 8, 8, x.shape[1]), axis=0)


def transpose_into(t_ref, x_ref, start, count):
    for i in range(D // 128):
        t_ref[i * 128 : (i + 1) * 128, 0:count] = x_ref[pl.ds(start, count), i * 128 : (i + 1) * 128].T


def feed_forward(nb_ref, rows, w_ref, bias_ref, b0, h_ref, slope_ref, first, last):
    x = nb_ref[rows, :]
    tiles = D // TILE

    def body(i, carry):
        zb, t = i // tiles, i % tiles
        at = pl.ds(pl.multiple_of(t * TILE, TILE), TILE)
        u = dot(x, w_ref[zb, :, at], ((1,), (0,))) + bias_ref[pl.ds(b0 + zb, 1), at]
        phi = 0.5 + 0.5 * lax.erf(u * 0.5**0.5)
        h_ref[zb, rows, at] = (u * phi).astype(BF)
        slope_ref[zb, rows, at] = (phi + u * (jnp.exp(-0.5 * u * u) * 0.3989422804014327)).astype(BF)
        return carry

    lax.fori_loop(first * tiles, last * tiles, body, 0)


def feed_out_rows(h_ref, rows, w_ref, nn_ref, vec_ref, v0, res_ref):
    def body(t, carry):
        at = pl.ds(pl.multiple_of(t * TILE, TILE), TILE)
        y = nn_ref[rows, at] + vec_ref[pl.ds(v0, 1), at]
        for zb in range(h_ref.shape[0]):
            y = y + dot(h_ref[zb, rows, :], w_ref[zb, :, at], ((1,), (0,)))
        res_ref[rows, at] = y
        return carry

    lax.fori_loop(0, D // TILE, body, 0)


def norm_grad(hat, rstd, gain, g, acc):
    scaled = g * gain
    dz = rstd * (
        scaled - jnp.sum(scaled, axis=1, keepdims=True) * (1.0 / D) - hat * (jnp.sum(scaled * hat, axis=1, keepdims=True) * (1.0 / D))
    )
    return dz, (acc[0] + eighth(dz), acc[1] + eighth(g * hat), acc[2] + eighth(g))


def no_sums():
    return tuple(jnp.zeros((8, D), F32) for _ in range(3))


def keep_sums(acc, small, row):
    for i in range(3):
        small[row + i : row + i + 1, :] = jnp.sum(acc[i], axis=0, keepdims=True)


def last_norm(start, count, res_ref, vec_ref, v0, cot_ref, weight_ref, result_ref, db_ref, small, row):
    gain, shift = vec_ref[v0 + 1 : v0 + 2, :], vec_ref[v0 + 2 : v0 + 3, :]

    def body(i, acc):
        r = pl.ds(pl.multiple_of(start + i * 32, 16), 32)
        x = res_ref[r, :]
        center = x - jnp.sum(x, axis=1, keepdims=True) * (1.0 / D)
        rstd = lax.rsqrt(jnp.sum(center * center, axis=1, keepdims=True) * (1.0 / D) + LAYER_EPS)
        hat = center * rstd
        result_ref[r, :] = (hat * gain + shift).astype(BF)
        g = cot_ref[r, :].astype(F32) * weight_ref[r, 0:1]
        dz, acc = norm_grad(hat, rstd, gain, g, acc)
        res_ref[r, :] = dz
        db_ref[r, :] = dz.astype(BF)
        return acc

    keep_sums(lax.fori_loop(0, count // 32, body, no_sums()), small, row)


def norm_back(start, count, res_ref, hat_ref, rstd_ref, vec_ref, gain_row, db_ref, small, row):
    gain = vec_ref[gain_row : gain_row + 1, :]

    def body(i, acc):
        r = pl.ds(pl.multiple_of(start + i * 32, 16), 32)
        dz, acc = norm_grad(hat_ref[r, :].astype(F32), rstd_ref[r, 0:1], gain, res_ref[r, :], acc)
        res_ref[r, :] = dz
        db_ref[r, :] = dz.astype(BF)
        return acc

    keep_sums(lax.fori_loop(0, count // 32, body, no_sums()), small, row)


def hidden_grad(db_ref, rows, w_ref, slope_ref, small, row):
    db = db_ref[rows, :]
    tiles = D // TILE

    def body(i, carry):
        zb, t = i // tiles, i % tiles
        at = pl.ds(pl.multiple_of(t * TILE, TILE), TILE)
        du = (dot(db, w_ref[zb, at, :], ((1,), (1,))) * slope_ref[zb, rows, at].astype(F32)).astype(BF)
        slope_ref[zb, rows, at] = du
        small[pl.ds(row + zb, 1), at] = jnp.sum(eighth(du.astype(F32)), axis=0, keepdims=True)
        return carry

    lax.fori_loop(0, slope_ref.shape[0] * tiles, body, 0, unroll=2)


def add_products(res_ref, out_ref, rows, x_ref, count, w_ref, transposed):
    def body(t, carry):
        at = pl.ds(pl.multiple_of(t * TILE, TILE), TILE)
        y = res_ref[rows, at]
        for c in range(count):
            if transposed:
                y = y + dot(x_ref[c, rows, :], w_ref[c, at, :], ((1,), (1,)))
            else:
                y = y + dot(x_ref[c, rows, :], w_ref[c, :, at], ((1,), (0,)))
        out_ref[rows, at] = y
        return carry

    lax.fori_loop(0, D // TILE, body, 0)


def context_grad(db_ref, rows, w_ref, dctx_ref):
    db = db_ref[rows, :]

    def body(t, carry):
        at = pl.ds(pl.multiple_of(t * TILE, TILE), TILE)
        dctx_ref[rows, at] = dot(db, w_ref[3, at, :], ((1,), (1,))).astype(BF)
        return carry

    lax.fori_loop(0, D // TILE, body, 0)


def attend_back(qkv_ref, dctx_ref, p_ref, out_ref, q0, lq, k0, lk, first_pair=0, last_pair=D // (2 * HEAD_DIM)):
    first = half_lanes()
    keep = [jnp.where(first, 1.0, 0.0).astype(BF), jnp.where(first, 0.0, 1.0).astype(BF)]

    def body(pair, carry):
        lanes = pl.ds(pl.multiple_of(pair * 2 * HEAD_DIM, 2 * HEAD_DIM), 2 * HEAD_DIM)
        for g in range(2):
            qr, kr = pl.ds(q0 + g * lq, lq), pl.ds(k0 + g * lk, lk)
            q, k, v, dc = qkv_ref[0, qr, lanes], qkv_ref[1, kr, lanes], qkv_ref[2, kr, lanes], dctx_ref[qr, lanes]
            dq, dk, dv = [], [], []
            for h in range(2):
                pb = p_ref[g, 2 * pair + h]
                p = pb.astype(F32)
                dp = dot(dc * keep[h], v, ((1,), (1,)))
                ds = (p * (dp - jnp.sum(p * dp, axis=1, keepdims=True))).astype(BF)
                dq.append(dot(ds, k, ((1,), (0,))))
                dk.append(dot(ds, q, ((0,), (0,))))
                dv.append(dot(pb, dc, ((0,), (0,))))
            out_ref[0, qr, lanes] = (jnp.where(first, dq[0], dq[1]) * HEAD_DIM**-0.5).astype(BF)
            out_ref[1, kr, lanes] = (jnp.where(first, dk[0], dk[1]) * HEAD_DIM**-0.5).astype(BF)
            out_ref[2, kr, lanes] = jnp.where(first, dv[0], dv[1]).astype(BF)
        return carry

    lax.fori_loop(first_pair, last_pair, body, 0)


def bias_sums(x_ref, rows, count, small, row_q, row_v, add):
    ones = jnp.ones((8, count), BF)
    for c, row in ((0, row_q), (2, row_v)):
        total = dot(ones, x_ref[c, rows, :], ((1,), (0,)))[0:1, :]
        small[row : row + 1, :] = total


def grad_tiles(grad_ref, m, t_ref, count, x_ref, rows, first, last, lane0, mats):
    size = grad_ref.shape[3]
    left = t_ref[:, 0:count]
    tiles = D // TILE

    def body(i, carry):
        b, t = i // tiles, i % tiles
        at = pl.ds(pl.multiple_of(t * TILE, TILE), TILE)
        right = x_ref[b, rows, at] if mats else x_ref[rows, at]
        y = dot(left, right, ((1,), (0,))).astype(BF)
        lanes = pl.ds(pl.multiple_of(lane0 + i * TILE, TILE), TILE)
        grad_ref[:, :, :, :, lanes] = y.reshape(2, 2, 2, size, TILE)
        return carry

    lax.fori_loop(first * tiles, last * tiles, body, 0, unroll=3)


CROSS, SELF1, IN1, OUT1, SELF0, IN0, OUT0 = range(7)
MIXED = (False, False, True, False, False, True, True)


def layer_kernel(nz, lens, *refs):
    cp, co, sp, so, fi, fo, word_count, region_count, flags = refs[:9]
    lang, vis, cot_lang, cot_vis, cross_b, self_b, feed_b = refs[9:16]
    cob, cg, cs, sob, sg, ss, fob, fg, fs = refs[16:25]
    whole = refs[25:32]
    rs_out, small_out, result, res = refs[32:36]
    wb3 = refs[36]
    refs = refs[1:]
    wb0, wb1, wb2, x, qkv_c, ctx_c, p_c0, p_c1, hat1, rstd1, mb = refs[36:47]
    qkv_s, ctx_s, p_s0, p_s1, hat2, rstd2, mid, nb, hid, slope, db, dctx, t1, t2, small = refs[47:62]
    grad, crecv, xa, yb, ya, xb, zbuf, zrecv, sbuf, srecv, szrecv = refs[62:73]
    bias_src, bias_all, bias_ref, vec, weight = refs[73:78]
    masks = refs[78:82]
    send_sem, recv_sem, core_sem, w_sem, bias_send, bias_recv, rs_send, rs_recv, small_send, small_recv = refs[82:]
    dp, z, core, bx, by = place()
    lw, lv = lens
    rw, rv = 2 * lw, 2 * lv
    start, count = (0, rw), (rw, rv)
    rows = (pl.ds(0, rw), pl.ds(rw, rv))
    every = pl.ds(0, rw + rv)

    bias_src[...] = jnp.zeros_like(bias_src)
    part = cross_b.shape[1]
    for t in range(nz):

        @pl.when(z == t)
        def _(t=t):
            lanes = slice(t * part, (t + 1) * part)
            for i in range(2):
                bias_src[2 * i : 2 * i + 1, lanes] = cross_b[i : i + 1, :]
                for s in range(2):
                    bias_src[3 + 3 * s + 2 * i : 4 + 3 * s + 2 * i, lanes] = self_b[s, i : i + 1, :]
            for s in range(2):
                bias_src[9 + nz * s + t : 10 + nz * s + t, :] = feed_b[s : s + 1, :]

    targets = [((dp + 1 - 2 * core, z), None), ((dp + 2 - 4 * bx, z), None), ((dp + 4 - 8 * by, z), None)]
    for k in range(1, nz):
        targets.append(((dp, (z + k) % nz), None))
    greet(targets)
    units = (
        (cp, co),
        (sp.at[1], so.at[1]),
        (fi.at[1],),
        (fo.at[1],),
        (sp.at[0], so.at[0]),
        (fi.at[0],),
        (fo.at[0],),
    )
    z_send, gather, arrived, sent, loads = gather_steps(nz, units, whole, send_sem, recv_sem, core_sem)
    slot_bufs = (grad, crecv, xa, yb, ya, xb, zbuf, zrecv)
    core_copy, stage_a, stage_b, stage_c, stage_d = scatter_steps(nz, MIXED, slot_bufs, rs_send, rs_recv, rs_out)
    small_stage = small_steps(nz, small, sbuf, srecv, szrecv, small_out, small_send, small_recv)
    pieces = len(MIXED) * PARTS

    def scatter(n):
        if n + 1 < pieces and (n + 1) % PARTS:
            core_copy(n + 1).start()
        if n < pieces:
            stage_a(n)
        if 1 <= n < pieces + 1:
            stage_b(n - 1)
        if 2 <= n < pieces + 2:
            stage_c(n - 2)
        if 3 <= n < pieces + 3:
            stage_d(n - 3)

    def bias_copy(k, sending):
        return pltpu.make_async_remote_copy(
            src_ref=bias_src,
            dst_ref=bias_all.at[z if sending else (z + nz - k) % nz],
            send_sem=bias_send.at[k],
            recv_sem=bias_recv.at[k],
            device_id=(dp, (z + k) % nz),
            device_id_type=MESH,
        )

    def fetch(u, dst):
        arrived(u)
        for c in loads(u, dst, w_sem.at[u]):
            c.start()

    def ready(u, dst):
        for c in loads(u, dst, w_sem.at[u]):
            c.wait()

    cot = dctx

    def prepare():
        for i, ref in enumerate((cob, cg, cs)):
            vec[i : i + 1, :] = ref[...].reshape(1, D)
        for s in range(2):
            for i, ref in enumerate((sob, sg, ss)):
                vec[3 + 3 * s + i : 4 + 3 * s + i, :] = ref[s : s + 1, :]
            for i, ref in enumerate((fob, fg, fs)):
                vec[9 + 3 * s + i : 10 + 3 * s + i, :] = ref[s : s + 1, :]
        by_group(lang, x, 0, lang.shape[0])
        by_group(vis, x, rw, vis.shape[0])
        by_group(cot_lang, cot, 0, cot_lang.shape[0])
        by_group(cot_vis, cot, rw, cot_vis.shape[0])
        fill_masks(masks, (region_count, word_count, word_count, region_count), z * GROUP)
        for s in range(2):
            for g in range(2):
                row = lax.broadcasted_iota(jnp.int32, (lens[s], 128), 0)
                item = jnp.bitwise_and(row, 3)
                value = jnp.zeros((lens[s], 128), F32)
                for j in range(4):
                    n = 4 * g + j
                    other = flags[0, n].astype(F32)
                    if s == 0:
                        answer = jnp.maximum(flags[1, n], flags[2, n]).astype(F32)
                        value = jnp.where(item == j, jnp.where(row < 4, answer, other), value)
                    else:
                        value = jnp.where(item == j, other, value)
                weight[start[s] + g * lens[s] : start[s] + (g + 1) * lens[s], :] = value

    def bias_sum():
        for k in range(1, nz):
            bias_copy(k, False).wait_recv()
        bias_all[z] = bias_src[...]
        total = bias_all[0]
        for k in range(1, nz):
            total = total + bias_all[k]
        bias_ref[...] = total

    w_self, w_in, w_out = (wb3, wb1), (wb2, wb2), (wb1, wb3)
    u_self, u_in, u_out = (SELF0, SELF1), (IN0, IN1), (OUT0, OUT1)

    def cross_project_all():
        ready(CROSS, wb0)
        bias_sum()
        project(x, every, wb0, 0, bias_ref, 0, qkv_c)

    def cross_forward(s):
        if s == 0:
            attend(qkv_c, ctx_c, p_c0, masks[0], 0, lw, rw, lv)
        else:
            attend(qkv_c, ctx_c, p_c1, masks[1], rw, lv, 0, lw)

    def cross_norm(s):
        out_norm(ctx_c, start[s], count[s], wb0, 3, x, vec, 0, res, hat1, rstd1, mid, mb)

    def self_project(s):
        ready(u_self[s], w_self[s])
        project(mb, rows[s], w_self[s], 0, bias_ref, 3 + 3 * s, qkv_s)

    def self_forward(s):
        attend(qkv_s, ctx_s, (p_s0, p_s1)[s], masks[2 + s], start[s], lens[s], start[s], lens[s])

    def self_norm(s):
        out_norm(ctx_s, start[s], count[s], w_self[s], 3, mid, vec, 3 + 3 * s, res, hat2, rstd2, mid, nb)

    def forward(s, first, last):
        if first == 0:
            ready(u_in[s], w_in[s])
        feed_forward(nb, rows[s], w_in[s], bias_ref, 9 + nz * s, hid, slope, first, last)

    def out_rows(s):
        ready(u_out[s], w_out[s])
        feed_out_rows(hid, rows[s], w_out[s], mid, vec, 9 + 3 * s, res)

    def norm3(s):
        last_norm(start[s], count[s], res, vec, 9 + 3 * s, cot, weight, result, db, small, 15 + 3 * s)

    def du(s):
        hidden_grad(db, rows[s], w_out[s], slope, small, 21 + nz * s)

    def dn(s):
        add_products(res, res, rows[s], slope, nz, w_in[s], True)

    def self_in(s):
        norm_back(start[s], count[s], res, hat2, rstd2, vec, 4 + 3 * s, db, small, 7 + 5 * s)
        context_grad(db, rows[s], w_self[s], dctx)

    def self_back(s, first, last):
        attend_back(qkv_s, dctx, (p_s0, p_s1)[s], hid, start[s], lens[s], start[s], lens[s], first, last)

    def self_sums(s):
        bias_sums(hid, rows[s], count[s], small, 5 + 5 * s, 6 + 5 * s, False)

    def dm(s):
        add_products(res, res, rows[s], hid, 3, w_self[s], False)

    def cross_in():
        norm_back(0, rw + rv, res, hat1, rstd1, vec, 1, nb, small, 2)
        context_grad(nb, every, wb0, dctx)

    def cross_back(s, first, last):
        attend_back(qkv_c, dctx, (p_c0, p_c1)[s], slope, start[s], lens[s], start[1 - s], lens[1 - s], first, last)

    def cross_sums():
        bias_sums(slope, every, rw + rv, small, 0, 1, False)
        small_stage(0)

    def finish_rows():
        add_products(res, res, every, slope, 3, wb0, False)

    def grads(m):
        if m < 6:
            s = 1 - m // 3
            if m % 3 < 2:
                turned, src, right = ((t1, db, hid), (t2, nb, slope))[m % 3]
                transpose_into(turned, src, start[s], count[s])
                grad_tiles(grad, m, turned, count[s], right, rows[s], 0, nz, 0, True)
                core_copy(m * PARTS).start()
                return
            src, at, n, back, ctx, dqkv, dz = mb, start[s], count[s], rows[s], ctx_s, hid, db
        else:
            src, at, n, back, ctx, dqkv, dz = x, 0, rw + rv, every, ctx_c, slope, nb
        transpose_into(t1, dz, at, n)
        transpose_into(t2, src, at, n)
        grad_tiles(grad, m, t2, n, dqkv, back, 0, 3, 0, True)
        grad_tiles(grad, m, t1, n, ctx, back, 0, 1, 3 * D, False)
        core_copy(m * PARTS).start()

    for k in range(1, nz):
        z_send(0, k)
    for k in range(1, nz):
        bias_copy(k, True).start()
    for k in range(1, nz):
        z_send(1, k)
    prepare()
    for n in range(5):
        gather(n)
    fetch(CROSS, wb0)
    gather(5)
    cross_project_all()
    gather(6)
    cross_forward(1)
    gather(7)
    fetch(SELF1, wb1)
    cross_norm(1)
    gather(8)
    self_project(1)
    gather(9)
    self_forward(1)
    gather(10)
    fetch(IN1, wb2)
    self_norm(1)
    gather(11)
    forward(1, 0, 2)
    gather(12)
    forward(1, 2, nz)
    gather(13)
    fetch(OUT1, wb3)
    gather(14)
    out_rows(1)
    norm3(1)
    grads(0)
    gather(15)
    du(1)
    scatter(0)
    gather(16)
    fetch(SELF0, wb3)
    dn(1)
    scatter(1)
    gather(17)
    self_in(1)
    scatter(2)
    grads(1)
    gather(18)
    self_back(1, 0, 3)
    scatter(3)
    gather(19)
    fetch(IN0, wb2)
    self_back(1, 3, 6)
    scatter(4)
    gather(20)
    dm(1)
    self_sums(1)
    scatter(5)
    grads(2)
    gather(21)
    cross_forward(0)
    scatter(6)
    gather(22)
    fetch(OUT0, wb1)
    cross_norm(0)
    self_project(0)
    self_forward(0)
    scatter(7)
    self_norm(0)
    forward(0, 0, nz)
    out_rows(0)
    norm3(0)
    scatter(8)
    grads(3)
    du(0)
    scatter(9)
    dn(0)
    self_in(0)
    scatter(10)
    self_back(0, 0, 6)
    scatter(11)
    grads(4)
    dm(0)
    cross_in()
    scatter(12)
    cross_back(0, 0, 3)
    scatter(13)
    cross_back(0, 3, 6)
    scatter(14)
    self_sums(0)
    grads(5)
    cross_back(1, 0, 3)
    scatter(15)
    cross_back(1, 3, 6)
    scatter(16)
    scatter(17)
    grads(6)
    cross_sums()
    finish_rows()
    scatter(18)
    small_stage(1)
    scatter(19)
    small_stage(2)
    scatter(20)
    small_stage(3)
    scatter(21)
    small_stage(4)
    scatter(22)
    scatter(23)
    for u in range(len(units)):
        sent(u)
    for k in range(1, nz):
        bias_copy(k, True).wait_send()


def layer(nz, lens, shards, counts, flags, inputs, biases, vectors):
    rows = 2 * sum(lens)
    lw, lv = lens
    nh = D // HEAD_DIM
    size = D // GROUP // PARTS
    width = 4 * D
    any_spec = pl.BlockSpec(memory_space=pl.ANY)
    vmem = pl.BlockSpec(memory_space=pltpu.VMEM)
    smem = pl.BlockSpec(memory_space=pltpu.SMEM)
    sd = jax.ShapeDtypeStruct
    vm = pltpu.VMEM
    total = len(MIXED) * PARTS
    dma = pltpu.SemaphoreType.DMA
    act = vm((rows, D), BF)
    outs = pl.pallas_call(
        functools.partial(layer_kernel, nz, lens),
        out_shape=[sd((4, D, D), BF)] * 7
        + [sd((total, size, width // nz), F32), sd((32, D), F32), sd((rows, D), BF), sd((rows, D), F32)],
        in_specs=[any_spec] * 6 + [smem] * 3 + [vmem] * 16,
        out_specs=[any_spec] * 7 + [vmem] * 4,
        scratch_shapes=[
            vm((4, D, D), BF),
            vm((4, D, D), BF),
            vm((4, D, D), BF),
            vm((4, D, D), BF),
            act,
            vm((3, rows, D), BF),
            act,
            vm((2, nh, lw, lv), BF),
            vm((2, nh, lv, lw), BF),
            act,
            vm((rows, 128), F32),
            act,
            vm((3, rows, D), BF),
            act,
            vm((2, nh, lw, lw), BF),
            vm((2, nh, lv, lv), BF),
            act,
            vm((rows, 128), F32),
            vm((rows, D), F32),
            act,
            vm((nz, rows, D), BF),
            vm((nz, rows, D), BF),
            act,
            act,
            vm((D, rows), BF),
            vm((D, rows), BF),
            vm((32, D), F32),
            vm((2, 2, 2, size * PARTS, width), BF),
            vm((CORE_SLOTS, 2, 2, size, width), BF),
            vm((SLOTS, 2, size, width // 2), BF),
            vm((SLOTS, 2, size, width // 2), BF),
            vm((SLOTS, size, width // 2), BF),
            vm((SLOTS, size, width // 2), BF),
            vm((SLOTS, nz, size, width // nz), BF),
            vm((SLOTS, nz - 1, size, width // nz), BF),
            vm((4, 32, D), F32),
            vm((3, 32, D), F32),
            vm((nz, 32, D), F32),
            vm((24, D), F32),
            vm((nz, 24, D), F32),
            vm((24, D), F32),
            vm((16, D), F32),
            vm((rows, 128), F32),
            vm((2, lw, lv), F32),
            vm((2, lv, lw), F32),
            vm((2, lw, lw), F32),
            vm((2, lv, lv), F32),
            dma((7,)),
            dma((7, nz - 1, K_C)),
            dma((7,)),
            dma((7, nz + 1)),
            dma((nz,)),
            dma((nz,)),
            dma((CORE_SLOTS, 4 + nz)),
            dma((CORE_SLOTS, 4 + nz)),
            dma((2 + nz,)),
            dma((2 + nz,)),
        ],
        compiler_params=pltpu.CompilerParams(collective_id=1, has_side_effects=True, vmem_limit_bytes=VMEM_BYTES),
        name="layer",
    )(*shards, *counts, flags, *inputs, *biases, *vectors)
    return outs[7:]


VMEM_BYTES = 63 << 20


def finish_kernel(es, nz, slots, *refs):
    loads = [pltpu.make_async_copy(src, dst, refs[30].at[i]) for i, (src, dst) in enumerate(zip(refs[:4], refs[26:30]))]
    for c in loads:
        c.start()
    sums, small, result, dinput = refs[26:30]
    refs = refs[:26]
    lang, vis, dlang, dvis, gcp, gcb, gco, gcob, gcg, gcs, gsp, gsb, gso, gsob, gsg, gss, gfi, gfib, gfo, gfob, gfg, gfs = refs[4:]
    parts, rows = sums.shape[1], sums.shape[2]
    low = lax.broadcasted_iota(jnp.int32, (8, D), 0) < 4

    def by_slot(src, dst, start, n):
        half = n * GROUP // 2

        def body(i, carry):
            g = [src[pl.ds(pl.multiple_of(start + h * half + 16 * i, 16), 16), :].astype(F32) for h in range(2)]
            for t in range(2):
                one, two = g[0][8 * t : 8 * t + 8], g[1][8 * t : 8 * t + 8]
                dst[4 * i + 2 * t] = jnp.where(low, one, pltpu.roll(two, 4, 0)).astype(dst.dtype)
                dst[4 * i + 2 * t + 1] = jnp.where(low, pltpu.roll(one, 4, 0), two).astype(dst.dtype)
            return carry

        lax.fori_loop(0, n // 4, body, 0)

    loads[2].wait()
    by_slot(result, lang, 0, slots[0])
    by_slot(result, vis, GROUP * slots[0], slots[1])
    loads[3].wait()
    by_slot(dinput, dlang, 0, slots[0])
    by_slot(dinput, dvis, GROUP * slots[0], slots[1])
    loads[0].wait()
    loads[1].wait()
    for s in range(2):
        first = 3 * (1 - s)
        for p in range(parts):
            gfo[s, p * rows : (p + 1) * rows, :] = sums[first, p]
            gfi[s, p * rows : (p + 1) * rows, :] = sums[first + 1, p]
    for i, proj, out in ((5, gsp.at[0], gso.at[0]), (2, gsp.at[1], gso.at[1]), (6, gcp, gco)):
        full = sums[i].reshape(parts * rows, D)
        for c in range(3):
            proj[c] = full[:, c * es : (c + 1) * es]
        out[...] = full[:, 3 * es :].T
    gcb[...] = small[0:2]
    for i, ref in enumerate((gcob, gcg, gcs)):
        ref[...] = small[2 + i : 3 + i].reshape(D)
    for s in range(2):
        gsb[s] = small[5 + 5 * s : 7 + 5 * s]
        for i, ref in enumerate((gsob, gsg, gss)):
            ref[s : s + 1] = small[7 + 5 * s + i : 8 + 5 * s + i]
        for i, ref in enumerate((gfob, gfg, gfs)):
            ref[s : s + 1] = small[15 + 3 * s + i : 16 + 3 * s + i]
        for t in range(nz):
            gfib[s : s + 1, t * D : (t + 1) * D] = small[21 + nz * s + t : 22 + nz * s + t]


def finish(es, nz, slots, sums, small, result, dinput):
    sd = jax.ShapeDtypeStruct
    chunk = D // GROUP
    vmem = pl.BlockSpec(memory_space=pltpu.VMEM)
    two, one = sd((2, D), F32), sd((D,), F32)
    shapes = (
        [sd((n, GROUP, D), dt) for dt in (BF, F32) for n in slots]
        + [sd((3, chunk, es), F32), two, sd((es, chunk), F32), one, one, one]
        + [sd((2, 3, chunk, es), F32), sd((2, 2, D), F32), sd((2, es, chunk), F32), two, two, two]
        + [sd((2, chunk, D), F32), sd((2, nz * D), F32), sd((2, chunk, D), F32), two, two, two]
    )
    return pl.pallas_call(
        functools.partial(finish_kernel, es, nz, slots),
        out_shape=shapes,
        in_specs=[pl.BlockSpec(memory_space=pltpu.HBM)] * 4,
        out_specs=[vmem] * len(shapes),
        scratch_shapes=[pltpu.VMEM(v.shape, v.dtype) for v in (sums, small, result, dinput)] + [pltpu.SemaphoreType.DMA((4,))],
        compiler_params=pltpu.CompilerParams(vmem_limit_bytes=VMEM_BYTES),
        name="finish",
    )(sums, small, result, dinput)


def dot(a, b, dims):
    return lax.dot_general(a, b, (dims, ((), ())), preferred_element_type=F32)


def per_device(nz, ndp, *args):
    (
        language,
        visual,
        word_count,
        region_count,
        task_flags,
        grad_language,
        grad_visual,
        cross_project,
        cross_bias,
        cross_out,
        cross_out_bias,
        cross_gain,
        cross_shift,
        self_project,
        self_bias,
        self_out,
        self_out_bias,
        self_gain,
        self_shift,
        feed_in,
        feed_in_bias,
        feed_out,
        feed_out_bias,
        feed_gain,
        feed_shift,
    ) = args
    items = language.shape[0]
    slots = (language.shape[1], visual.shape[1])
    counts_rows = (items * slots[0], items * slots[1])
    z = lax.axis_index("tensor")
    es = cross_project.shape[2]
    fs = feed_in.shape[2]
    lens = tuple(items // 2 * n for n in slots)
    shards = (jnp.swapaxes(cross_project, 1, 2), cross_out, jnp.swapaxes(self_project, 2, 3), self_out, feed_in, feed_out)
    sums, vectors, result, dinput = layer(
        nz,
        lens,
        shards,
        (word_count, region_count),
        task_flags.T,
        tuple(jnp.swapaxes(v, 0, 1) for v in (language, visual, grad_language, grad_visual)),
        (cross_bias, self_bias, feed_in_bias),
        (cross_out_bias, cross_gain, cross_shift, self_out_bias, self_gain, self_shift, feed_out_bias, feed_gain, feed_shift),
    )
    outer = ndp // GROUP
    if outer == 1:
        outs = list(finish(es, nz, slots, sums.reshape((7, PARTS) + sums.shape[1:]), vectors, result, dinput))
        for i in range(4):
            outs[i] = jnp.swapaxes(outs[i], 0, 1)
        outs[18] = jnp.swapaxes(outs[18], 1, 2)
        return tuple(outs)
    sums = sums.reshape(7, -1, sums.shape[2])
    if outer > 1:
        members = [[i * GROUP + j for i in range(outer)] for j in range(GROUP)]
        sums = lax.psum_scatter(sums, "dp", scatter_dimension=1, axis_index_groups=members, tiled=True)
        sums = lax.ppermute(sums, "dp", [(i * GROUP + j, j * outer + i) for i in range(outer) for j in range(GROUP)])
        vectors = lax.psum(vectors, "dp", axis_index_groups=members)
    names = [("out", 1), ("in", 1), ("self", 1), ("out", 0), ("in", 0), ("self", 0), "cross"]
    total = {name: sums[i] for i, name in enumerate(names)}

    def columns(v):
        return jnp.stack([v[:, i * es : (i + 1) * es] for i in range(3)]), v[:, 3 * es :].T

    gcp, gco = columns(total["cross"])
    gs = [columns(total["self", s]) for s in range(2)]
    v = vectors

    def by_item(x, s, shape):
        x = x[s * counts_rows[0] : s * counts_rows[0] + counts_rows[s]]
        return x.reshape(2, shape[1], shape[0] // 2, D).transpose(0, 2, 1, 3).reshape(shape)

    f0 = 21
    nf = nz * fs // D
    return (
        by_item(result, 0, language.shape),
        by_item(result, 1, visual.shape),
        by_item(dinput, 0, language.shape),
        by_item(dinput, 1, visual.shape),
        gcp,
        v[0:2],
        gco,
        v[2],
        v[3],
        v[4],
        jnp.stack([gs[0][0], gs[1][0]]),
        jnp.stack([v[5:7], v[10:12]]),
        jnp.stack([gs[0][1], gs[1][1]]),
        jnp.stack([v[7], v[12]]),
        jnp.stack([v[8], v[13]]),
        jnp.stack([v[9], v[14]]),
        jnp.stack([total["in", 0], total["in", 1]]),
        v[f0 : f0 + 2 * nf].reshape(2, nz * fs),
        jnp.stack([total["out", 0].T, total["out", 1].T]),
        jnp.stack([v[15], v[18]]),
        jnp.stack([v[16], v[19]]),
        jnp.stack([v[17], v[20]]),
    )


def solution(mesh):
    rows = P(("dp", "tensor"), None, None)
    placed = (
        rows,
        rows,
        P("dp"),
        P("dp"),
        P(("dp", "tensor"), None),
        rows,
        rows,
        P(None, None, "tensor"),
        P(None, "tensor"),
        P("tensor", None),
        P(),
        P(),
        P(),
        P(None, None, None, "tensor"),
        P(None, None, "tensor"),
        P(None, "tensor", None),
        P(),
        P(),
        P(),
        P(None, None, "tensor"),
        P(None, "tensor"),
        P(None, "tensor", None),
        P(),
        P(),
        P(),
    )
    return jax.shard_map(
        functools.partial(per_device, mesh.shape["tensor"], mesh.shape["dp"]),
        mesh=mesh,
        in_specs=placed,
        out_specs=(
            rows,
            rows,
            rows,
            rows,
            P(None, "dp", "tensor"),
            P(),
            P("tensor", "dp"),
            P(),
            P(),
            P(),
            P(None, None, "dp", "tensor"),
            P(),
            P(None, "tensor", "dp"),
            P(),
            P(),
            P(),
            P(None, "dp", "tensor"),
            P(),
            P(None, "tensor", "dp"),
            P(),
            P(),
            P(),
        ),
        check_vma=False,
    )
```
